32 devices in a mesh: depth: 2 (over core), height: 4 (over y, x), dp: 4 (over z).
Axes of the slice: x: 2, y: 2, z: 4, core: 2. Of those that a mesh axis runs over, the one named last changes fastest.
Arguments:
- inputs: bfloat16 [4, 32, 16, 16, 128], P('dp', None, 'depth', 'height'), may hold values from -6 to 6
- weight: bfloat16 [64, 32, 3, 3, 3], replicated, may hold values from -0.21875 to 0.21875
- bias: float32 [64], replicated, may hold values from -3 to 3
- cotangent: bfloat16 [4, 64, 16, 16, 128], P('dp', None, 'depth', 'height'), may hold values from -6 to 6
Outputs:
- grad_input: bfloat16 [4, 32, 16, 16, 128], P('dp', None, 'depth', 'height')
- grad_weight: float32 [64, 32, 3, 3, 3], replicated
- grad_bias: float32 [64], replicated
The draws below stay inside these ranges and needn't reach their ends.
All inputs are finite; a program needn't handle non-finite values.
Results may differ from the reference program's by a relative error of at most 0.0065.
Values may be sent and summed in bfloat16 or wider, within the bound.
No kernel may reach another device: no remote copies, remote signals or barrier semaphores. Data moves between devices by JAX's collectives and lax.ppermute only.
A program may use at most 64 MiB of HBM per device.

```python
import jax
import jax.numpy as jnp
from jax import lax

CI = 32
CO = 64
WID = 128
CUBES = 4
DEPTH = 16
HEIGHT = 16


def block_levels(key, extent, split, least, high):
    gain, own = 1.0, jax.random.fold_in(key, 6)
    for axis_at, blocks in split:
        heights = jnp.exp(jax.random.uniform(jax.random.fold_in(own, axis_at), (blocks,), jnp.float32, least / len(split), high / len(split)))
        gain = gain * jnp.repeat(heights, extent[axis_at] // blocks).reshape([-1 if axis == axis_at else 1 for axis in range(len(extent))])
    return gain


def bell_draw(own_key, dims, scale, bound, pieces=(), dtype=jnp.bfloat16):
    array = jax.random.normal(own_key, dims, jnp.float32) * scale
    if len(pieces) > 0:
        array = block_levels(own_key, dims, pieces, -0.22, 0.18) * array
    return jnp.clip(array, min=-bound, max=bound).astype(dtype)


def setup_inputs(seed: int = 0) -> dict:
    key_list = jax.random.split(jax.random.key(seed), 5)
    return {
        "inputs": bell_draw(key_list[0], (CUBES, CI, DEPTH, HEIGHT, WID), 1.0, 6.0, ((0, 4), (2, 2), (3, 4))),
        "weight": bell_draw(key_list[1], (CO, CI, 3, 3, 3), (CI * 27) ** -0.5, 0.21875),
        "bias": bell_draw(key_list[2], (CO,), 0.5, 3.0, (), jnp.float32),
        "cotangent": bell_draw(key_list[3], (CUBES, CO, DEPTH, HEIGHT, WID), 1.0, 6.0, ((0, 4), (2, 2), (3, 4))),
    }


def pad_all(field):
    return jnp.pad(field, ((0, 0), (0, 0), (1, 1), (1, 1), (1, 1)))


def correlate(field, kernel):
    return lax.conv_general_dilated(field, kernel, (1, 1, 1), "VALID", dimension_numbers=("NCDHW", "OIDHW", "NCDHW"), precision=lax.Precision.HIGHEST, preferred_element_type=jnp.float32)


def kernel_terms(field, delta_part):
    result = lax.conv_general_dilated(field, delta_part, (1, 1, 1), "VALID", dimension_numbers=("CNDHW", "IODHW", "NCDHW"), precision=lax.Precision.HIGHEST, preferred_element_type=jnp.float32)
    return result.transpose(1, 0, 2, 3, 4)


def reference(inputs, weight, bias, cotangent):
    kernel = weight.astype(jnp.float32)
    flipped = jnp.flip(kernel, (2, 3, 4)).transpose(1, 0, 2, 3, 4)
    bias_full = bias.astype(jnp.float32)[None, :, None, None, None]

    def one_cube(cube_pair):
        field = pad_all(cube_pair[0][None].astype(jnp.float32))
        linear = correlate(field, kernel) + bias_full
        sigma = jax.nn.sigmoid(linear)
        delta = (cube_pair[1][None].astype(jnp.float32) * sigma * (1.0 + linear * (1.0 - sigma))).astype(jnp.bfloat16)
        delta_wide = delta.astype(jnp.float32)
        grad_part = correlate(pad_all(delta_wide), flipped).astype(jnp.bfloat16)
        weight_part = kernel_terms(field, delta_wide)
        bias_part = jnp.sum(delta_wide, axis=(0, 2, 3, 4))
        return grad_part[0], weight_part, bias_part

    grad_input, weight_parts, bias_parts = lax.map(one_cube, (inputs, cotangent))
    norm_scale = float(CUBES * DEPTH * HEIGHT * WID) ** -0.5
    return grad_input, jnp.sum(weight_parts, axis=0) * norm_scale, jnp.sum(bias_parts, axis=0) * norm_scale
```

```python
import jax
import jax.numpy as jnp
from jax import lax
from jax.experimental import pallas as pl
from jax.experimental.pallas import tpu as pltpu
from jax.sharding import PartitionSpec as P

F32 = jnp.float32
BF16 = jnp.bfloat16
AXES = ("depth", "height", "dp")


def exchange(low_edge, high_edge, axis):
    count = lax.axis_size(axis)
    if count == 1:
        return jnp.zeros_like(high_edge), jnp.zeros_like(low_edge)
    if count == 2:
        first = lax.axis_index(axis) == 0
        got = lax.ppermute(jnp.where(first, high_edge, low_edge), axis, [(0, 1), (1, 0)])
        none = jnp.zeros_like(got)
        return jnp.where(first, none, got), jnp.where(first, got, none)
    up = [(i, i + 1) for i in range(count - 1)]
    down = [(i + 1, i) for i in range(count - 1)]
    return lax.ppermute(high_edge, axis, up), lax.ppermute(low_edge, axis, down)


def halo(field):
    below, above = exchange(field[0], field[-1], "depth")

    def column(at):
        return jnp.concatenate([below[at][None], field[:, at], above[at][None]], axis=0)

    left, right = exchange(column(0), column(-1), "height")
    return below, above, left, right


def swap(array, axis, bit):
    return lax.ppermute(array, axis, [(i, i ^ bit) for i in range(lax.axis_size(axis))])


def padded_row(core, below, above, left, right, d, h):
    depth, height = core.shape[0], core.shape[1]
    if h == 0:
        return left[d]
    if h == height + 1:
        return right[d]
    if d == 0:
        return below[h - 1]
    if d == depth + 1:
        return above[h - 1]
    return core[d - 1, h - 1]


def fill_patches(refs, patches):
    depth, height, chans, width = refs[0].shape
    for d in range(depth + 2):
        for row in range(height + 2):
            value = padded_row(*refs, d, row)
            for b in range(3):
                h = row - b
                if 0 <= h < height:
                    patches[pl.ds((d * 3 + b) * chans, chans), pl.ds(h * width, width)] = value


def shifted(value, step):
    if step == 0:
        return value
    width = value.shape[1]
    lane = lax.broadcasted_iota(jnp.int32, value.shape, 1)
    edge = width - 1 if step == 1 else 0
    return jnp.where(lane == edge, 0.0, pltpu.roll(value, (-step) % width, 1))


def forward_kernel(x, below, above, left, right, w1, bias, cot, delta, payload, patches, grad):
    depth, height, ci, width = x.shape
    co = cot.shape[2]
    fill_patches((x, below, above, left, right), patches)
    shift_bias = jnp.broadcast_to(bias[...], (co, width))
    bias_acc = jnp.zeros((co, width), F32)
    for d in range(depth):
        window = pl.ds(d * 3 * ci, 9 * ci)
        taps = jnp.dot(w1[...], patches[window, :], preferred_element_type=F32)
        blocks = [[], [], []]
        for h in range(height):
            lanes = slice(h * width, (h + 1) * width)
            linear = taps[co : 2 * co, lanes] + shift_bias
            linear = linear + shifted(taps[:co, lanes], -1) + shifted(taps[2 * co :, lanes], 1)
            sigma = 1.0 / (1.0 + jnp.exp(-linear))
            slope = cot[d, h].astype(F32) * sigma * (1.0 + linear * (1.0 - sigma))
            rounded = slope.astype(BF16)
            delta[d, h] = rounded
            wide = rounded.astype(F32)
            bias_acc = bias_acc + wide
            blocks[0].append(shifted(wide, 1).astype(BF16))
            blocks[1].append(rounded)
            blocks[2].append(shifted(wide, -1).astype(BF16))
        slopes = jnp.concatenate([jnp.concatenate(part, axis=1) for part in blocks], axis=0)
        term = lax.dot_general(
            patches[window, :], slopes, (((1,), (1,)), ((), ())), preferred_element_type=F32
        )
        if d == 0:
            grad[...] = term
        else:
            grad[...] += term
    rows = 9 * ci
    payload[0:rows, :] = grad[:, : 2 * co]
    payload[rows : rows + rows // 2, :co] = grad[: rows // 2, 2 * co :]
    payload[rows : rows + rows // 2, co:] = grad[rows // 2 :, 2 * co :]
    tail = rows + rows // 2
    total = jnp.sum(bias_acc.T, axis=0, keepdims=True)
    left_over = payload.shape[0] - tail
    row_at = lax.broadcasted_iota(jnp.int32, (left_over, co), 0)
    payload[tail:, :co] = jnp.where(row_at == 0, jnp.broadcast_to(total, (left_over, co)), 0.0)
    payload[tail:, co:] = jnp.zeros((left_over, payload.shape[1] - co), F32)


def input_kernel(delta, below, above, left, right, w2, out, patches):
    depth, height, co, width = delta.shape
    ci = out.shape[2]
    fill_patches((delta, below, above, left, right), patches)
    for d in range(depth):
        taps = jnp.dot(w2[...], patches[pl.ds(d * 3 * co, 9 * co), :], preferred_element_type=F32)
        for h in range(height):
            lanes = slice(h * width, (h + 1) * width)
            total = taps[ci : 2 * ci, lanes]
            total = total + shifted(taps[:ci, lanes], 1) + shifted(taps[2 * ci :, lanes], -1)
            out[d, h] = total.astype(BF16)


def unpack_kernel(scale, low, high, weight_out, bias_out, full):
    half = low.shape[0]
    co = bias_out.shape[1]
    full[:half, :] = low[...] * scale
    full[half:, :] = high[...] * scale
    rows = weight_out.shape[0] // 3
    ci = rows // 9
    step = ci // 2
    for j in range(9):
        for part in range(2):
            source = j * ci + part * step
            to = 3 * j * ci + part * step
            weight_out[pl.ds(to, step), :] = full[pl.ds(source, step), :co]
            weight_out[pl.ds(to + ci, step), :] = full[pl.ds(source, step), co:]
            at = rows + source % (rows // 2)
            lanes = slice(0, co) if source < rows // 2 else slice(co, 2 * co)
            weight_out[pl.ds(to + 2 * ci, step), :] = full[pl.ds(at, step), lanes]
    bias_out[...] = full[rows + rows // 2 : rows + rows // 2 + 1, :co]


def call(kernel, outs, scratch, flops, *args):
    size = sum(a.size * a.dtype.itemsize for a in args) + sum(o.size * o.dtype.itemsize for o in outs)
    return pl.pallas_call(
        kernel,
        out_shape=outs,
        scratch_shapes=scratch,
        compiler_params=pltpu.CompilerParams(vmem_limit_bytes=40 << 20),
        cost_estimate=pl.CostEstimate(flops=flops, bytes_accessed=size, transcendentals=0),
    )(*args)


def summed(total):
    stages = []
    for axis in AXES:
        count = lax.axis_size(axis)
        assert count & (count - 1) == 0
        stages += [(axis, 1 << bit) for bit in range(count.bit_length() - 1)]
    half = total.shape[0] // 2
    low, high = total[:half], total[half:]
    scattered = bool(stages) and stages[0] == ("depth", 1)
    if scattered:
        first = lax.axis_index("depth") % 2 == 0
        got = swap(jnp.where(first, high, low), "depth", 1)
        part = jnp.where(first, low, high) + got
        stages = stages[1:]
    else:
        part = total
    for axis, bit in stages:
        own = lax.reduce_precision(part, 8, 7)
        part = own + swap(own.astype(BF16), axis, bit).astype(F32)
    if not scattered:
        return part[:half], part[half:]
    other = swap(part, "depth", 1)
    return jnp.where(first, part, other), jnp.where(first, other, part)


def local(inputs, weight, bias, cotangent):
    cubes, ci, depth, height, width = inputs.shape
    co = cotangent.shape[1]
    taps = weight.transpose(2, 3, 4, 1, 0)
    w1 = taps.transpose(2, 4, 0, 1, 3).reshape(3 * co, 9 * ci)
    w2 = jnp.flip(taps, (0, 1)).transpose(2, 3, 0, 1, 4).reshape(3 * ci, 9 * co)
    payload_rows = 9 * ci + 9 * ci // 2 + 16
    voxels = cubes * depth * height * width
    total = None
    grads = []
    for cube in range(cubes):
        x = inputs[cube].transpose(1, 2, 0, 3)
        cot = cotangent[cube].transpose(1, 2, 0, 3)
        flops = 2 * depth * height * width * 27 * ci * co
        delta, payload = call(
            forward_kernel,
            (
                jax.ShapeDtypeStruct((depth, height, co, width), BF16),
                jax.ShapeDtypeStruct((payload_rows, 2 * co), F32),
            ),
            [
                pltpu.VMEM(((depth + 2) * 3 * ci, height * width), BF16),
                pltpu.VMEM((9 * ci, 3 * co), F32),
            ],
            2 * flops,
            x,
            *halo(x),
            w1,
            bias[:, None],
            cot,
        )
        total = payload if total is None else total + payload
        (grad,) = call(
            input_kernel,
            (jax.ShapeDtypeStruct((depth, height, ci, width), BF16),),
            [pltpu.VMEM(((depth + 2) * 3 * co, height * width), BF16)],
            flops,
            delta,
            *halo(delta),
            w2,
        )
        grads.append(grad.transpose(2, 0, 1, 3))
    for axis in AXES:
        voxels *= lax.axis_size(axis)
    scale = float(voxels) ** -0.5
    low, high = summed(total)
    grad_taps, grad_bias = call(
        lambda *refs: unpack_kernel(scale, *refs),
        (jax.ShapeDtypeStruct((27 * ci, co), F32), jax.ShapeDtypeStruct((1, co), F32)),
        [pltpu.VMEM((payload_rows, 2 * co), F32)],
        payload_rows * 2 * co,
        low,
        high,
    )
    grad_weight = grad_taps.reshape(3, 3, 3, ci, co).transpose(4, 3, 0, 1, 2)
    return jnp.stack(grads), grad_weight, grad_bias.reshape(co)


def solution(mesh):
    voxels = P("dp", None, "depth", "height", None)
    return jax.shard_map(
        local,
        mesh=mesh,
        in_specs=(voxels, P(), P(), voxels),
        out_specs=(voxels, P(), P()),
        check_vma=False,
    )
```

```python
import jax
import jax.numpy as jnp
from jax import lax
from jax.experimental import pallas as pl
from jax.experimental.pallas import tpu as pltpu
from jax.sharding import PartitionSpec as P

F32 = jnp.float32
BF16 = jnp.bfloat16
AXES = ("depth", "height", "dp")


def exchange(low_edge, high_edge, axis):
    count = lax.axis_size(axis)
    none = jnp.zeros_like(low_edge)
    if count == 1:
        return none, none
    at = lax.axis_index(axis)
    if count % 2:
        up = [(i, i + 1) for i in range(count - 1)]
        down = [(i + 1, i) for i in range(count - 1)]
        return lax.ppermute(high_edge, axis, up), lax.ppermute(low_edge, axis, down)
    even = at % 2 == 0
    inner = [(i, i ^ 1) for i in range(count)]
    got = lax.ppermute(jnp.where(even, high_edge, low_edge), axis, inner)
    if count == 2:
        return jnp.where(even, none, got), jnp.where(even, got, none)
    outer = [(i, (i - 1 if i % 2 == 0 else i + 1) % count) for i in range(count)]
    other = lax.ppermute(jnp.where(even, low_edge, high_edge), axis, outer)
    below = jnp.where(at == 0, none, jnp.where(even, other, got))
    above = jnp.where(at == count - 1, none, jnp.where(even, got, other))
    return below, above


def height_halo(first_row, last_row, below, above):
    def column(rows, at):
        return jnp.concatenate([below[at][None], rows, above[at][None]], axis=0)

    return exchange(column(first_row, 0), column(last_row, -1), "height")


def swap(array, axis, mask):
    return lax.ppermute(array, axis, [(i, i ^ mask) for i in range(lax.axis_size(axis))])


def fill_patches(row_of, depth, rows, patches):
    chans, width = row_of(1, 1).shape
    for d in range(depth + 2):
        for at, h in enumerate(rows):
            for b in range(3):
                patches[pl.ds((d * 3 + b) * chans, chans), pl.ds(at * width, width)] = row_of(d, h + b)


def shifted(value, step):
    if step == 0:
        return value
    width = value.shape[1]
    lane = lax.broadcasted_iota(jnp.int32, value.shape, 1)
    edge = width - 1 if step == 1 else 0
    return jnp.where(lane == edge, 0.0, pltpu.roll(value, (-step) % width, 1))


def forward_rows(row_of, rows, w1, bias, cot, delta, before, payload, patches, grad):
    depth, co = cot.shape[0], cot.shape[2]
    width = cot.shape[3]
    ci = row_of(1, 1).shape[0]
    fill_patches(row_of, depth, rows, patches)
    shift_bias = jnp.broadcast_to(bias[...], (co, width))
    bias_acc = jnp.zeros((co, width), F32)
    for d in range(depth):
        window = pl.ds(d * 3 * ci, 9 * ci)
        taps = jnp.dot(w1[...], patches[window, :], preferred_element_type=F32)
        blocks = [[], [], []]
        for at, h in enumerate(rows):
            lanes = slice(at * width, (at + 1) * width)
            linear = taps[co : 2 * co, lanes] + shift_bias
            linear = linear + shifted(taps[:co, lanes], -1) + shifted(taps[2 * co :, lanes], 1)
            sigma = 1.0 / (1.0 + jnp.exp(-linear))
            slope = cot[d, h].astype(F32) * sigma * (1.0 + linear * (1.0 - sigma))
            rounded = slope.astype(BF16)
            delta[at, d] = rounded
            wide = rounded.astype(F32)
            bias_acc = bias_acc + wide
            blocks[0].append(shifted(wide, 1).astype(BF16))
            blocks[1].append(rounded)
            blocks[2].append(shifted(wide, -1).astype(BF16))
        slopes = jnp.concatenate([jnp.concatenate(part, axis=1) for part in blocks], axis=0)
        term = lax.dot_general(
            patches[window, :], slopes, (((1,), (1,)), ((), ())), preferred_element_type=F32
        )
        if d == 0:
            grad[...] = term
        else:
            grad[...] += term
    taps_rows = 9 * ci
    tail = taps_rows + taps_rows // 2
    total = jnp.sum(bias_acc.T, axis=0, keepdims=True)
    left_over = payload.shape[0] - tail
    row_at = lax.broadcasted_iota(jnp.int32, (left_over, co), 0)
    bias_rows = jnp.where(row_at == 0, jnp.broadcast_to(total, (left_over, co)), 0.0)
    zeros = jnp.zeros((left_over, payload.shape[1] - co), F32)
    for at, value in (
        (pl.ds(0, taps_rows), grad[:, : 2 * co]),
        (
            pl.ds(taps_rows, taps_rows // 2),
            jnp.concatenate(
                [grad[: taps_rows // 2, 2 * co :], grad[taps_rows // 2 :, 2 * co :]], axis=1
            ),
        ),
        (pl.ds(tail, left_over), jnp.concatenate([bias_rows, zeros], axis=1)),
    ):
        payload[at, :] = value if before is None else before[at, :] + value


def inner_kernel(x, below, above, w1, bias, cot, delta, payload, patches, grad):
    depth, height = x.shape[:2]

    def row_of(d, h):
        return below[h - 1] if d == 0 else above[h - 1] if d == depth + 1 else x[d - 1, h - 1]

    rows = range(1, height - 1)
    forward_rows(row_of, rows, w1, bias, cot, delta, None, payload, patches, grad)


def outer_kernel(x, below, above, left, right, w1, bias, cot, before, delta, payload, patches, grad):
    depth, height = x.shape[:2]

    def row_of(d, h):
        if h == 0:
            return left[d]
        if h == height + 1:
            return right[d]
        return below[h - 1] if d == 0 else above[h - 1] if d == depth + 1 else x[d - 1, h - 1]

    rows = (0, height - 1)
    forward_rows(row_of, rows, w1, bias, cot, delta, before, payload, patches, grad)


def input_kernel(inner, outer, below, above, left, right, w2, out, patches):
    co, width = inner.shape[2:]
    depth, height, ci = out.shape[:3]

    def row_of(d, h):
        if h == 0:
            return left[d]
        if h == height + 1:
            return right[d]
        if d == 0:
            return below[h - 1]
        if d == depth + 1:
            return above[h - 1]
        return outer[0, d - 1] if h == 1 else outer[1, d - 1] if h == height else inner[h - 2, d - 1]

    fill_patches(row_of, depth, range(height), patches)
    for d in range(depth):
        taps = jnp.dot(w2[...], patches[pl.ds(d * 3 * co, 9 * co), :], preferred_element_type=F32)
        for h in range(height):
            lanes = slice(h * width, (h + 1) * width)
            total = taps[ci : 2 * ci, lanes]
            total = total + shifted(taps[:ci, lanes], 1) + shifted(taps[2 * ci :, lanes], -1)
            out[d, h] = total.astype(BF16)


def unpack_kernel(scale, low, high, weight_out, bias_out, full):
    half = low.shape[0]
    co = bias_out.shape[1]
    full[:half, :] = low[...] * scale
    full[half:, :] = high[...] * scale
    rows = weight_out.shape[0] // 3
    ci = rows // 9
    step = ci // 2
    for j in range(9):
        for part in range(2):
            source = j * ci + part * step
            to = 3 * j * ci + part * step
            weight_out[pl.ds(to, step), :] = full[pl.ds(source, step), :co]
            weight_out[pl.ds(to + ci, step), :] = full[pl.ds(source, step), co:]
            at = rows + source % (rows // 2)
            lanes = slice(0, co) if source < rows // 2 else slice(co, 2 * co)
            weight_out[pl.ds(to + 2 * ci, step), :] = full[pl.ds(at, step), lanes]
    bias_out[...] = full[rows + rows // 2 : rows + rows // 2 + 1, :co]


def call(kernel, outs, scratch, flops, *args):
    size = sum(a.size * a.dtype.itemsize for a in args) + sum(o.size * o.dtype.itemsize for o in outs)
    return pl.pallas_call(
        kernel,
        out_shape=outs,
        scratch_shapes=scratch,
        compiler_params=pltpu.CompilerParams(vmem_limit_bytes=40 << 20),
        cost_estimate=pl.CostEstimate(flops=flops, bytes_accessed=size, transcendentals=0),
    )(*args)


def gathered_sum(part, axis, masks):
    own = lax.reduce_precision(part, 8, 7)
    sent = own.astype(BF16)
    terms = [own] + [swap(sent, axis, mask).astype(F32) for mask in masks]
    while len(terms) > 1:
        terms = [terms[i] + terms[i + 1] for i in range(0, len(terms), 2)]
    return terms[0]


def summed(total, meanwhile, work):
    half = total.shape[0] // 2
    low, high = total[:half], total[half:]
    first = lax.axis_index("depth") % 2 == 0
    got = swap(jnp.where(first, high, low), "depth", 1)
    part = jnp.where(first, low, high) + got
    for axis in AXES:
        count = lax.axis_size(axis)
        assert count & (count - 1) == 0
        if axis == AXES[-1]:
            part, meanwhile = lax.optimization_barrier((part, meanwhile))
        bit = 2 if axis == "depth" else 1
        while bit < count:
            masks = [bit, 2 * bit, 3 * bit] if 2 * bit < count else [bit]
            part = gathered_sum(part, axis, masks)
            bit *= len(masks) + 1
    part, done = lax.optimization_barrier((part, work(meanwhile)))
    other = swap(part, "depth", 1)
    return jnp.where(first, part, other), jnp.where(first, other, part), done


def local(inputs, weight, bias, cotangent):
    cubes, ci, depth, height, width = inputs.shape
    co = cotangent.shape[1]
    taps = weight.transpose(2, 3, 4, 1, 0)
    w1 = taps.transpose(2, 4, 0, 1, 3).reshape(3 * co, 9 * ci)
    w2 = jnp.flip(taps, (0, 1)).transpose(2, 3, 0, 1, 4).reshape(3 * ci, 9 * co)
    w1, w2 = lax.optimization_barrier((w1, w2))
    column = bias[:, None]
    payload_rows = 9 * ci + 9 * ci // 2 + 16
    payload_shape = jax.ShapeDtypeStruct((payload_rows, 2 * co), F32)
    flops = 2 * depth * width * 27 * ci * co
    total = None
    fields = []
    for cube in range(cubes):
        edges = exchange(inputs[cube][:, 0], inputs[cube][:, -1], "depth")
        below, above = (edge.transpose(1, 0, 2) for edge in edges)
        x = inputs[cube].transpose(1, 2, 0, 3)
        cot = cotangent[cube].transpose(1, 2, 0, 3)

        def forward(kernel, rows, *args):
            return call(
                kernel,
                (jax.ShapeDtypeStruct((rows, depth, co, width), BF16), payload_shape),
                [
                    pltpu.VMEM(((depth + 2) * 3 * ci, rows * width), BF16),
                    pltpu.VMEM((9 * ci, 3 * co), F32),
                ],
                2 * flops * rows,
                *args,
            )

        inner, part = forward(inner_kernel, height - 2, x, below, above, w1, column, cot)
        sides = height_halo(x[:, 0], x[:, -1], below, above)
        outer, part = forward(outer_kernel, 2, x, below, above, *sides, w1, column, cot, part)
        total = part if total is None else total + part

        def layer(at):
            return jnp.concatenate([outer[:1, at], inner[:, at], outer[1:, at]], axis=0)

        below, above = exchange(layer(0), layer(-1), "depth")
        sides = height_halo(outer[0], outer[1], below, above)
        fields.append((inner, outer, below, above, *sides))

    def input_gradients(fields):
        grads = []
        for field in fields:
            (grad,) = call(
                input_kernel,
                (jax.ShapeDtypeStruct((depth, height, ci, width), BF16),),
                [pltpu.VMEM(((depth + 2) * 3 * co, height * width), BF16)],
                flops * height,
                *field,
                w2,
            )
            grads.append(grad.transpose(2, 0, 1, 3))
        return jnp.stack(grads)

    low, high, grads = summed(total, fields, input_gradients)
    voxels = cubes * depth * height * width
    for axis in AXES:
        voxels *= lax.axis_size(axis)
    scale = float(voxels) ** -0.5
    grad_taps, grad_bias = call(
        lambda *refs: unpack_kernel(scale, *refs),
        (jax.ShapeDtypeStruct((27 * ci, co), F32), jax.ShapeDtypeStruct((1, co), F32)),
        [pltpu.VMEM((payload_rows, 2 * co), F32)],
        payload_rows * 2 * co,
        low,
        high,
    )
    grad_weight = grad_taps.reshape(3, 3, 3, ci, co).transpose(4, 3, 0, 1, 2)
    return grads, grad_weight, grad_bias.reshape(co)


def solution(mesh):
    voxels = P("dp", None, "depth", "height", None)
    return jax.shard_map(
        local,
        mesh=mesh,
        in_specs=(voxels, P(), P(), voxels),
        out_specs=(voxels, P(), P()),
        check_vma=False,
    )
```

```python
import jax
import jax.numpy as jnp
from jax import lax
from jax.experimental import pallas as pl
from jax.experimental.pallas import tpu as pltpu
from jax.sharding import PartitionSpec as P

F32 = jnp.float32
BF16 = jnp.bfloat16
AXES = ("depth", "height", "dp")


def exchange(low_edge, high_edge, axis):
    count = lax.axis_size(axis)
    none = jnp.zeros_like(low_edge)
    if count == 1:
        return none, none
    at = lax.axis_index(axis)
    if count % 2:
        up = [(i, i + 1) for i in range(count - 1)]
        down = [(i + 1, i) for i in range(count - 1)]
        return lax.ppermute(high_edge, axis, up), lax.ppermute(low_edge, axis, down)
    even = at % 2 == 0
    inner = [(i, i ^ 1) for i in range(count)]
    got = lax.ppermute(jnp.where(even, high_edge, low_edge), axis, inner)
    if count == 2:
        return jnp.where(even, none, got), jnp.where(even, got, none)
    outer = [(i, (i - 1 if i % 2 == 0 else i + 1) % count) for i in range(count)]
    other = lax.ppermute(jnp.where(even, low_edge, high_edge), axis, outer)
    below = jnp.where(at == 0, none, jnp.where(even, other, got))
    above = jnp.where(at == count - 1, none, jnp.where(even, got, other))
    return below, above


def height_halo(first_row, last_row, below, above):
    def column(rows, at):
        return jnp.concatenate([below[at][None], rows, above[at][None]], axis=0)

    return exchange(column(first_row, 0), column(last_row, -1), "height")


def swap(array, axis, mask):
    return lax.ppermute(array, axis, [(i, i ^ mask) for i in range(lax.axis_size(axis))])


def fill_patches(row_of, depth, rows, patches):
    chans, width = row_of(1, 1).shape
    for d in range(depth + 2):
        for at, h in enumerate(rows):
            for b in range(3):
                patches[pl.ds((d * 3 + b) * chans, chans), pl.ds(at * width, width)] = row_of(d, h + b)


def shifted(value, step):
    if step == 0:
        return value
    width = value.shape[1]
    lane = lax.broadcasted_iota(jnp.int32, value.shape, 1)
    edge = width - 1 if step == 1 else 0
    return jnp.where(lane == edge, 0.0, pltpu.roll(value, (-step) % width, 1))


def forward_rows(row_of, rows, w1, bias, cot, delta, before, payload, patches, grad):
    depth, co = cot.shape[0], cot.shape[2]
    width = cot.shape[3]
    ci = row_of(1, 1).shape[0]
    fill_patches(row_of, depth, rows, patches)
    shift_bias = jnp.broadcast_to(bias[...], (co, width))
    bias_acc = jnp.zeros((co, width), F32)
    for d in range(depth):
        window = pl.ds(d * 3 * ci, 9 * ci)
        taps = jnp.dot(w1[...], patches[window, :], preferred_element_type=F32)
        blocks = [[], [], []]
        for at, h in enumerate(rows):
            lanes = slice(at * width, (at + 1) * width)
            linear = taps[co : 2 * co, lanes] + shift_bias
            linear = linear + shifted(taps[:co, lanes], -1) + shifted(taps[2 * co :, lanes], 1)
            sigma = 1.0 / (1.0 + jnp.exp(-linear))
            slope = cot[d, h].astype(F32) * sigma * (1.0 + linear * (1.0 - sigma))
            rounded = slope.astype(BF16)
            delta[at, d] = rounded
            wide = rounded.astype(F32)
            bias_acc = bias_acc + wide
            blocks[0].append(shifted(wide, 1).astype(BF16))
            blocks[1].append(rounded)
            blocks[2].append(shifted(wide, -1).astype(BF16))
        slopes = jnp.concatenate([jnp.concatenate(part, axis=1) for part in blocks], axis=0)
        term = lax.dot_general(
            patches[window, :], slopes, (((1,), (1,)), ((), ())), preferred_element_type=F32
        )
        if d == 0:
            grad[...] = term
        else:
            grad[...] += term
    taps_rows = 9 * ci
    tail = taps_rows + taps_rows // 2
    total = jnp.sum(bias_acc.T, axis=0, keepdims=True)
    left_over = payload.shape[0] - tail
    row_at = lax.broadcasted_iota(jnp.int32, (left_over, co), 0)
    bias_rows = jnp.where(row_at == 0, jnp.broadcast_to(total, (left_over, co)), 0.0)
    zeros = jnp.zeros((left_over, payload.shape[1] - co), F32)
    for at, value in (
        (pl.ds(0, taps_rows), grad[:, : 2 * co]),
        (
            pl.ds(taps_rows, taps_rows // 2),
            jnp.concatenate(
                [grad[: taps_rows // 2, 2 * co :], grad[taps_rows // 2 :, 2 * co :]], axis=1
            ),
        ),
        (pl.ds(tail, left_over), jnp.concatenate([bias_rows, zeros], axis=1)),
    ):
        payload[at, :] = value if before is None else before[at, :] + value


def inner_kernel(x, below, above, w1, bias, cot, delta, payload, patches, grad):
    depth, height = x.shape[:2]

    def row_of(d, h):
        return below[h - 1] if d == 0 else above[h - 1] if d == depth + 1 else x[d - 1, h - 1]

    rows = range(1, height - 1)
    forward_rows(row_of, rows, w1, bias, cot, delta, None, payload, patches, grad)


def outer_kernel(x, below, above, left, right, w1, bias, cot, before, delta, payload, patches, grad):
    depth, height = x.shape[:2]

    def row_of(d, h):
        if h == 0:
            return left[d]
        if h == height + 1:
            return right[d]
        return below[h - 1] if d == 0 else above[h - 1] if d == depth + 1 else x[d - 1, h - 1]

    rows = (0, height - 1)
    forward_rows(row_of, rows, w1, bias, cot, delta, before, payload, patches, grad)


def input_kernel(inner, outer, below, above, left, right, w2, out, patches):
    co, width = inner.shape[2:]
    depth, height, ci = out.shape[:3]

    def row_of(d, h):
        if h == 0:
            return left[d]
        if h == height + 1:
            return right[d]
        if d == 0:
            return below[h - 1]
        if d == depth + 1:
            return above[h - 1]
        return outer[0, d - 1] if h == 1 else outer[1, d - 1] if h == height else inner[h - 2, d - 1]

    fill_patches(row_of, depth, range(height), patches)
    for d in range(depth):
        taps = jnp.dot(w2[...], patches[pl.ds(d * 3 * co, 9 * co), :], preferred_element_type=F32)
        for h in range(height):
            lanes = slice(h * width, (h + 1) * width)
            total = taps[ci : 2 * ci, lanes]
            total = total + shifted(taps[:ci, lanes], 1) + shifted(taps[2 * ci :, lanes], -1)
            out[d, h] = total.astype(BF16)


def unpack_kernel(scale, low, high, weight_out, bias_out, full):
    half = low.shape[0]
    co = bias_out.shape[1]
    full[:half, :] = low[...] * scale
    full[half:, :] = high[...] * scale
    rows = weight_out.shape[0] // 3
    ci = rows // 9
    step = ci // 2
    for j in range(9):
        for part in range(2):
            source = j * ci + part * step
            to = 3 * j * ci + part * step
            weight_out[pl.ds(to, step), :] = full[pl.ds(source, step), :co]
            weight_out[pl.ds(to + ci, step), :] = full[pl.ds(source, step), co:]
            at = rows + source % (rows // 2)
            lanes = slice(0, co) if source < rows // 2 else slice(co, 2 * co)
            weight_out[pl.ds(to + 2 * ci, step), :] = full[pl.ds(at, step), lanes]
    bias_out[...] = full[rows + rows // 2 : rows + rows // 2 + 1, :co]


def call(kernel, outs, scratch, flops, *args):
    size = sum(a.size * a.dtype.itemsize for a in args) + sum(o.size * o.dtype.itemsize for o in outs)
    return pl.pallas_call(
        kernel,
        out_shape=outs,
        scratch_shapes=scratch,
        compiler_params=pltpu.CompilerParams(vmem_limit_bytes=40 << 20),
        cost_estimate=pl.CostEstimate(flops=flops, bytes_accessed=size, transcendentals=0),
    )(*args)


def gathered_sum(part, axis, masks):
    own = lax.reduce_precision(part, 8, 7)
    sent = own.astype(BF16)
    terms = [own] + [swap(sent, axis, mask).astype(F32) for mask in masks]
    while len(terms) > 1:
        terms = [terms[i] + terms[i + 1] for i in range(0, len(terms), 2)]
    return terms[0]


def summed(total, meanwhile, work):
    half = total.shape[0] // 2
    low, high = total[:half], total[half:]
    first = lax.axis_index("depth") % 2 == 0
    got = swap(jnp.where(first, high, low), "depth", 1)
    part = jnp.where(first, low, high) + got
    for axis in AXES:
        count = lax.axis_size(axis)
        assert count & (count - 1) == 0
        bit = 2 if axis == "depth" else 1
        while bit < count:
            masks = [bit, 2 * bit, 3 * bit] if 2 * bit < count else [bit]
            part = gathered_sum(part, axis, masks)
            bit *= len(masks) + 1
    part, done = lax.optimization_barrier((part, work(meanwhile)))
    other = swap(part, "depth", 1)
    return jnp.where(first, part, other), jnp.where(first, other, part), done


def local(inputs, weight, bias, cotangent):
    cubes, ci, depth, height, width = inputs.shape
    co = cotangent.shape[1]
    taps = weight.transpose(2, 3, 4, 1, 0)
    w1 = taps.transpose(2, 4, 0, 1, 3).reshape(3 * co, 9 * ci)
    w2 = jnp.flip(taps, (0, 1)).transpose(2, 3, 0, 1, 4).reshape(3 * ci, 9 * co)
    w1, w2 = lax.optimization_barrier((w1, w2))
    column = bias[:, None]
    payload_rows = 9 * ci + 9 * ci // 2 + 16
    payload_shape = jax.ShapeDtypeStruct((payload_rows, 2 * co), F32)
    flops = 2 * depth * width * 27 * ci * co
    total = None
    fields = []
    for cube in range(cubes):
        edges = exchange(inputs[cube][:, 0], inputs[cube][:, -1], "depth")
        below, above = (edge.transpose(1, 0, 2) for edge in edges)
        x = inputs[cube].transpose(1, 2, 0, 3)
        cot = cotangent[cube].transpose(1, 2, 0, 3)

        def forward(kernel, rows, *args):
            return call(
                kernel,
                (jax.ShapeDtypeStruct((rows, depth, co, width), BF16), payload_shape),
                [
                    pltpu.VMEM(((depth + 2) * 3 * ci, rows * width), BF16),
                    pltpu.VMEM((9 * ci, 3 * co), F32),
                ],
                2 * flops * rows,
                *args,
            )

        inner, part = forward(inner_kernel, height - 2, x, below, above, w1, column, cot)
        sides = height_halo(x[:, 0], x[:, -1], below, above)
        outer, part = forward(outer_kernel, 2, x, below, above, *sides, w1, column, cot, part)
        total = part if total is None else total + part

        def layer(at):
            return jnp.concatenate([outer[:1, at], inner[:, at], outer[1:, at]], axis=0)

        below, above = exchange(layer(0), layer(-1), "depth")
        sides = height_halo(outer[0], outer[1], below, above)
        fields.append((inner, outer, below, above, *sides))

    def input_gradients(fields):
        grads = []
        for field in fields:
            (grad,) = call(
                input_kernel,
                (jax.ShapeDtypeStruct((depth, height, ci, width), BF16),),
                [pltpu.VMEM(((depth + 2) * 3 * co, height * width), BF16)],
                flops * height,
                *field,
                w2,
            )
            grads.append(grad.transpose(2, 0, 1, 3))
        return jnp.stack(grads)

    low, high, grads = summed(total, fields, input_gradients)
    voxels = cubes * depth * height * width
    for axis in AXES:
        voxels *= lax.axis_size(axis)
    scale = float(voxels) ** -0.5
    grad_taps, grad_bias = call(
        lambda *refs: unpack_kernel(scale, *refs),
        (jax.ShapeDtypeStruct((27 * ci, co), F32), jax.ShapeDtypeStruct((1, co), F32)),
        [pltpu.VMEM((payload_rows, 2 * co), F32)],
        payload_rows * 2 * co,
        low,
        high,
    )
    grad_weight = grad_taps.reshape(3, 3, 3, ci, co).transpose(4, 3, 0, 1, 2)
    return grads, grad_weight, grad_bias.reshape(co)


def solution(mesh):
    voxels = P("dp", None, "depth", "height", None)
    return jax.shard_map(
        local,
        mesh=mesh,
        in_specs=(voxels, P(), P(), voxels),
        out_specs=(voxels, P(), P()),
        check_vma=False,
    )
```

```python
import jax
import jax.numpy as jnp
from jax import lax
from jax.experimental import pallas as pl
from jax.experimental.layout import Layout, with_layout_constraint
from jax.experimental.pallas import tpu as pltpu
from jax.sharding import PartitionSpec as P

F32 = jnp.float32
BF16 = jnp.bfloat16
AXES = ("depth", "height", "dp")


def exchange(low_edge, high_edge, axis):
    count = lax.axis_size(axis)
    none = jnp.zeros_like(low_edge)
    if count == 1:
        return none, none
    at = lax.axis_index(axis)
    if count % 2:
        up = [(i, i + 1) for i in range(count - 1)]
        down = [(i + 1, i) for i in range(count - 1)]
        return lax.ppermute(high_edge, axis, up), lax.ppermute(low_edge, axis, down)
    even = at % 2 == 0
    inner = [(i, i ^ 1) for i in range(count)]
    got = lax.ppermute(jnp.where(even, high_edge, low_edge), axis, inner)
    if count == 2:
        return jnp.where(even, none, got), jnp.where(even, got, none)
    outer = [(i, (i - 1 if i % 2 == 0 else i + 1) % count) for i in range(count)]
    other = lax.ppermute(jnp.where(even, low_edge, high_edge), axis, outer)
    below = jnp.where(at == 0, none, jnp.where(even, other, got))
    above = jnp.where(at == count - 1, none, jnp.where(even, got, other))
    return below, above


def height_halo(first_row, last_row, below, above):
    def column(rows, at):
        return jnp.concatenate([below[at][None], rows, above[at][None]], axis=0)

    return exchange(column(first_row, 0), column(last_row, -1), "height")


def swap(array, axis, mask):
    return lax.ppermute(array, axis, [(i, i ^ mask) for i in range(lax.axis_size(axis))])


def fill_patches(row_of, depth, rows, patches):
    chans, width = row_of(1, 1).shape
    for d in range(depth + 2):
        for at, h in enumerate(rows):
            for b in range(3):
                patches[pl.ds((d * 3 + b) * chans, chans), pl.ds(at * width, width)] = row_of(d, h + b)


def shifted(value, step):
    if step == 0:
        return value
    width = value.shape[1]
    lane = lax.broadcasted_iota(jnp.int32, value.shape, 1)
    edge = width - 1 if step == 1 else 0
    return jnp.where(lane == edge, 0.0, pltpu.roll(value, (-step) % width, 1))


def forward_rows(row_of, rows, w1, bias, cot, delta, before, payload, patches, taps, slopes, grad):
    depth, co, width = cot.shape[0], cot.shape[2], cot.shape[3]
    ci = row_of(1, 1).shape[0]
    count = len(rows)
    for d in range(depth):
        for at, h in enumerate(rows):
            for a in range(3):
                for b in range(3):
                    lanes = pl.ds((d * count + at) * width, width)
                    patches[pl.ds((a * 3 + b) * ci, ci), lanes] = row_of(d + a, h + b)
    taps[...] = jnp.dot(w1[...], patches[...], preferred_element_type=F32)
    shift_bias = jnp.broadcast_to(bias[...], (co, width))
    bias_acc = jnp.zeros((co, width), F32)
    for d in range(depth):
        for at, h in enumerate(rows):
            lanes = pl.ds((d * count + at) * width, width)
            linear = taps[co : 2 * co, lanes] + shift_bias
            linear = linear + shifted(taps[:co, lanes], -1) + shifted(taps[2 * co :, lanes], 1)
            sigma = 1.0 / (1.0 + jnp.exp(-linear))
            slope = cot[d, h].astype(F32) * sigma * (1.0 + linear * (1.0 - sigma))
            rounded = slope.astype(BF16)
            delta[at, d] = rounded
            wide = rounded.astype(F32)
            bias_acc = bias_acc + wide
            slopes[:co, lanes] = shifted(wide, 1).astype(BF16)
            slopes[co : 2 * co, lanes] = rounded
            slopes[2 * co :, lanes] = shifted(wide, -1).astype(BF16)
    grad[...] = lax.dot_general(
        patches[...], slopes[...], (((1,), (1,)), ((), ())), preferred_element_type=F32
    )
    taps_rows = 9 * ci
    tail = taps_rows + taps_rows // 2
    total = jnp.sum(bias_acc.T, axis=0, keepdims=True)
    left_over = payload.shape[0] - tail
    row_at = lax.broadcasted_iota(jnp.int32, (left_over, co), 0)
    bias_rows = jnp.where(row_at == 0, jnp.broadcast_to(total, (left_over, co)), 0.0)
    zeros = jnp.zeros((left_over, payload.shape[1] - co), F32)
    for at, value in (
        (pl.ds(0, taps_rows), grad[:, : 2 * co]),
        (
            pl.ds(taps_rows, taps_rows // 2),
            jnp.concatenate(
                [grad[: taps_rows // 2, 2 * co :], grad[taps_rows // 2 :, 2 * co :]], axis=1
            ),
        ),
        (pl.ds(tail, left_over), jnp.concatenate([bias_rows, zeros], axis=1)),
    ):
        payload[at, :] = value if before is None else before[at, :] + value


def inner_kernel(x, below, above, w1, bias, cot, delta, payload, *scratch):
    depth, height = x.shape[:2]

    def row_of(d, h):
        return below[h - 1] if d == 0 else above[h - 1] if d == depth + 1 else x[d - 1, h - 1]

    rows = range(1, height - 1)
    forward_rows(row_of, rows, w1, bias, cot, delta, None, payload, *scratch)


def outer_kernel(x, below, above, left, right, w1, bias, cot, before, delta, payload, *scratch):
    depth, height = x.shape[:2]

    def row_of(d, h):
        if h == 0:
            return left[d]
        if h == height + 1:
            return right[d]
        return below[h - 1] if d == 0 else above[h - 1] if d == depth + 1 else x[d - 1, h - 1]

    rows = (0, height - 1)
    forward_rows(row_of, rows, w1, bias, cot, delta, before, payload, *scratch)


def input_kernel(inner, outer, below, above, left, right, w2, out, patches):
    co, width = inner.shape[2:]
    depth, height, ci = out.shape[:3]

    def row_of(d, h):
        if h == 0:
            return left[d]
        if h == height + 1:
            return right[d]
        if d == 0:
            return below[h - 1]
        if d == depth + 1:
            return above[h - 1]
        return outer[0, d - 1] if h == 1 else outer[1, d - 1] if h == height else inner[h - 2, d - 1]

    fill_patches(row_of, depth, range(height), patches)
    for d in range(depth):
        taps = jnp.dot(w2[...], patches[pl.ds(d * 3 * co, 9 * co), :], preferred_element_type=F32)
        for h in range(height):
            lanes = slice(h * width, (h + 1) * width)
            total = taps[ci : 2 * ci, lanes]
            total = total + shifted(taps[:ci, lanes], 1) + shifted(taps[2 * ci :, lanes], -1)
            out[d, h] = total.astype(BF16)


def unpack_kernel(scale, low, high, weight_out, bias_out, full):
    half = low.shape[0]
    co = bias_out.shape[1]
    full[:half, :] = low[...] * scale
    full[half:, :] = high[...] * scale
    rows = weight_out.shape[0] // 3
    ci = rows // 9
    step = ci // 2
    for j in range(9):
        for part in range(2):
            source = j * ci + part * step
            to = 3 * j * ci + part * step
            weight_out[pl.ds(to, step), :] = full[pl.ds(source, step), :co]
            weight_out[pl.ds(to + ci, step), :] = full[pl.ds(source, step), co:]
            at = rows + source % (rows // 2)
            lanes = slice(0, co) if source < rows // 2 else slice(co, 2 * co)
            weight_out[pl.ds(to + 2 * ci, step), :] = full[pl.ds(at, step), lanes]
    bias_out[...] = full[rows + rows // 2 : rows + rows // 2 + 1, :co]


def call(kernel, outs, scratch, flops, *args):
    size = sum(a.size * a.dtype.itemsize for a in args) + sum(o.size * o.dtype.itemsize for o in outs)
    return pl.pallas_call(
        kernel,
        out_shape=outs,
        scratch_shapes=scratch,
        compiler_params=pltpu.CompilerParams(vmem_limit_bytes=40 << 20),
        cost_estimate=pl.CostEstimate(flops=flops, bytes_accessed=size, transcendentals=0),
    )(*args)


def gathered_sum(part, axis, masks):
    own = lax.reduce_precision(part, 8, 7)
    sent = own.astype(BF16)
    terms = [own] + [swap(sent, axis, mask).astype(F32) for mask in masks]
    while len(terms) > 1:
        terms = [terms[i] + terms[i + 1] for i in range(0, len(terms), 2)]
    return terms[0]


def summed(total, meanwhile, work):
    half = total.shape[0] // 2
    low, high = total[:half], total[half:]
    first = lax.axis_index("depth") % 2 == 0
    got = swap(jnp.where(first, high, low), "depth", 1)
    part = jnp.where(first, low, high) + got
    for axis in AXES:
        count = lax.axis_size(axis)
        assert count & (count - 1) == 0
        bit = 2 if axis == "depth" else 1
        while bit < count:
            masks = [bit, 2 * bit, 3 * bit] if 2 * bit < count else [bit]
            part = gathered_sum(part, axis, masks)
            bit *= len(masks) + 1
    part, done = lax.optimization_barrier((part, work(meanwhile)))
    other = swap(part, "depth", 1)
    return jnp.where(first, part, other), jnp.where(first, other, part), done


def local(inputs, weight, bias, cotangent):
    cubes, ci, depth, height, width = inputs.shape
    co = cotangent.shape[1]
    payload_rows = 9 * ci + 9 * ci // 2 + 16
    payload_shape = jax.ShapeDtypeStruct((payload_rows, 2 * co), F32)
    flops = 2 * depth * width * 27 * ci * co
    total = None
    fields = []
    edges = exchange(inputs[:, :, 0], inputs[:, :, -1], "depth")
    edges = [with_layout_constraint(edge, Layout((0, 1, 2, 3))) for edge in edges]
    edges, weight, bias, cotangent = lax.optimization_barrier((edges, weight, bias, cotangent))
    taps = weight.transpose(2, 3, 4, 1, 0)
    w1 = taps.transpose(2, 4, 0, 1, 3).reshape(3 * co, 9 * ci)
    column = bias[:, None]
    for cube in range(cubes):
        below, above = (edge[cube].transpose(1, 0, 2) for edge in edges)
        x = inputs[cube].transpose(1, 2, 0, 3)
        cot = cotangent[cube].transpose(1, 2, 0, 3)

        def forward(kernel, rows, *args):
            return call(
                kernel,
                (jax.ShapeDtypeStruct((rows, depth, co, width), BF16), payload_shape),
                [
                    pltpu.VMEM((9 * ci, depth * rows * width), BF16),
                    pltpu.VMEM((3 * co, depth * rows * width), F32),
                    pltpu.VMEM((3 * co, depth * rows * width), BF16),
                    pltpu.VMEM((9 * ci, 3 * co), F32),
                ],
                2 * flops * rows,
                *args,
            )

        inner, part = forward(inner_kernel, height - 2, x, below, above, w1, column, cot)
        sides = height_halo(x[:, 0], x[:, -1], below, above)
        outer, part = forward(outer_kernel, 2, x, below, above, *sides, w1, column, cot, part)
        total = part if total is None else total + part

        def layer(at):
            return jnp.concatenate([outer[:1, at], inner[:, at], outer[1:, at]], axis=0)

        below, above = exchange(layer(0), layer(-1), "depth")
        sides = height_halo(outer[0], outer[1], below, above)
        fields.append((inner, outer, below, above, *sides))

    total, taps = lax.optimization_barrier((total, taps))
    w2 = jnp.flip(taps, (0, 1)).transpose(2, 3, 0, 1, 4).reshape(3 * ci, 9 * co)

    def input_gradients(fields):
        grads = []
        for field in fields:
            (grad,) = call(
                input_kernel,
                (jax.ShapeDtypeStruct((depth, height, ci, width), BF16),),
                [pltpu.VMEM(((depth + 2) * 3 * co, height * width), BF16)],
                flops * height,
                *field,
                w2,
            )
            grads.append(grad.transpose(2, 0, 1, 3))
        return jnp.stack(grads)

    low, high, grads = summed(total, fields, input_gradients)
    voxels = cubes * depth * height * width
    for axis in AXES:
        voxels *= lax.axis_size(axis)
    scale = float(voxels) ** -0.5
    grad_taps, grad_bias = call(
        lambda *refs: unpack_kernel(scale, *refs),
        (jax.ShapeDtypeStruct((27 * ci, co), F32), jax.ShapeDtypeStruct((1, co), F32)),
        [pltpu.VMEM((payload_rows, 2 * co), F32)],
        payload_rows * 2 * co,
        low,
        high,
    )
    grad_weight = grad_taps.reshape(3, 3, 3, ci, co).transpose(4, 3, 0, 1, 2)
    return grads, grad_weight, grad_bias.reshape(co)


def solution(mesh):
    voxels = P("dp", None, "depth", "height", None)
    return jax.shard_map(
        local,
        mesh=mesh,
        in_specs=(voxels, P(), P(), voxels),
        out_specs=(voxels, P(), P()),
        check_vma=False,
    )
```

```python
import jax
import jax.numpy as jnp
from jax import lax
from jax.experimental import pallas as pl
from jax.experimental.layout import Layout, with_layout_constraint
from jax.experimental.pallas import tpu as pltpu
from jax.sharding import PartitionSpec as P

F32 = jnp.float32
BF16 = jnp.bfloat16
AXES = ("depth", "height", "dp")


def paired(axis):
    return lax.axis_index(axis) % 2 == 0 if lax.axis_size(axis) % 2 == 0 else jnp.bool_(True)


def meet(low_edge, high_edge, axis):
    count = lax.axis_size(axis)
    none = jnp.zeros_like(low_edge)
    if count == 1:
        return none, none
    if count % 2:
        up = [(i, i + 1) for i in range(count - 1)]
        down = [(i + 1, i) for i in range(count - 1)]
        return lax.ppermute(high_edge, axis, up), lax.ppermute(low_edge, axis, down)
    at, even = lax.axis_index(axis), paired(axis)
    inner = [(i, i ^ 1) for i in range(count)]
    first = lax.ppermute(jnp.where(even, high_edge, low_edge), axis, inner)
    if count == 2:
        return none, first
    outer = [(i, (i - 1 if i % 2 == 0 else i + 1) % count) for i in range(count)]
    second = lax.ppermute(jnp.where(even, low_edge, high_edge), axis, outer)
    return jnp.where((at == 0) | (at == count - 1), none, second), first


def exchange(low_edge, high_edge, axis):
    second, first = meet(low_edge, high_edge, axis)
    even = paired(axis)
    return jnp.where(even, second, first), jnp.where(even, first, second)


def columns(first_row, last_row, below, above):
    def column(rows, at):
        return jnp.concatenate([below[at][None], rows, above[at][None]], axis=0)

    return column(first_row, 0), column(last_row, -1)


def swap(array, axis, mask):
    return lax.ppermute(array, axis, [(i, i ^ mask) for i in range(lax.axis_size(axis))])


def fill_patches(row_of, depth, rows, patches):
    chans, width = row_of(1, 1).shape
    for d in range(depth + 2):
        for at, h in enumerate(rows):
            for b in range(3):
                patches[pl.ds((d * 3 + b) * chans, chans), pl.ds(at * width, width)] = row_of(d, h + b)


def shifted(value, step):
    if step == 0:
        return value
    width = value.shape[1]
    lane = lax.broadcasted_iota(jnp.int32, value.shape, 1)
    edge = width - 1 if step == 1 else 0
    return jnp.where(lane == edge, 0.0, pltpu.roll(value, (-step) % width, 1))


def forward_rows(count, width, cot_of, w1, bias, delta, before, payload, patches, taps, slopes, grad):
    co = bias.shape[1]
    depth = patches.shape[1] // (count * width)
    taps[...] = jnp.dot(w1[...], patches[...], preferred_element_type=F32)
    shift_bias = jnp.broadcast_to(bias[...], (width, co)).T
    bias_acc = jnp.zeros((co, width), F32)
    for d in range(depth):
        for at in range(count):
            lanes = pl.ds((d * count + at) * width, width)
            linear = taps[co : 2 * co, lanes] + shift_bias
            linear = linear + shifted(taps[:co, lanes], -1) + shifted(taps[2 * co :, lanes], 1)
            sigma = 1.0 / (1.0 + jnp.exp(-linear))
            slope = cot_of(d, at).astype(F32) * sigma * (1.0 + linear * (1.0 - sigma))
            rounded = slope.astype(BF16)
            delta[at, d] = rounded
            wide = rounded.astype(F32)
            bias_acc = bias_acc + wide
            slopes[:co, lanes] = shifted(wide, 1).astype(BF16)
            slopes[co : 2 * co, lanes] = rounded
            slopes[2 * co :, lanes] = shifted(wide, -1).astype(BF16)
    grad[...] = lax.dot_general(
        patches[...], slopes[...], (((1,), (1,)), ((), ())), preferred_element_type=F32
    )
    rows = grad.shape[0]
    tail = rows + rows // 2
    total = jnp.sum(bias_acc.T, axis=0, keepdims=True)
    left_over = payload.shape[0] - tail
    row_at = lax.broadcasted_iota(jnp.int32, (left_over, co), 0)
    bias_rows = jnp.where(row_at == 0, jnp.broadcast_to(total, (left_over, co)), 0.0)
    zeros = jnp.zeros((left_over, payload.shape[1] - co), F32)
    for at, value in (
        (pl.ds(0, rows), grad[:, : 2 * co]),
        (
            pl.ds(rows, rows // 2),
            jnp.concatenate([grad[: rows // 2, 2 * co :], grad[rows // 2 :, 2 * co :]], axis=1),
        ),
        (pl.ds(tail, left_over), jnp.concatenate([bias_rows, zeros], axis=1)),
    ):
        payload[at, :] = value if before is None else before[at, :] + value


def inner_kernel(x, below, above, w1, bias, cot, delta, payload, patches, *scratch):
    depth, height, ci, width = x.shape
    count = height - 2
    for dd in range(depth + 2):
        for hh in range(height):
            row = below[hh] if dd == 0 else above[hh] if dd == depth + 1 else x[dd - 1, hh]
            for a in range(3):
                for b in range(3):
                    d, at = dd - a, hh - b
                    if 0 <= d < depth and 0 <= at < count:
                        patches[pl.ds((a * 3 + b) * ci, ci), pl.ds((d * count + at) * width, width)] = row

    def cot_of(d, at):
        return cot[d, at + 1]

    forward_rows(count, width, cot_of, w1, bias, delta, None, payload, patches, *scratch)


def outer_kernel(last, x, below, above, side, w1, bias, cot, before, delta, payload, patches, *scratch):
    depth, height, ci, width = x.shape
    flag = last[0]
    for dd in range(depth + 2):
        for part in range(3):
            if part == 2:
                row, b = side[dd], 2 * flag
            else:
                h = flag * (height - 2) + part
                row = below[h] if dd == 0 else above[h] if dd == depth + 1 else x[dd - 1, h]
                b = part + 1 - flag
            for a in range(3):
                d = dd - a
                if 0 <= d < depth:
                    to = pl.ds(pl.multiple_of((a * 3 + b) * ci, ci), ci)
                    patches[to, pl.ds(d * width, width)] = row

    def cot_of(d, at):
        return cot[d, flag * (height - 1)]

    forward_rows(1, width, cot_of, w1, bias, delta, before, payload, patches, *scratch)


def input_kernel(inner, top, bottom, below, above, left, right, w2, out, patches):
    depth, co, width = top.shape
    height, ci = out.shape[1:3]

    def row_of(d, h):
        if h == 0:
            return left[d]
        if h == height + 1:
            return right[d]
        if d == 0:
            return below[h - 1]
        if d == depth + 1:
            return above[h - 1]
        return top[d - 1] if h == 1 else bottom[d - 1] if h == height else inner[h - 2, d - 1]

    fill_patches(row_of, depth, range(height), patches)
    for d in range(depth):
        taps = jnp.dot(w2[...], patches[pl.ds(d * 3 * co, 9 * co), :], preferred_element_type=F32)
        for h in range(height):
            lanes = slice(h * width, (h + 1) * width)
            total = taps[ci : 2 * ci, lanes]
            total = total + shifted(taps[:ci, lanes], 1) + shifted(taps[2 * ci :, lanes], -1)
            out[d, h] = total.astype(BF16)


def unpack_kernel(scale, low, high, weight_out, bias_out, full):
    half = low.shape[0]
    co = bias_out.shape[1]
    full[:half, :] = low[...] * scale
    full[half:, :] = high[...] * scale
    rows = weight_out.shape[0] // 3
    ci = rows // 9
    step = ci // 2
    for j in range(9):
        for part in range(2):
            source = j * ci + part * step
            to = 3 * j * ci + part * step
            weight_out[pl.ds(to, step), :] = full[pl.ds(source, step), :co]
            weight_out[pl.ds(to + ci, step), :] = full[pl.ds(source, step), co:]
            at = rows + source % (rows // 2)
            lanes = slice(0, co) if source < rows // 2 else slice(co, 2 * co)
            weight_out[pl.ds(to + 2 * ci, step), :] = full[pl.ds(at, step), lanes]
    bias_out[...] = full[rows + rows // 2 : rows + rows // 2 + 1, :co]


def call(kernel, outs, scratch, flops, *args, scalar=None):
    size = sum(a.size * a.dtype.itemsize for a in args) + sum(o.size * o.dtype.itemsize for o in outs)
    specs = {}
    if scalar is not None:
        vmem = pl.BlockSpec(memory_space=pltpu.VMEM)
        specs["in_specs"] = [pl.BlockSpec(memory_space=pltpu.SMEM)] + [vmem] * len(args)
        args = (scalar.astype(jnp.int32).reshape(1), *args)
    return pl.pallas_call(
        kernel,
        out_shape=outs,
        scratch_shapes=scratch,
        compiler_params=pltpu.CompilerParams(vmem_limit_bytes=40 << 20),
        cost_estimate=pl.CostEstimate(flops=flops, bytes_accessed=size, transcendentals=0),
        **specs,
    )(*args)


def gathered_sum(part, axis, masks):
    own = lax.reduce_precision(part, 8, 7)
    sent = own.astype(BF16)
    terms = [own] + [swap(sent, axis, mask).astype(F32) for mask in masks]
    while len(terms) > 1:
        terms = [terms[i] + terms[i + 1] for i in range(0, len(terms), 2)]
    return terms[0]


def summed(total, meanwhile, work):
    half = total.shape[0] // 2
    low, high = total[:half], total[half:]
    first = lax.axis_index("depth") % 2 == 0
    got = swap(jnp.where(first, high, low), "depth", 1)
    part = jnp.where(first, low, high) + got
    for axis in AXES:
        count = lax.axis_size(axis)
        assert count & (count - 1) == 0
        bit = 2 if axis == "depth" else 1
        while bit < count:
            masks = [bit, 2 * bit, 3 * bit] if 2 * bit < count else [bit]
            part = gathered_sum(part, axis, masks)
            bit *= len(masks) + 1
    part, done = lax.optimization_barrier((part, work(meanwhile)))
    other = swap(part, "depth", 1)
    return jnp.where(first, part, other), jnp.where(first, other, part), done


def local(inputs, weight, bias, cotangent):
    cubes, ci, depth, height, width = inputs.shape
    co = cotangent.shape[1]
    payload_rows = 9 * ci + 9 * ci // 2 + 16
    payload_shape = jax.ShapeDtypeStruct((payload_rows, 2 * co), F32)
    flops = 2 * depth * width * 27 * ci * co
    total = None
    fields = []
    edges = exchange(inputs[:, :, 0], inputs[:, :, -1], "depth")
    edges = [with_layout_constraint(edge, Layout((0, 1, 2, 3))) for edge in edges]
    sides = []
    for cube in range(cubes):
        below, above = (edge[cube].transpose(1, 0, 2) for edge in edges)
        first_row, last_row = (inputs[cube, :, :, at].transpose(1, 0, 2) for at in (0, -1))
        sides.append(columns(first_row, last_row, below, above))
    edges, sides, inputs, weight, bias, cotangent = lax.optimization_barrier(
        (edges, sides, inputs, weight, bias, cotangent)
    )
    taps = weight.transpose(2, 3, 4, 1, 0)
    w1 = taps.transpose(2, 4, 0, 1, 3).reshape(3 * co, 9 * ci)
    bias_row = bias[None]
    above_first = paired("height")
    for cube in range(cubes):
        below, above = (edge[cube].transpose(1, 0, 2) for edge in edges)
        second, first = meet(*sides[cube], "height")
        x = inputs[cube].transpose(1, 2, 0, 3)
        cot = cotangent[cube].transpose(1, 2, 0, 3)

        def forward(kernel, rows, *args, scalar=None):
            return call(
                kernel,
                (jax.ShapeDtypeStruct((rows, depth, co, width), BF16), payload_shape),
                [
                    pltpu.VMEM((9 * ci, depth * rows * width), BF16),
                    pltpu.VMEM((3 * co, depth * rows * width), F32),
                    pltpu.VMEM((3 * co, depth * rows * width), BF16),
                    pltpu.VMEM((9 * ci, 3 * co), F32),
                ],
                2 * flops * rows,
                *args,
                scalar=scalar,
            )

        shared = (x, below, above)
        inner, part = forward(inner_kernel, height - 2, *shared, w1, bias_row, cot)
        late, part = forward(
            outer_kernel, 1, *shared, second, w1, bias_row, cot, part, scalar=~above_first
        )
        early, part = forward(
            outer_kernel, 1, *shared, first, w1, bias_row, cot, part, scalar=above_first
        )
        total = part if total is None else total + part
        top = jnp.where(above_first, late[0], early[0])
        bottom = jnp.where(above_first, early[0], late[0])

        def layer(at):
            return jnp.concatenate([top[at][None], inner[:, at], bottom[at][None]], axis=0)

        below, above = exchange(layer(0), layer(-1), "depth")
        around = exchange(*columns(top, bottom, below, above), "height")
        fields.append((inner, top, bottom, below, above, *around))
    total, taps = lax.optimization_barrier((total, taps))
    w2 = jnp.flip(taps, (0, 1)).transpose(2, 3, 0, 1, 4).reshape(3 * ci, 9 * co)

    def input_gradients(fields):
        grads = []
        for field in fields:
            (grad,) = call(
                input_kernel,
                (jax.ShapeDtypeStruct((depth, height, ci, width), BF16),),
                [pltpu.VMEM(((depth + 2) * 3 * co, height * width), BF16)],
                flops * height,
                *field,
                w2,
            )
            grads.append(grad.transpose(2, 0, 1, 3))
        return jnp.stack(grads)

    low, high, grads = summed(total, fields, input_gradients)
    voxels = cubes * depth * height * width
    for axis in AXES:
        voxels *= lax.axis_size(axis)
    scale = float(voxels) ** -0.5
    grad_taps, grad_bias = call(
        lambda *refs: unpack_kernel(scale, *refs),
        (jax.ShapeDtypeStruct((27 * ci, co), F32), jax.ShapeDtypeStruct((1, co), F32)),
        [pltpu.VMEM((payload_rows, 2 * co), F32)],
        payload_rows * 2 * co,
        low,
        high,
    )
    grad_weight = grad_taps.reshape(3, 3, 3, ci, co).transpose(4, 3, 0, 1, 2)
    return grads, grad_weight, grad_bias.reshape(co)


def solution(mesh):
    voxels = P("dp", None, "depth", "height", None)
    return jax.shard_map(
        local,
        mesh=mesh,
        in_specs=(voxels, P(), P(), voxels),
        out_specs=(voxels, P(), P()),
        check_vma=False,
    )
```

```python
import jax
import jax.numpy as jnp
from jax import lax
from jax.experimental import pallas as pl
from jax.experimental.pallas import tpu as pltpu
from jax.sharding import PartitionSpec as P

F32 = jnp.float32
BF16 = jnp.bfloat16
AXES = ("depth", "height", "dp")


def paired(axis):
    return lax.axis_index(axis) % 2 == 0 if lax.axis_size(axis) % 2 == 0 else jnp.bool_(True)


def meet(low_edge, high_edge, axis):
    count = lax.axis_size(axis)
    none = jnp.zeros_like(low_edge)
    if count == 1:
        return none, none
    if count % 2:
        up = [(i, i + 1) for i in range(count - 1)]
        down = [(i + 1, i) for i in range(count - 1)]
        return lax.ppermute(high_edge, axis, up), lax.ppermute(low_edge, axis, down)
    at, even = lax.axis_index(axis), paired(axis)
    inner = [(i, i ^ 1) for i in range(count)]
    first = lax.ppermute(jnp.where(even, high_edge, low_edge), axis, inner)
    if count == 2:
        return none, first
    outer = [(i, (i - 1 if i % 2 == 0 else i + 1) % count) for i in range(count)]
    second = lax.ppermute(jnp.where(even, low_edge, high_edge), axis, outer)
    return jnp.where((at == 0) | (at == count - 1), none, second), first


def exchange(low_edge, high_edge, axis):
    second, first = meet(low_edge, high_edge, axis)
    even = paired(axis)
    return jnp.where(even, second, first), jnp.where(even, first, second)


def columns(first_row, last_row, below, above):
    def column(rows, at):
        return jnp.concatenate([below[at][None], rows, above[at][None]], axis=0)

    return column(first_row, 0), column(last_row, -1)


def swap(array, axis, mask):
    return lax.ppermute(array, axis, [(i, i ^ mask) for i in range(lax.axis_size(axis))])


def fill_patches(row_of, depth, rows, patches):
    chans, width = row_of(1, 1).shape
    for d in range(depth + 2):
        for at, h in enumerate(rows):
            for b in range(3):
                patches[pl.ds((d * 3 + b) * chans, chans), pl.ds(at * width, width)] = row_of(d, h + b)


def shifted(value, step):
    if step == 0:
        return value
    width = value.shape[1]
    lane = lax.broadcasted_iota(jnp.int32, value.shape, 1)
    edge = width - 1 if step == 1 else 0
    return jnp.where(lane == edge, 0.0, pltpu.roll(value, (-step) % width, 1))


def forward_rows(count, width, cot_of, w1, bias, delta, before, payload, patches, taps, slopes, grad):
    co = bias.shape[1]
    depth = patches.shape[1] // (count * width)
    taps[...] = jnp.dot(w1[...], patches[...], preferred_element_type=F32)
    shift_bias = jnp.broadcast_to(bias[...], (width, co)).T
    bias_acc = jnp.zeros((co, width), F32)
    for d in range(depth):
        for at in range(count):
            lanes = pl.ds((d * count + at) * width, width)
            linear = taps[co : 2 * co, lanes] + shift_bias
            linear = linear + shifted(taps[:co, lanes], -1) + shifted(taps[2 * co :, lanes], 1)
            sigma = 1.0 / (1.0 + jnp.exp(-linear))
            slope = cot_of(d, at).astype(F32) * sigma * (1.0 + linear * (1.0 - sigma))
            rounded = slope.astype(BF16)
            delta[at, d] = rounded
            wide = rounded.astype(F32)
            bias_acc = bias_acc + wide
            slopes[:co, lanes] = shifted(wide, 1).astype(BF16)
            slopes[co : 2 * co, lanes] = rounded
            slopes[2 * co :, lanes] = shifted(wide, -1).astype(BF16)
    grad[...] = lax.dot_general(
        patches[...], slopes[...], (((1,), (1,)), ((), ())), preferred_element_type=F32
    )
    rows = grad.shape[0]
    tail = rows + rows // 2
    total = jnp.sum(bias_acc.T, axis=0, keepdims=True)
    left_over = payload.shape[0] - tail
    row_at = lax.broadcasted_iota(jnp.int32, (left_over, co), 0)
    bias_rows = jnp.where(row_at == 0, jnp.broadcast_to(total, (left_over, co)), 0.0)
    zeros = jnp.zeros((left_over, payload.shape[1] - co), F32)
    for at, value in (
        (pl.ds(0, rows), grad[:, : 2 * co]),
        (
            pl.ds(rows, rows // 2),
            jnp.concatenate([grad[: rows // 2, 2 * co :], grad[rows // 2 :, 2 * co :]], axis=1),
        ),
        (pl.ds(tail, left_over), jnp.concatenate([bias_rows, zeros], axis=1)),
    ):
        payload[at, :] = value if before is None else before[at, :] + value


def inner_kernel(x, below, above, w1, bias, cot, delta, payload, patches, *scratch):
    depth, height, ci, width = x.shape
    count = height - 2
    for dd in range(depth + 2):
        for hh in range(height):
            row = below[hh] if dd == 0 else above[hh] if dd == depth + 1 else x[dd - 1, hh]
            for a in range(3):
                for b in range(3):
                    d, at = dd - a, hh - b
                    if 0 <= d < depth and 0 <= at < count:
                        patches[pl.ds((a * 3 + b) * ci, ci), pl.ds((d * count + at) * width, width)] = row

    def cot_of(d, at):
        return cot[d, at + 1]

    forward_rows(count, width, cot_of, w1, bias, delta, None, payload, patches, *scratch)


def outer_kernel(last, x, below, above, side, w1, bias, cot, before, delta, payload, patches, *scratch):
    depth, height, ci, width = x.shape
    flag = last[0]
    for dd in range(depth + 2):
        for part in range(3):
            if part == 2:
                row, b = side[dd], 2 * flag
            else:
                h = flag * (height - 2) + part
                row = below[h] if dd == 0 else above[h] if dd == depth + 1 else x[dd - 1, h]
                b = part + 1 - flag
            for a in range(3):
                d = dd - a
                if 0 <= d < depth:
                    to = pl.ds(pl.multiple_of((a * 3 + b) * ci, ci), ci)
                    patches[to, pl.ds(d * width, width)] = row

    def cot_of(d, at):
        return cot[d, flag * (height - 1)]

    forward_rows(1, width, cot_of, w1, bias, delta, before, payload, patches, *scratch)


def input_kernel(inner, top, bottom, below, above, left, right, w2, out, patches):
    depth, co, width = top.shape
    height, ci = out.shape[1:3]

    def row_of(d, h):
        if h == 0:
            return left[d]
        if h == height + 1:
            return right[d]
        if d == 0:
            return below[h - 1]
        if d == depth + 1:
            return above[h - 1]
        return top[d - 1] if h == 1 else bottom[d - 1] if h == height else inner[h - 2, d - 1]

    fill_patches(row_of, depth, range(height), patches)
    for d in range(depth):
        taps = jnp.dot(w2[...], patches[pl.ds(d * 3 * co, 9 * co), :], preferred_element_type=F32)
        for h in range(height):
            lanes = slice(h * width, (h + 1) * width)
            total = taps[ci : 2 * ci, lanes]
            total = total + shifted(taps[:ci, lanes], 1) + shifted(taps[2 * ci :, lanes], -1)
            out[d, h] = total.astype(BF16)


def unpack_kernel(scale, low, high, weight_out, bias_out, full):
    half = low.shape[0]
    co = bias_out.shape[1]
    full[:half, :] = low[...] * scale
    full[half:, :] = high[...] * scale
    rows = weight_out.shape[0] // 3
    ci = rows // 9
    step = ci // 2
    for j in range(9):
        for part in range(2):
            source = j * ci + part * step
            to = 3 * j * ci + part * step
            weight_out[pl.ds(to, step), :] = full[pl.ds(source, step), :co]
            weight_out[pl.ds(to + ci, step), :] = full[pl.ds(source, step), co:]
            at = rows + source % (rows // 2)
            lanes = slice(0, co) if source < rows // 2 else slice(co, 2 * co)
            weight_out[pl.ds(to + 2 * ci, step), :] = full[pl.ds(at, step), lanes]
    bias_out[...] = full[rows + rows // 2 : rows + rows // 2 + 1, :co]


def load_kernel(*refs):
    count = len(refs) // 2
    done = refs[-1]
    copies = [pltpu.make_async_copy(refs[i], refs[count + i], done.at[i]) for i in range(count)]
    for copy in copies:
        copy.start()
    for copy in copies:
        copy.wait()


def loaded(*arrays):
    return pl.pallas_call(
        load_kernel,
        out_shape=[jax.ShapeDtypeStruct(a.shape, a.dtype) for a in arrays],
        in_specs=[pl.BlockSpec(memory_space=pltpu.HBM) for a in arrays],
        out_specs=[pl.BlockSpec(memory_space=pltpu.VMEM) for a in arrays],
        scratch_shapes=[pltpu.SemaphoreType.DMA((len(arrays),))],
        compiler_params=pltpu.CompilerParams(vmem_limit_bytes=16 << 20),
    )(*(pltpu.with_memory_space_constraint(a, pltpu.HBM) for a in arrays))


def call(kernel, outs, scratch, flops, *args, scalar=None):
    size = sum(a.size * a.dtype.itemsize for a in args) + sum(o.size * o.dtype.itemsize for o in outs)
    specs = {}
    if scalar is not None:
        vmem = pl.BlockSpec(memory_space=pltpu.VMEM)
        specs["in_specs"] = [pl.BlockSpec(memory_space=pltpu.SMEM)] + [vmem] * len(args)
        args = (scalar.astype(jnp.int32).reshape(1), *args)
    return pl.pallas_call(
        kernel,
        out_shape=outs,
        scratch_shapes=scratch,
        compiler_params=pltpu.CompilerParams(vmem_limit_bytes=40 << 20),
        cost_estimate=pl.CostEstimate(flops=flops, bytes_accessed=size, transcendentals=0),
        **specs,
    )(*args)


def gathered_sum(part, axis, masks):
    own = lax.reduce_precision(part, 8, 7)
    sent = own.astype(BF16)
    terms = [own] + [swap(sent, axis, mask).astype(F32) for mask in masks]
    while len(terms) > 1:
        terms = [terms[i] + terms[i + 1] for i in range(0, len(terms), 2)]
    return terms[0]


def summed(total, meanwhile, work):
    half = total.shape[0] // 2
    low, high = total[:half], total[half:]
    first = lax.axis_index("depth") % 2 == 0
    got = swap(jnp.where(first, high, low), "depth", 1)
    part = jnp.where(first, low, high) + got
    for axis in AXES:
        count = lax.axis_size(axis)
        assert count & (count - 1) == 0
        bit = 2 if axis == "depth" else 1
        while bit < count:
            masks = [bit, 2 * bit, 3 * bit] if 2 * bit < count else [bit]
            part = gathered_sum(part, axis, masks)
            bit *= len(masks) + 1
    part, done = lax.optimization_barrier((part, work(meanwhile)))
    other = swap(part, "depth", 1)
    return jnp.where(first, part, other), jnp.where(first, other, part), done


def local(inputs, weight, bias, cotangent):
    cubes, ci, depth, height, width = inputs.shape
    co = cotangent.shape[1]
    payload_rows = 9 * ci + 9 * ci // 2 + 16
    payload_shape = jax.ShapeDtypeStruct((payload_rows, 2 * co), F32)
    flops = 2 * depth * width * 27 * ci * co
    total = None
    fields = []
    inputs, taps, bias_row, cotangent = loaded(
        inputs, weight.transpose(2, 3, 4, 1, 0), bias[None], cotangent
    )
    edges = exchange(inputs[:, :, 0], inputs[:, :, -1], "depth")
    sides = []
    for cube in range(cubes):
        below, above = (edge[cube].transpose(1, 0, 2) for edge in edges)
        first_row, last_row = (inputs[cube, :, :, at].transpose(1, 0, 2) for at in (0, -1))
        sides.append(columns(first_row, last_row, below, above))
    w1 = taps.transpose(2, 4, 0, 1, 3).reshape(3 * co, 9 * ci)
    above_first = paired("height")
    for cube in range(cubes):
        below, above = (edge[cube].transpose(1, 0, 2) for edge in edges)
        second, first = meet(*sides[cube], "height")
        x = inputs[cube].transpose(1, 2, 0, 3)
        cot = cotangent[cube].transpose(1, 2, 0, 3)

        def forward(kernel, rows, *args, scalar=None):
            return call(
                kernel,
                (jax.ShapeDtypeStruct((rows, depth, co, width), BF16), payload_shape),
                [
                    pltpu.VMEM((9 * ci, depth * rows * width), BF16),
                    pltpu.VMEM((3 * co, depth * rows * width), F32),
                    pltpu.VMEM((3 * co, depth * rows * width), BF16),
                    pltpu.VMEM((9 * ci, 3 * co), F32),
                ],
                2 * flops * rows,
                *args,
                scalar=scalar,
            )

        shared = (x, below, above)
        inner, part = forward(inner_kernel, height - 2, *shared, w1, bias_row, cot)
        late, part = forward(
            outer_kernel, 1, *shared, second, w1, bias_row, cot, part, scalar=~above_first
        )
        early, part = forward(
            outer_kernel, 1, *shared, first, w1, bias_row, cot, part, scalar=above_first
        )
        total = part if total is None else total + part
        top = jnp.where(above_first, late[0], early[0])
        bottom = jnp.where(above_first, early[0], late[0])

        def layer(at):
            return jnp.concatenate([top[at][None], inner[:, at], bottom[at][None]], axis=0)

        below, above = exchange(layer(0), layer(-1), "depth")
        around = exchange(*columns(top, bottom, below, above), "height")
        fields.append((inner, top, bottom, below, above, *around))
    total, taps = lax.optimization_barrier((total, taps))
    w2 = jnp.flip(taps, (0, 1)).transpose(2, 3, 0, 1, 4).reshape(3 * ci, 9 * co)

    def input_gradients(fields):
        grads = []
        for field in fields:
            (grad,) = call(
                input_kernel,
                (jax.ShapeDtypeStruct((depth, height, ci, width), BF16),),
                [pltpu.VMEM(((depth + 2) * 3 * co, height * width), BF16)],
                flops * height,
                *field,
                w2,
            )
            grads.append(grad.transpose(2, 0, 1, 3))
        return jnp.stack(grads)

    low, high, grads = summed(total, fields, input_gradients)
    voxels = cubes * depth * height * width
    for axis in AXES:
        voxels *= lax.axis_size(axis)
    scale = float(voxels) ** -0.5
    grad_taps, grad_bias = call(
        lambda *refs: unpack_kernel(scale, *refs),
        (jax.ShapeDtypeStruct((27 * ci, co), F32), jax.ShapeDtypeStruct((1, co), F32)),
        [pltpu.VMEM((payload_rows, 2 * co), F32)],
        payload_rows * 2 * co,
        low,
        high,
    )
    grad_weight = grad_taps.reshape(3, 3, 3, ci, co).transpose(4, 3, 0, 1, 2)
    return grads, grad_weight, grad_bias.reshape(co)


def solution(mesh):
    voxels = P("dp", None, "depth", "height", None)
    return jax.shard_map(
        local,
        mesh=mesh,
        in_specs=(voxels, P(), P(), voxels),
        out_specs=(voxels, P(), P()),
        check_vma=False,
    )
```

```python
import jax
import jax.numpy as jnp
from jax import lax
from jax.experimental import pallas as pl
from jax.experimental.pallas import tpu as pltpu
from jax.sharding import PartitionSpec as P

F32 = jnp.float32
BF16 = jnp.bfloat16
AXES = ("depth", "height", "dp")


def paired(axis):
    return lax.axis_index(axis) % 2 == 0 if lax.axis_size(axis) % 2 == 0 else jnp.bool_(True)


def meet(low_edge, high_edge, axis):
    count = lax.axis_size(axis)
    none = jnp.zeros_like(low_edge)
    if count == 1:
        return none, none
    if count % 2:
        up = [(i, i + 1) for i in range(count - 1)]
        down = [(i + 1, i) for i in range(count - 1)]
        return lax.ppermute(high_edge, axis, up), lax.ppermute(low_edge, axis, down)
    at, even = lax.axis_index(axis), paired(axis)
    inner = [(i, i ^ 1) for i in range(count)]
    first = lax.ppermute(jnp.where(even, high_edge, low_edge), axis, inner)
    if count == 2:
        return none, first
    outer = [(i, (i - 1 if i % 2 == 0 else i + 1) % count) for i in range(count)]
    second = lax.ppermute(jnp.where(even, low_edge, high_edge), axis, outer)
    return jnp.where((at == 0) | (at == count - 1), none, second), first


def exchange(low_edge, high_edge, axis):
    second, first = meet(low_edge, high_edge, axis)
    even = paired(axis)
    return jnp.where(even, second, first), jnp.where(even, first, second)


def columns(first_row, last_row, below, above):
    def column(rows, at):
        return jnp.concatenate([below[at][None], rows, above[at][None]], axis=0)

    return column(first_row, 0), column(last_row, -1)


def swap(array, axis, mask):
    return lax.ppermute(array, axis, [(i, i ^ mask) for i in range(lax.axis_size(axis))])


def fill_patches(row_of, depth, rows, patches):
    chans, width = row_of(1, 1).shape
    for d in range(depth + 2):
        for at, h in enumerate(rows):
            for b in range(3):
                patches[pl.ds((d * 3 + b) * chans, chans), pl.ds(at * width, width)] = row_of(d, h + b)


def shifted(value, step):
    if step == 0:
        return value
    width = value.shape[1]
    lane = lax.broadcasted_iota(jnp.int32, value.shape, 1)
    edge = width - 1 if step == 1 else 0
    return jnp.where(lane == edge, 0.0, pltpu.roll(value, (-step) % width, 1))


def forward_rows(count, width, cot_of, w1, bias, delta, before, payload, patches, taps, slopes, grad):
    co = bias.shape[1]
    depth = patches.shape[1] // (count * width)
    taps[...] = jnp.dot(w1[...], patches[...], preferred_element_type=F32)
    shift_bias = jnp.broadcast_to(bias[...], (width, co)).T
    bias_acc = jnp.zeros((co, width), F32)
    for d in range(depth):
        for at in range(count):
            lanes = pl.ds((d * count + at) * width, width)
            linear = taps[co : 2 * co, lanes] + shift_bias
            linear = linear + shifted(taps[:co, lanes], -1) + shifted(taps[2 * co :, lanes], 1)
            sigma = 1.0 / (1.0 + jnp.exp(-linear))
            slope = cot_of(d, at).astype(F32) * sigma * (1.0 + linear * (1.0 - sigma))
            rounded = slope.astype(BF16)
            delta[at, d] = rounded
            wide = rounded.astype(F32)
            bias_acc = bias_acc + wide
            slopes[:co, lanes] = shifted(wide, 1).astype(BF16)
            slopes[co : 2 * co, lanes] = rounded
            slopes[2 * co :, lanes] = shifted(wide, -1).astype(BF16)
    grad[...] = lax.dot_general(
        patches[...], slopes[...], (((1,), (1,)), ((), ())), preferred_element_type=F32
    )
    rows = grad.shape[0]
    tail = rows + rows // 2
    total = jnp.sum(bias_acc.T, axis=0, keepdims=True)
    left_over = payload.shape[0] - tail
    row_at = lax.broadcasted_iota(jnp.int32, (left_over, co), 0)
    bias_rows = jnp.where(row_at == 0, jnp.broadcast_to(total, (left_over, co)), 0.0)
    zeros = jnp.zeros((left_over, payload.shape[1] - co), F32)
    for at, value in (
        (pl.ds(0, rows), grad[:, : 2 * co]),
        (
            pl.ds(rows, rows // 2),
            jnp.concatenate([grad[: rows // 2, 2 * co :], grad[rows // 2 :, 2 * co :]], axis=1),
        ),
        (pl.ds(tail, left_over), jnp.concatenate([bias_rows, zeros], axis=1)),
    ):
        payload[at, :] = value if before is None else before[at, :] + value


def inner_kernel(x, below, above, w1, bias, cot, delta, payload, patches, *scratch):
    depth, height, ci, width = x.shape
    count = height - 2
    for dd in range(depth + 2):
        for hh in range(height):
            row = below[hh] if dd == 0 else above[hh] if dd == depth + 1 else x[dd - 1, hh]
            for a in range(3):
                for b in range(3):
                    d, at = dd - a, hh - b
                    if 0 <= d < depth and 0 <= at < count:
                        patches[pl.ds((a * 3 + b) * ci, ci), pl.ds((d * count + at) * width, width)] = row

    def cot_of(d, at):
        return cot[d, at + 1]

    forward_rows(count, width, cot_of, w1, bias, delta, None, payload, patches, *scratch)


def outer_kernel(last, x, below, above, side, w1, bias, cot, before, delta, payload, patches, *scratch):
    depth, height, ci, width = x.shape
    flag = last[0]
    for dd in range(depth + 2):
        for part in range(3):
            if part == 2:
                row, b = side[dd], 2 * flag
            else:
                h = flag * (height - 2) + part
                row = below[h] if dd == 0 else above[h] if dd == depth + 1 else x[dd - 1, h]
                b = part + 1 - flag
            for a in range(3):
                d = dd - a
                if 0 <= d < depth:
                    to = pl.ds(pl.multiple_of((a * 3 + b) * ci, ci), ci)
                    patches[to, pl.ds(d * width, width)] = row

    def cot_of(d, at):
        return cot[d, flag * (height - 1)]

    forward_rows(1, width, cot_of, w1, bias, delta, before, payload, patches, *scratch)


def input_kernel(inner, top, bottom, below, above, left, right, w2, out, patches):
    depth, co, width = top.shape
    height, ci = out.shape[1:3]

    def row_of(d, h):
        if h == 0:
            return left[d]
        if h == height + 1:
            return right[d]
        if d == 0:
            return below[h - 1]
        if d == depth + 1:
            return above[h - 1]
        return top[d - 1] if h == 1 else bottom[d - 1] if h == height else inner[h - 2, d - 1]

    fill_patches(row_of, depth, range(height), patches)
    for d in range(depth):
        taps = jnp.dot(w2[...], patches[pl.ds(d * 3 * co, 9 * co), :], preferred_element_type=F32)
        for h in range(height):
            lanes = slice(h * width, (h + 1) * width)
            total = taps[ci : 2 * ci, lanes]
            total = total + shifted(taps[:ci, lanes], 1) + shifted(taps[2 * ci :, lanes], -1)
            out[d, h] = total.astype(BF16)


def unpack_kernel(scale, low, high, weight_out, bias_out, full):
    half = low.shape[0]
    co = bias_out.shape[1]
    full[:half, :] = low[...] * scale
    full[half:, :] = high[...] * scale
    rows = weight_out.shape[0] // 3
    ci = rows // 9
    step = ci // 2
    for j in range(9):
        for part in range(2):
            source = j * ci + part * step
            to = 3 * j * ci + part * step
            weight_out[pl.ds(to, step), :] = full[pl.ds(source, step), :co]
            weight_out[pl.ds(to + ci, step), :] = full[pl.ds(source, step), co:]
            at = rows + source % (rows // 2)
            lanes = slice(0, co) if source < rows // 2 else slice(co, 2 * co)
            weight_out[pl.ds(to + 2 * ci, step), :] = full[pl.ds(at, step), lanes]
    bias_out[...] = full[rows + rows // 2 : rows + rows // 2 + 1, :co]


def chunks(shape):
    parts = 8 if shape[1] % 8 == 0 and len(shape) > 2 else 1
    step = shape[1] // parts
    return [(slice(None), slice(i * step, (i + 1) * step)) for i in range(parts)]


def load_kernel(*refs):
    count = len(refs) // 2
    copies = []
    for source, target in zip(refs[:count], refs[count : 2 * count]):
        for at in chunks(source.shape):
            copies.append(pltpu.make_async_copy(source.at[at], target.at[at], refs[-1].at[len(copies)]))
    for copy in copies:
        copy.start()
    for copy in copies:
        copy.wait()


def loaded(*arrays):
    return pl.pallas_call(
        load_kernel,
        out_shape=[jax.ShapeDtypeStruct(a.shape, a.dtype) for a in arrays],
        in_specs=[pl.BlockSpec(memory_space=pltpu.HBM) for a in arrays],
        out_specs=[pl.BlockSpec(memory_space=pltpu.VMEM) for a in arrays],
        scratch_shapes=[pltpu.SemaphoreType.DMA((sum(len(chunks(a.shape)) for a in arrays),))],
        compiler_params=pltpu.CompilerParams(vmem_limit_bytes=16 << 20),
    )(*(pltpu.with_memory_space_constraint(a, pltpu.HBM) for a in arrays))


def call(kernel, outs, scratch, flops, *args, scalar=None):
    size = sum(a.size * a.dtype.itemsize for a in args) + sum(o.size * o.dtype.itemsize for o in outs)
    specs = {}
    if scalar is not None:
        vmem = pl.BlockSpec(memory_space=pltpu.VMEM)
        specs["in_specs"] = [pl.BlockSpec(memory_space=pltpu.SMEM)] + [vmem] * len(args)
        args = (scalar.astype(jnp.int32).reshape(1), *args)
    return pl.pallas_call(
        kernel,
        out_shape=outs,
        scratch_shapes=scratch,
        compiler_params=pltpu.CompilerParams(vmem_limit_bytes=40 << 20),
        cost_estimate=pl.CostEstimate(flops=flops, bytes_accessed=size, transcendentals=0),
        **specs,
    )(*args)


def gathered_sum(part, axis, masks):
    own = lax.reduce_precision(part, 8, 7)
    sent = own.astype(BF16)
    terms = [own] + [swap(sent, axis, mask).astype(F32) for mask in masks]
    while len(terms) > 1:
        terms = [terms[i] + terms[i + 1] for i in range(0, len(terms), 2)]
    return terms[0]


def summed(total, meanwhile, work):
    half = total.shape[0] // 2
    low, high = total[:half], total[half:]
    first = lax.axis_index("depth") % 2 == 0
    got = swap(jnp.where(first, high, low), "depth", 1)
    part = jnp.where(first, low, high) + got
    for axis in ("depth", "dp", "height"):
        count = lax.axis_size(axis)
        assert count & (count - 1) == 0
        bit = 2 if axis == "depth" else 1
        while bit < count:
            masks = [bit, 2 * bit, 3 * bit] if 2 * bit < count else [bit]
            part = gathered_sum(part, axis, masks)
            bit *= len(masks) + 1
    part, done = lax.optimization_barrier((part, work(meanwhile)))
    other = swap(part, "depth", 1)
    return jnp.where(first, part, other), jnp.where(first, other, part), done


def local(inputs, weight, bias, cotangent):
    cubes, ci, depth, height, width = inputs.shape
    co = cotangent.shape[1]
    payload_rows = 9 * ci + 9 * ci // 2 + 16
    payload_shape = jax.ShapeDtypeStruct((payload_rows, 2 * co), F32)
    flops = 2 * depth * width * 27 * ci * co
    total = None
    fields = []
    inputs, taps, bias_row, cotangent = loaded(
        inputs, weight.transpose(2, 3, 4, 1, 0), bias[None], cotangent
    )
    edges = exchange(inputs[:, :, 0], inputs[:, :, -1], "depth")
    sides = []
    for cube in range(cubes):
        below, above = (edge[cube].transpose(1, 0, 2) for edge in edges)
        first_row, last_row = (inputs[cube, :, :, at].transpose(1, 0, 2) for at in (0, -1))
        sides.append(columns(first_row, last_row, below, above))
    w1 = taps.transpose(2, 4, 0, 1, 3).reshape(3 * co, 9 * ci)
    above_first = paired("height")
    for cube in range(cubes):
        below, above = (edge[cube].transpose(1, 0, 2) for edge in edges)
        second, first = meet(*sides[cube], "height")
        x = inputs[cube].transpose(1, 2, 0, 3)
        cot = cotangent[cube].transpose(1, 2, 0, 3)

        def forward(kernel, rows, *args, scalar=None):
            return call(
                kernel,
                (jax.ShapeDtypeStruct((rows, depth, co, width), BF16), payload_shape),
                [
                    pltpu.VMEM((9 * ci, depth * rows * width), BF16),
                    pltpu.VMEM((3 * co, depth * rows * width), F32),
                    pltpu.VMEM((3 * co, depth * rows * width), BF16),
                    pltpu.VMEM((9 * ci, 3 * co), F32),
                ],
                2 * flops * rows,
                *args,
                scalar=scalar,
            )

        shared = (x, below, above)
        inner, part = forward(inner_kernel, height - 2, *shared, w1, bias_row, cot)
        part, taps = lax.optimization_barrier((part, taps))
        w2 = jnp.flip(taps, (0, 1)).transpose(2, 3, 0, 1, 4).reshape(3 * ci, 9 * co)
        part, w2 = lax.optimization_barrier((part, w2))
        late, part = forward(
            outer_kernel, 1, *shared, second, w1, bias_row, cot, part, scalar=~above_first
        )
        early, part = forward(
            outer_kernel, 1, *shared, first, w1, bias_row, cot, part, scalar=above_first
        )
        total = part if total is None else total + part
        top = jnp.where(above_first, late[0], early[0])
        bottom = jnp.where(above_first, early[0], late[0])

        def layer(at):
            return jnp.concatenate([top[at][None], inner[:, at], bottom[at][None]], axis=0)

        below, above = exchange(layer(0), layer(-1), "depth")
        around = exchange(*columns(top, bottom, below, above), "height")
        fields.append((inner, top, bottom, below, above, *around))
    def input_gradients(fields):
        grads = []
        for field in fields:
            (grad,) = call(
                input_kernel,
                (jax.ShapeDtypeStruct((depth, height, ci, width), BF16),),
                [pltpu.VMEM(((depth + 2) * 3 * co, height * width), BF16)],
                flops * height,
                *field,
                w2,
            )
            grads.append(grad.transpose(2, 0, 1, 3))
        return jnp.stack(grads)

    low, high, grads = summed(total, fields, input_gradients)
    voxels = cubes * depth * height * width
    for axis in AXES:
        voxels *= lax.axis_size(axis)
    scale = float(voxels) ** -0.5
    grad_taps, grad_bias = call(
        lambda *refs: unpack_kernel(scale, *refs),
        (jax.ShapeDtypeStruct((27 * ci, co), F32), jax.ShapeDtypeStruct((1, co), F32)),
        [pltpu.VMEM((payload_rows, 2 * co), F32)],
        payload_rows * 2 * co,
        low,
        high,
    )
    grad_weight = grad_taps.reshape(3, 3, 3, ci, co).transpose(4, 3, 0, 1, 2)
    return grads, grad_weight, grad_bias.reshape(co)


def solution(mesh):
    voxels = P("dp", None, "depth", "height", None)
    return jax.shard_map(
        local,
        mesh=mesh,
        in_specs=(voxels, P(), P(), voxels),
        out_specs=(voxels, P(), P()),
        check_vma=False,
    )
```

```python
import jax
import jax.numpy as jnp
from jax import lax
from jax.experimental import pallas as pl
from jax.experimental.pallas import tpu as pltpu
from jax.sharding import PartitionSpec as P

F32 = jnp.float32
BF16 = jnp.bfloat16
AXES = ("depth", "height", "dp")
WAYS = {"depth": (3, 2, 1), "height": (3, 2, 1), "dp": (2, 1, 3)}


def paired(axis):
    return lax.axis_index(axis) % 2 == 0 if lax.axis_size(axis) % 2 == 0 else jnp.bool_(True)


def meet(low_edge, high_edge, axis):
    count = lax.axis_size(axis)
    none = jnp.zeros_like(low_edge)
    if count == 1:
        return none, none
    if count % 2:
        up = [(i, i + 1) for i in range(count - 1)]
        down = [(i + 1, i) for i in range(count - 1)]
        return lax.ppermute(high_edge, axis, up), lax.ppermute(low_edge, axis, down)
    at, even = lax.axis_index(axis), paired(axis)
    inner = [(i, i ^ 1) for i in range(count)]
    first = lax.ppermute(jnp.where(even, high_edge, low_edge), axis, inner)
    if count == 2:
        return none, first
    outer = [(i, (i - 1 if i % 2 == 0 else i + 1) % count) for i in range(count)]
    second = lax.ppermute(jnp.where(even, low_edge, high_edge), axis, outer)
    return jnp.where((at == 0) | (at == count - 1), none, second), first


def exchange(low_edge, high_edge, axis):
    second, first = meet(low_edge, high_edge, axis)
    even = paired(axis)
    return jnp.where(even, second, first), jnp.where(even, first, second)


def columns(first_row, last_row, below, above):
    def column(rows, at):
        return jnp.concatenate([below[at][None], rows, above[at][None]], axis=0)

    return column(first_row, 0), column(last_row, -1)


def swap(array, axis, mask):
    return lax.ppermute(array, axis, [(i, i ^ mask) for i in range(lax.axis_size(axis))])


def fill_patches(row_of, depth, rows, patches):
    chans, width = row_of(1, 1).shape
    for d in range(depth + 2):
        for at, h in enumerate(rows):
            for b in range(3):
                patches[pl.ds((d * 3 + b) * chans, chans), pl.ds(at * width, width)] = row_of(d, h + b)


def shifted(value, step):
    if step == 0:
        return value
    width = value.shape[1]
    lane = lax.broadcasted_iota(jnp.int32, value.shape, 1)
    edge = width - 1 if step == 1 else 0
    return jnp.where(lane == edge, 0.0, pltpu.roll(value, (-step) % width, 1))


def forward_rows(count, width, cot_of, w1, bias, delta, before, payload, patches, taps, slopes, grad):
    co = bias.shape[1]
    depth = patches.shape[1] // (count * width)
    taps[...] = jnp.dot(w1[...], patches[...], preferred_element_type=F32)
    shift_bias = jnp.broadcast_to(bias[...], (width, co)).T
    bias_acc = jnp.zeros((co, width), F32)
    for d in range(depth):
        for at in range(count):
            lanes = pl.ds((d * count + at) * width, width)
            linear = taps[co : 2 * co, lanes] + shift_bias
            linear = linear + shifted(taps[:co, lanes], -1) + shifted(taps[2 * co :, lanes], 1)
            sigma = 1.0 / (1.0 + jnp.exp(-linear))
            slope = cot_of(d, at).astype(F32) * sigma * (1.0 + linear * (1.0 - sigma))
            rounded = slope.astype(BF16)
            delta[at, d] = rounded
            wide = rounded.astype(F32)
            bias_acc = bias_acc + wide
            slopes[:co, lanes] = shifted(wide, 1).astype(BF16)
            slopes[co : 2 * co, lanes] = rounded
            slopes[2 * co :, lanes] = shifted(wide, -1).astype(BF16)
    grad[...] = lax.dot_general(
        patches[...], slopes[...], (((1,), (1,)), ((), ())), preferred_element_type=F32
    )
    rows = grad.shape[0]
    tail = rows + rows // 2
    total = jnp.sum(bias_acc.T, axis=0, keepdims=True)
    left_over = payload.shape[0] - tail
    row_at = lax.broadcasted_iota(jnp.int32, (left_over, co), 0)
    bias_rows = jnp.where(row_at == 0, jnp.broadcast_to(total, (left_over, co)), 0.0)
    zeros = jnp.zeros((left_over, payload.shape[1] - co), F32)
    for at, value in (
        (pl.ds(0, rows), grad[:, : 2 * co]),
        (
            pl.ds(rows, rows // 2),
            jnp.concatenate([grad[: rows // 2, 2 * co :], grad[rows // 2 :, 2 * co :]], axis=1),
        ),
        (pl.ds(tail, left_over), jnp.concatenate([bias_rows, zeros], axis=1)),
    ):
        payload[at, :] = value if before is None else before[at, :] + value


def fill_taps(row_of, depth, rows, patches):
    ci, width = row_of(1, 1).shape
    count = len(rows)
    for d in range(depth):
        for at, h in enumerate(rows):
            for a in range(3):
                for b in range(3):
                    lanes = pl.ds((d * count + at) * width, width)
                    patches[pl.ds((a * 3 + b) * ci, ci), lanes] = row_of(d + a, h + b)


def inner_kernel(x, below, above, w1, bias, cot, delta, payload, patches, *scratch):
    depth, height = x.shape[:2]

    def row_of(d, h):
        return below[h - 1] if d == 0 else above[h - 1] if d == depth + 1 else x[d - 1, h - 1]

    def cot_of(d, at):
        return cot[d, at + 1]

    fill_taps(row_of, depth, range(1, height - 1), patches)
    width = x.shape[3]
    forward_rows(height - 2, width, cot_of, w1, bias, delta, None, payload, patches, *scratch)


def outer_kernel(
    x, below, above, left, right, corners_below, corners_above, w1, bias, cot, before, *refs
):
    delta, payload, patches, *scratch = refs
    depth, height = x.shape[:2]

    def row_of(d, h):
        if 0 < h <= height:
            return below[h - 1] if d == 0 else above[h - 1] if d == depth + 1 else x[d - 1, h - 1]
        side = 0 if h == 0 else 1
        if d == 0:
            return corners_below[side]
        if d == depth + 1:
            return corners_above[side]
        return right[d - 1] if side else left[d - 1]

    def cot_of(d, at):
        return cot[d, at * (height - 1)]

    fill_taps(row_of, depth, (0, height - 1), patches)
    forward_rows(2, x.shape[3], cot_of, w1, bias, delta, before, payload, patches, *scratch)


def input_kernel(inner, top, bottom, below, above, left, right, w2, out, patches):
    depth, co, width = top.shape
    height, ci = out.shape[1:3]

    def row_of(d, h):
        if h == 0:
            return left[d]
        if h == height + 1:
            return right[d]
        if d == 0:
            return below[h - 1]
        if d == depth + 1:
            return above[h - 1]
        return top[d - 1] if h == 1 else bottom[d - 1] if h == height else inner[h - 2, d - 1]

    fill_patches(row_of, depth, range(height), patches)
    for d in range(depth):
        taps = jnp.dot(w2[...], patches[pl.ds(d * 3 * co, 9 * co), :], preferred_element_type=F32)
        for h in range(height):
            lanes = slice(h * width, (h + 1) * width)
            total = taps[ci : 2 * ci, lanes]
            total = total + shifted(taps[:ci, lanes], 1) + shifted(taps[2 * ci :, lanes], -1)
            out[d, h] = total.astype(BF16)


def unpack_kernel(scale, low, high, weight_out, bias_out, full):
    half = low.shape[0]
    co = bias_out.shape[1]
    full[:half, :] = low[...] * scale
    full[half:, :] = high[...] * scale
    rows = weight_out.shape[0] // 3
    ci = rows // 9
    step = ci // 2
    for j in range(9):
        for part in range(2):
            source = j * ci + part * step
            to = 3 * j * ci + part * step
            weight_out[pl.ds(to, step), :] = full[pl.ds(source, step), :co]
            weight_out[pl.ds(to + ci, step), :] = full[pl.ds(source, step), co:]
            at = rows + source % (rows // 2)
            lanes = slice(0, co) if source < rows // 2 else slice(co, 2 * co)
            weight_out[pl.ds(to + 2 * ci, step), :] = full[pl.ds(at, step), lanes]
    bias_out[...] = full[rows + rows // 2 : rows + rows // 2 + 1, :co]


def load_kernel(*refs):
    count = len(refs) // 2
    done = refs[-1]
    copies = [pltpu.make_async_copy(refs[i], refs[count + i], done.at[i]) for i in range(count)]
    for copy in copies:
        copy.start()
    for copy in copies:
        copy.wait()


def loaded(*arrays):
    return pl.pallas_call(
        load_kernel,
        out_shape=[jax.ShapeDtypeStruct(a.shape, a.dtype) for a in arrays],
        in_specs=[pl.BlockSpec(memory_space=pltpu.HBM) for a in arrays],
        out_specs=[pl.BlockSpec(memory_space=pltpu.VMEM) for a in arrays],
        scratch_shapes=[pltpu.SemaphoreType.DMA((len(arrays),))],
        compiler_params=pltpu.CompilerParams(vmem_limit_bytes=16 << 20),
    )(*(pltpu.with_memory_space_constraint(a, pltpu.HBM) for a in arrays))


def call(kernel, outs, scratch, flops, *args):
    size = sum(a.size * a.dtype.itemsize for a in args) + sum(o.size * o.dtype.itemsize for o in outs)
    return pl.pallas_call(
        kernel,
        out_shape=outs,
        scratch_shapes=scratch,
        compiler_params=pltpu.CompilerParams(vmem_limit_bytes=40 << 20),
        cost_estimate=pl.CostEstimate(flops=flops, bytes_accessed=size, transcendentals=0),
    )(*args)


def gathered_sum(part, axis, masks):
    own = lax.reduce_precision(part, 8, 7)
    sent = own.astype(BF16)
    terms = [own] + [swap(sent, axis, mask).astype(F32) for mask in masks]
    while len(terms) > 1:
        terms = [terms[i] + terms[i + 1] for i in range(0, len(terms), 2)]
    return terms[0]


def summed(total, meanwhile, work):
    half = total.shape[0] // 2
    low, high = total[:half], total[half:]
    first = lax.axis_index("depth") % 2 == 0
    got = swap(jnp.where(first, high, low), "depth", 1)
    part = jnp.where(first, low, high) + got
    for axis in AXES:
        count = lax.axis_size(axis)
        assert count & (count - 1) == 0
        bit = 2 if axis == "depth" else 1
        while bit < count:
            masks = [bit * way for way in WAYS[axis]] if 2 * bit < count else [bit]
            part = gathered_sum(part, axis, masks)
            bit *= len(masks) + 1
    part, done = lax.optimization_barrier((part, work(meanwhile)))
    other = swap(part, "depth", 1)
    return jnp.where(first, part, other), jnp.where(first, other, part), done


def local(inputs, weight, bias, cotangent):
    cubes, ci, depth, height, width = inputs.shape
    co = cotangent.shape[1]
    payload_rows = 9 * ci + 9 * ci // 2 + 16
    payload_shape = jax.ShapeDtypeStruct((payload_rows, 2 * co), F32)
    flops = 2 * depth * width * 27 * ci * co
    total = None
    fields = []
    fields_in = [inputs[cube].transpose(1, 2, 0, 3) for cube in range(cubes)]
    rows = [(x[:, 0], x[:, -1]) for x in fields_in]
    rows, fields_in, weight, bias, cotangent = lax.optimization_barrier(
        (rows, fields_in, weight, bias, cotangent)
    )
    taps, bias_row, cotangent = loaded(weight.transpose(2, 3, 4, 1, 0), bias[None], cotangent)
    w1 = taps.transpose(2, 4, 0, 1, 3).reshape(3 * co, 9 * ci)
    for cube in range(cubes):
        x = fields_in[cube]
        left, right = exchange(*rows[cube], "height")
        below, above = exchange(x[0], x[-1], "depth")
        cot = cotangent[cube].transpose(1, 2, 0, 3)

        def forward(kernel, rows, *args):
            return call(
                kernel,
                (jax.ShapeDtypeStruct((rows, depth, co, width), BF16), payload_shape),
                [
                    pltpu.VMEM((9 * ci, depth * rows * width), BF16),
                    pltpu.VMEM((3 * co, depth * rows * width), F32),
                    pltpu.VMEM((3 * co, depth * rows * width), BF16),
                    pltpu.VMEM((9 * ci, 3 * co), F32),
                ],
                2 * flops * rows,
                *args,
            )

        shared = (x, below, above)
        inner, part = forward(inner_kernel, height - 2, *shared, w1, bias_row, cot)
        part, taps = lax.optimization_barrier((part, taps))
        w2 = jnp.flip(taps, (0, 1)).transpose(2, 3, 0, 1, 4).reshape(3 * ci, 9 * co)
        part, w2 = lax.optimization_barrier((part, w2))
        corners = exchange(jnp.stack([left[0], right[0]]), jnp.stack([left[-1], right[-1]]), "depth")
        outer, part = forward(
            outer_kernel, 2, *shared, left, right, *corners, w1, bias_row, cot, part
        )
        total = part if total is None else total + part
        top, bottom = outer[0], outer[1]

        def layer(at):
            return jnp.concatenate([top[at][None], inner[:, at], bottom[at][None]], axis=0)

        below, above = exchange(layer(0), layer(-1), "depth")
        around = exchange(*columns(top, bottom, below, above), "height")
        fields.append((inner, top, bottom, below, above, *around))
    def input_gradients(fields):
        grads = []
        for field in fields:
            (grad,) = call(
                input_kernel,
                (jax.ShapeDtypeStruct((depth, height, ci, width), BF16),),
                [pltpu.VMEM(((depth + 2) * 3 * co, height * width), BF16)],
                flops * height,
                *field,
                w2,
            )
            grads.append(grad.transpose(2, 0, 1, 3))
        return jnp.stack(grads)

    low, high, grads = summed(total, fields, input_gradients)
    voxels = cubes * depth * height * width
    for axis in AXES:
        voxels *= lax.axis_size(axis)
    scale = float(voxels) ** -0.5
    grad_taps, grad_bias = call(
        lambda *refs: unpack_kernel(scale, *refs),
        (jax.ShapeDtypeStruct((27 * ci, co), F32), jax.ShapeDtypeStruct((1, co), F32)),
        [pltpu.VMEM((payload_rows, 2 * co), F32)],
        payload_rows * 2 * co,
        low,
        high,
    )
    grad_weight = grad_taps.reshape(3, 3, 3, ci, co).transpose(4, 3, 0, 1, 2)
    return grads, grad_weight, grad_bias.reshape(co)


def solution(mesh):
    voxels = P("dp", None, "depth", "height", None)
    return jax.shard_map(
        local,
        mesh=mesh,
        in_specs=(voxels, P(), P(), voxels),
        out_specs=(voxels, P(), P()),
        check_vma=False,
    )
```

```python
import functools

import jax
import jax.numpy as jnp
from jax import lax
from jax.experimental import pallas as pl
from jax.experimental.pallas import tpu as pltpu
from jax.sharding import PartitionSpec as P

F32 = jnp.float32
BF16 = jnp.bfloat16
AXES = ("depth", "height", "dp")
WAYS = {"depth": (1, 2, 3), "height": (1, 2, 3), "dp": (1, 2, 3)}


def paired(axis):
    return lax.axis_index(axis) % 2 == 0 if lax.axis_size(axis) % 2 == 0 else jnp.bool_(True)


def meet(low_edge, high_edge, axis):
    count = lax.axis_size(axis)
    none = jnp.zeros_like(low_edge)
    if count == 1:
        return none, none
    if count % 2:
        up = [(i, i + 1) for i in range(count - 1)]
        down = [(i + 1, i) for i in range(count - 1)]
        return lax.ppermute(high_edge, axis, up), lax.ppermute(low_edge, axis, down)
    at, even = lax.axis_index(axis), paired(axis)
    inner = [(i, i ^ 1) for i in range(count)]
    first = lax.ppermute(jnp.where(even, high_edge, low_edge), axis, inner)
    if count == 2:
        return none, first
    outer = [(i, (i - 1 if i % 2 == 0 else i + 1) % count) for i in range(count)]
    second = lax.ppermute(jnp.where(even, low_edge, high_edge), axis, outer)
    return jnp.where((at == 0) | (at == count - 1), none, second), first


def exchange(low_edge, high_edge, axis):
    second, first = meet(low_edge, high_edge, axis)
    even = paired(axis)
    return jnp.where(even, second, first), jnp.where(even, first, second)


def columns(first_row, last_row, below, above):
    def column(rows, at):
        return jnp.concatenate([below[at][None], rows, above[at][None]], axis=0)

    return column(first_row, 0), column(last_row, -1)


def swap(array, axis, mask):
    return lax.ppermute(array, axis, [(i, i ^ mask) for i in range(lax.axis_size(axis))])


def fill_patches(row_of, depth, rows, patches):
    chans, width = row_of(1, 1).shape
    for d in range(depth + 2):
        for at, h in enumerate(rows):
            for b in range(3):
                patches[pl.ds((d * 3 + b) * chans, chans), pl.ds(at * width, width)] = row_of(d, h + b)


def shifted(value, step):
    if step == 0:
        return value
    width = value.shape[1]
    lane = lax.broadcasted_iota(jnp.int32, value.shape, 1)
    edge = width - 1 if step == 1 else 0
    return jnp.where(lane == edge, 0.0, pltpu.roll(value, (-step) % width, 1))


def forward_rows(positions, row_of, w1, bias, cot, delta, before, payload, patches, taps, slopes, grad):
    co, width = bias.shape[1], cot.shape[3]
    ci = patches.shape[0] // 9
    for at, (d, h) in enumerate(positions):
        for a in range(3):
            for b in range(3):
                patches[pl.ds((a * 3 + b) * ci, ci), pl.ds(at * width, width)] = row_of(d + a, h + b)
    taps[...] = jnp.dot(w1[...], patches[...], preferred_element_type=F32)
    shift_bias = jnp.broadcast_to(bias[...], (width, co)).T
    bias_acc = jnp.zeros((co, width), F32)
    for at, (d, h) in enumerate(positions):
        lanes = pl.ds(at * width, width)
        linear = taps[co : 2 * co, lanes] + shift_bias
        linear = linear + shifted(taps[:co, lanes], -1) + shifted(taps[2 * co :, lanes], 1)
        sigma = 1.0 / (1.0 + jnp.exp(-linear))
        slope = cot[d, h].astype(F32) * sigma * (1.0 + linear * (1.0 - sigma))
        rounded = slope.astype(BF16)
        delta[at] = rounded
        wide = rounded.astype(F32)
        bias_acc = bias_acc + wide
        slopes[:co, lanes] = shifted(wide, 1).astype(BF16)
        slopes[co : 2 * co, lanes] = rounded
        slopes[2 * co :, lanes] = shifted(wide, -1).astype(BF16)
    grad[...] = lax.dot_general(
        patches[...], slopes[...], (((1,), (1,)), ((), ())), preferred_element_type=F32
    )
    rows = grad.shape[0]
    tail = rows + rows // 2
    total = jnp.sum(bias_acc.T, axis=0, keepdims=True)
    left_over = payload.shape[0] - tail
    row_at = lax.broadcasted_iota(jnp.int32, (left_over, co), 0)
    bias_rows = jnp.where(row_at == 0, jnp.broadcast_to(total, (left_over, co)), 0.0)
    zeros = jnp.zeros((left_over, payload.shape[1] - co), F32)
    for at, value in (
        (pl.ds(0, rows), grad[:, : 2 * co]),
        (
            pl.ds(rows, rows // 2),
            jnp.concatenate([grad[: rows // 2, 2 * co :], grad[rows // 2 :, 2 * co :]], axis=1),
        ),
        (pl.ds(tail, left_over), jnp.concatenate([bias_rows, zeros], axis=1)),
    ):
        payload[at, :] = value if before is None else before[at, :] + value


def parts_of(depth, height):
    layers, rows = range(1, depth - 1), range(1, height - 1)
    return (
        [(d, h) for d in layers for h in rows],
        [(d, h) for h in (0, height - 1) for d in layers],
        [(d, h) for d in (0, depth - 1) for h in range(height)],
    )


def forward_kernel(positions, halos, x, *refs):
    left, right, low, high = (*refs[:halos], None, None, None, None)[:4]
    w1, bias, cot, *refs = refs[halos:]
    before, *refs = refs if halos else (None, *refs)
    depth, height = x.shape[:2]

    def row_of(d, h):
        if d == 0:
            return low[h]
        if d == depth + 1:
            return high[h]
        return left[d - 1] if h == 0 else right[d - 1] if h == height + 1 else x[d - 1, h - 1]

    delta, *refs = refs
    forward_rows(positions, row_of, w1, bias, cot, delta, before, *refs)


def input_kernel(inner, sides, ends, below, above, left, right, w2, out, patches):
    depth, height, ci, width = out.shape
    co = inner.shape[1]
    place = {}
    for ref, positions in zip((inner, sides, ends), parts_of(depth, height)):
        place.update({position: (ref, at) for at, position in enumerate(positions)})

    def row_of(d, h):
        if h == 0:
            return left[d]
        if h == height + 1:
            return right[d]
        if d == 0:
            return below[h - 1]
        if d == depth + 1:
            return above[h - 1]
        ref, at = place[d - 1, h - 1]
        return ref[at]

    fill_patches(row_of, depth, range(height), patches)
    for d in range(depth):
        taps = jnp.dot(w2[...], patches[pl.ds(d * 3 * co, 9 * co), :], preferred_element_type=F32)
        for h in range(height):
            lanes = slice(h * width, (h + 1) * width)
            total = taps[ci : 2 * ci, lanes]
            total = total + shifted(taps[:ci, lanes], 1) + shifted(taps[2 * ci :, lanes], -1)
            out[d, h] = total.astype(BF16)


def unpack_kernel(scale, low, high, weight_out, bias_out, full):
    half = low.shape[0]
    co = bias_out.shape[1]
    full[:half, :] = low[...] * scale
    full[half:, :] = high[...] * scale
    rows = weight_out.shape[0] // 3
    ci = rows // 9
    step = ci // 2
    for j in range(9):
        for part in range(2):
            source = j * ci + part * step
            to = 3 * j * ci + part * step
            weight_out[pl.ds(to, step), :] = full[pl.ds(source, step), :co]
            weight_out[pl.ds(to + ci, step), :] = full[pl.ds(source, step), co:]
            at = rows + source % (rows // 2)
            lanes = slice(0, co) if source < rows // 2 else slice(co, 2 * co)
            weight_out[pl.ds(to + 2 * ci, step), :] = full[pl.ds(at, step), lanes]
    bias_out[...] = full[rows + rows // 2 : rows + rows // 2 + 1, :co]


def load_kernel(*refs):
    count = len(refs) // 2
    done = refs[-1]
    copies = [pltpu.make_async_copy(refs[i], refs[count + i], done.at[i]) for i in range(count)]
    for copy in copies:
        copy.start()
    for copy in copies:
        copy.wait()


def loaded(*arrays):
    return pl.pallas_call(
        load_kernel,
        out_shape=[jax.ShapeDtypeStruct(a.shape, a.dtype) for a in arrays],
        in_specs=[pl.BlockSpec(memory_space=pltpu.HBM) for a in arrays],
        out_specs=[pl.BlockSpec(memory_space=pltpu.VMEM) for a in arrays],
        scratch_shapes=[pltpu.SemaphoreType.DMA((len(arrays),))],
        compiler_params=pltpu.CompilerParams(vmem_limit_bytes=16 << 20),
    )(*(pltpu.with_memory_space_constraint(a, pltpu.HBM) for a in arrays))


def call(kernel, outs, scratch, flops, *args):
    size = sum(a.size * a.dtype.itemsize for a in args) + sum(o.size * o.dtype.itemsize for o in outs)
    return pl.pallas_call(
        kernel,
        out_shape=outs,
        scratch_shapes=scratch,
        compiler_params=pltpu.CompilerParams(vmem_limit_bytes=40 << 20),
        cost_estimate=pl.CostEstimate(flops=flops, bytes_accessed=size, transcendentals=0),
    )(*args)


def gathered_sum(part, axis, masks):
    own = lax.reduce_precision(part, 8, 7)
    sent = own.astype(BF16)
    terms = [own] + [swap(sent, axis, mask).astype(F32) for mask in masks]
    while len(terms) > 1:
        terms = [terms[i] + terms[i + 1] for i in range(0, len(terms), 2)]
    return terms[0]


def summed(total, meanwhile, work):
    half = total.shape[0] // 2
    low, high = total[:half], total[half:]
    first = lax.axis_index("depth") % 2 == 0
    got = swap(jnp.where(first, high, low), "depth", 1)
    part = jnp.where(first, low, high) + got
    for axis in AXES:
        count = lax.axis_size(axis)
        assert count & (count - 1) == 0
        bit = 2 if axis == "depth" else 1
        while bit < count:
            masks = [bit * way for way in WAYS[axis]] if 2 * bit < count else [bit]
            part = gathered_sum(part, axis, masks)
            bit *= len(masks) + 1
    part, done = lax.optimization_barrier((part, work(meanwhile)))
    other = swap(part, "depth", 1)
    return jnp.where(first, part, other), jnp.where(first, other, part), done


def local(inputs, weight, bias, cotangent):
    cubes, ci, depth, height, width = inputs.shape
    co = cotangent.shape[1]
    payload_rows = 9 * ci + 9 * ci // 2 + 16
    payload_shape = jax.ShapeDtypeStruct((payload_rows, 2 * co), F32)
    flops = 4 * width * 27 * ci * co
    total = None
    fields = []
    fields_in = [inputs[cube].transpose(1, 2, 0, 3) for cube in range(cubes)]
    rows = [(x[:, 0], x[:, -1]) for x in fields_in]
    rows, fields_in, weight, bias, cotangent = lax.optimization_barrier(
        (rows, fields_in, weight, bias, cotangent)
    )
    taps, bias_row, cotangent = loaded(weight.transpose(2, 3, 4, 1, 0), bias[None], cotangent)
    w1 = taps.transpose(2, 4, 0, 1, 3).reshape(3 * co, 9 * ci)
    for cube in range(cubes):
        x = fields_in[cube]
        cot = cotangent[cube].transpose(1, 2, 0, 3)
        parts = parts_of(depth, height)

        def forward(which, halos, so_far):
            count = len(parts[which])
            return call(
                functools.partial(forward_kernel, parts[which], len(halos)),
                (jax.ShapeDtypeStruct((count, co, width), BF16), payload_shape),
                [
                    pltpu.VMEM((9 * ci, count * width), BF16),
                    pltpu.VMEM((3 * co, count * width), F32),
                    pltpu.VMEM((3 * co, count * width), BF16),
                    pltpu.VMEM((9 * ci, 3 * co), F32),
                ],
                flops * count,
                x,
                *halos,
                w1,
                bias_row,
                cot,
                *so_far,
            )

        inner, part = forward(0, (), ())
        left, right = exchange(*rows[cube], "height")
        part, left, right = lax.optimization_barrier((part, left, right))

        def layer(at):
            return jnp.concatenate([left[at][None], x[at], right[at][None]], axis=0)

        low, high = exchange(layer(0), layer(-1), "depth")
        sides, part = forward(1, (left, right), (part,))
        ends, part = forward(2, (left, right, low, high), (part,))
        total = part if total is None else total + part
        below, above = exchange(ends[:height], ends[height:], "depth")
        below, above, taps = lax.optimization_barrier((below, above, taps))
        first_row = jnp.concatenate([ends[:1], sides[: depth - 2], ends[height : height + 1]], axis=0)
        last_row = jnp.concatenate([ends[height - 1 : height], sides[depth - 2 :], ends[-1:]], axis=0)
        around = exchange(*columns(first_row, last_row, below, above), "height")
        fields.append((inner, sides, ends, below, above, *around))
    w2 = jnp.flip(taps, (0, 1)).transpose(2, 3, 0, 1, 4).reshape(3 * ci, 9 * co)

    def input_gradients(fields):
        grads = []
        for field in fields:
            (grad,) = call(
                input_kernel,
                (jax.ShapeDtypeStruct((depth, height, ci, width), BF16),),
                [pltpu.VMEM(((depth + 2) * 3 * co, height * width), BF16)],
                flops // 2 * depth * height,
                *field,
                w2,
            )
            grads.append(grad.transpose(2, 0, 1, 3))
        return jnp.stack(grads)

    low, high, grads = summed(total, fields, input_gradients)
    voxels = cubes * depth * height * width
    for axis in AXES:
        voxels *= lax.axis_size(axis)
    scale = float(voxels) ** -0.5
    grad_taps, grad_bias = call(
        lambda *refs: unpack_kernel(scale, *refs),
        (jax.ShapeDtypeStruct((27 * ci, co), F32), jax.ShapeDtypeStruct((1, co), F32)),
        [pltpu.VMEM((payload_rows, 2 * co), F32)],
        payload_rows * 2 * co,
        low,
        high,
    )
    grad_weight = grad_taps.reshape(3, 3, 3, ci, co).transpose(4, 3, 0, 1, 2)
    return grads, grad_weight, grad_bias.reshape(co)


def solution(mesh):
    voxels = P("dp", None, "depth", "height", None)
    return jax.shard_map(
        local,
        mesh=mesh,
        in_specs=(voxels, P(), P(), voxels),
        out_specs=(voxels, P(), P()),
        check_vma=False,
    )
```

```python
import functools

import jax
import jax.numpy as jnp
from jax import lax
from jax.experimental import pallas as pl
from jax.experimental.pallas import tpu as pltpu
from jax.sharding import PartitionSpec as P

F32 = jnp.float32
BF16 = jnp.bfloat16
AXES = ("depth", "height", "dp")
WAYS = {"depth": (1, 2, 3), "height": (1, 2, 3), "dp": (1, 2, 3)}


def paired(axis):
    return lax.axis_index(axis) % 2 == 0 if lax.axis_size(axis) % 2 == 0 else jnp.bool_(True)


def meet(low_edge, high_edge, axis, first=None):
    count = lax.axis_size(axis)
    none = jnp.zeros_like(low_edge)
    if count == 1:
        return none, none
    if count % 2:
        up = [(i, i + 1) for i in range(count - 1)]
        down = [(i + 1, i) for i in range(count - 1)]
        return lax.ppermute(high_edge, axis, up), lax.ppermute(low_edge, axis, down)
    at, even = lax.axis_index(axis), paired(axis)
    inner = [(i, i ^ 1) for i in range(count)]
    if first is None:
        first = lax.ppermute(jnp.where(even, high_edge, low_edge), axis, inner)
    if count == 2:
        return none, first
    outer = [(i, (i - 1 if i % 2 == 0 else i + 1) % count) for i in range(count)]
    second = lax.ppermute(jnp.where(even, low_edge, high_edge), axis, outer)
    return jnp.where((at == 0) | (at == count - 1), none, second), first


def exchange(low_edge, high_edge, axis, first=None):
    second, first = meet(low_edge, high_edge, axis, first)
    even = paired(axis)
    return jnp.where(even, second, first), jnp.where(even, first, second)


def columns(first_row, last_row, below, above):
    def column(rows, at):
        return jnp.concatenate([below[at][None], rows, above[at][None]], axis=0)

    return column(first_row, 0), column(last_row, -1)


def swap(array, axis, mask):
    return lax.ppermute(array, axis, [(i, i ^ mask) for i in range(lax.axis_size(axis))])


def fill_patches(row_of, depth, rows, patches):
    chans, width = row_of(1, 1).shape
    for d in range(depth + 2):
        for at, h in enumerate(rows):
            for b in range(3):
                patches[pl.ds((d * 3 + b) * chans, chans), pl.ds(at * width, width)] = row_of(d, h + b)


def shifted(value, step):
    if step == 0:
        return value
    width = value.shape[1]
    lane = lax.broadcasted_iota(jnp.int32, value.shape, 1)
    edge = width - 1 if step == 1 else 0
    return jnp.where(lane == edge, 0.0, pltpu.roll(value, (-step) % width, 1))


def forward_rows(positions, row_of, w1, bias, cot, delta, before, payload, patches, taps, slopes, grad):
    co, width = bias.shape[1], cot.shape[3]
    ci = patches.shape[0] // 9
    for at, (d, h) in enumerate(positions):
        for a in range(3):
            for b in range(3):
                patches[pl.ds((a * 3 + b) * ci, ci), pl.ds(at * width, width)] = row_of(d + a, h + b)
    taps[...] = jnp.dot(w1[...], patches[...], preferred_element_type=F32)
    shift_bias = jnp.broadcast_to(bias[...], (width, co)).T
    bias_acc = jnp.zeros((co, width), F32)
    for at, (d, h) in enumerate(positions):
        lanes = pl.ds(at * width, width)
        linear = taps[co : 2 * co, lanes] + shift_bias
        linear = linear + shifted(taps[:co, lanes], -1) + shifted(taps[2 * co :, lanes], 1)
        sigma = 1.0 / (1.0 + jnp.exp(-linear))
        slope = cot[d, h].astype(F32) * sigma * (1.0 + linear * (1.0 - sigma))
        rounded = slope.astype(BF16)
        delta[at] = rounded
        wide = rounded.astype(F32)
        bias_acc = bias_acc + wide
        slopes[:co, lanes] = shifted(wide, 1).astype(BF16)
        slopes[co : 2 * co, lanes] = rounded
        slopes[2 * co :, lanes] = shifted(wide, -1).astype(BF16)
    grad[...] = lax.dot_general(
        patches[...], slopes[...], (((1,), (1,)), ((), ())), preferred_element_type=F32
    )
    rows = grad.shape[0]
    tail = rows + rows // 2
    total = jnp.sum(bias_acc.T, axis=0, keepdims=True)
    left_over = payload.shape[0] - tail
    row_at = lax.broadcasted_iota(jnp.int32, (left_over, co), 0)
    bias_rows = jnp.where(row_at == 0, jnp.broadcast_to(total, (left_over, co)), 0.0)
    zeros = jnp.zeros((left_over, payload.shape[1] - co), F32)
    for at, value in (
        (pl.ds(0, rows), grad[:, : 2 * co]),
        (
            pl.ds(rows, rows // 2),
            jnp.concatenate([grad[: rows // 2, 2 * co :], grad[rows // 2 :, 2 * co :]], axis=1),
        ),
        (pl.ds(tail, left_over), jnp.concatenate([bias_rows, zeros], axis=1)),
    ):
        payload[at, :] = value if before is None else before[at, :] + value


def parts_of(depth, height):
    layers, rows = range(1, depth - 1), range(1, height - 1)
    return (
        [(d, h) for d in layers for h in rows],
        [(d, h) for h in (0, height - 1) for d in layers],
        [(d, h) for d in (0, depth - 1) for h in range(height)],
    )


def forward_kernel(positions, halos, x, *refs):
    left, right, low, high = (*refs[:halos], None, None, None, None)[:4]
    w1, bias, cot, *refs = refs[halos:]
    before, *refs = refs if halos else (None, *refs)
    depth, height = x.shape[:2]

    def row_of(d, h):
        if d == 0:
            return low[h]
        if d == depth + 1:
            return high[h]
        return left[d - 1] if h == 0 else right[d - 1] if h == height + 1 else x[d - 1, h - 1]

    delta, *refs = refs
    forward_rows(positions, row_of, w1, bias, cot, delta, before, *refs)


def input_kernel(inner, sides, ends, below, above, left, right, w2, out, patches):
    depth, height, ci, width = out.shape
    co = inner.shape[1]
    place = {}
    for ref, positions in zip((inner, sides, ends), parts_of(depth, height)):
        place.update({position: (ref, at) for at, position in enumerate(positions)})

    def row_of(d, h):
        if h == 0:
            return left[d]
        if h == height + 1:
            return right[d]
        if d == 0:
            return below[h - 1]
        if d == depth + 1:
            return above[h - 1]
        ref, at = place[d - 1, h - 1]
        return ref[at]

    fill_patches(row_of, depth, range(height), patches)
    for d in range(depth):
        taps = jnp.dot(w2[...], patches[pl.ds(d * 3 * co, 9 * co), :], preferred_element_type=F32)
        for h in range(height):
            lanes = slice(h * width, (h + 1) * width)
            total = taps[ci : 2 * ci, lanes]
            total = total + shifted(taps[:ci, lanes], 1) + shifted(taps[2 * ci :, lanes], -1)
            out[d, h] = total.astype(BF16)


def unpack_kernel(scale, low, high, weight_out, bias_out, full):
    half = low.shape[0]
    co = bias_out.shape[1]
    full[:half, :] = low[...] * scale
    full[half:, :] = high[...] * scale
    rows = weight_out.shape[0] // 3
    ci = rows // 9
    step = ci // 2
    for j in range(9):
        for part in range(2):
            source = j * ci + part * step
            to = 3 * j * ci + part * step
            weight_out[pl.ds(to, step), :] = full[pl.ds(source, step), :co]
            weight_out[pl.ds(to + ci, step), :] = full[pl.ds(source, step), co:]
            at = rows + source % (rows // 2)
            lanes = slice(0, co) if source < rows // 2 else slice(co, 2 * co)
            weight_out[pl.ds(to + 2 * ci, step), :] = full[pl.ds(at, step), lanes]
    bias_out[...] = full[rows + rows // 2 : rows + rows // 2 + 1, :co]


def load_kernel(*refs):
    count = len(refs) // 2
    done = refs[-1]
    copies = [pltpu.make_async_copy(refs[i], refs[count + i], done.at[i]) for i in range(count)]
    for copy in copies:
        copy.start()
    for copy in copies:
        copy.wait()


def loaded(*arrays):
    return pl.pallas_call(
        load_kernel,
        out_shape=[jax.ShapeDtypeStruct(a.shape, a.dtype) for a in arrays],
        in_specs=[pl.BlockSpec(memory_space=pltpu.HBM) for a in arrays],
        out_specs=[pl.BlockSpec(memory_space=pltpu.VMEM) for a in arrays],
        scratch_shapes=[pltpu.SemaphoreType.DMA((len(arrays),))],
        compiler_params=pltpu.CompilerParams(vmem_limit_bytes=16 << 20),
    )(*(pltpu.with_memory_space_constraint(a, pltpu.HBM) for a in arrays))


def call(kernel, outs, scratch, flops, *args):
    size = sum(a.size * a.dtype.itemsize for a in args) + sum(o.size * o.dtype.itemsize for o in outs)
    return pl.pallas_call(
        kernel,
        out_shape=outs,
        scratch_shapes=scratch,
        compiler_params=pltpu.CompilerParams(vmem_limit_bytes=40 << 20),
        cost_estimate=pl.CostEstimate(flops=flops, bytes_accessed=size, transcendentals=0),
    )(*args)


def gathered_sum(part, axis, masks, meanwhile):
    own = lax.reduce_precision(part, 8, 7)
    sent = own.astype(BF16)
    near, meanwhile = lax.optimization_barrier((sent, meanwhile))
    terms = [own]
    for mask in masks:
        terms.append(swap(near if mask == min(masks) else sent, axis, mask).astype(F32))
    while len(terms) > 1:
        terms = [terms[i] + terms[i + 1] for i in range(0, len(terms), 2)]
    return terms[0], meanwhile


def halved(total, edges):
    half, lanes = total.shape[0] // 2, total.shape[1]
    first = lax.axis_index("depth") % 2 == 0
    low, high = total[:half], total[half:]
    flat = [edge.astype(F32).reshape(-1, lanes) for edge in edges]
    got = swap(jnp.concatenate([jnp.where(first, high, low), *flat], axis=0), "depth", 1)
    part = jnp.where(first, low, high) + got[:half]
    received, at = [], half
    for edge, rows in zip(edges, flat):
        received.append(got[at : at + rows.shape[0]].reshape(edge.shape).astype(BF16))
        at += rows.shape[0]
    return part, received


def summed(part, meanwhile, work):
    first = lax.axis_index("depth") % 2 == 0
    for axis in AXES:
        count = lax.axis_size(axis)
        assert count & (count - 1) == 0
        bit = 2 if axis == "depth" else 1
        while bit < count:
            masks = [bit * way for way in WAYS[axis]] if 2 * bit < count else [bit]
            if axis == AXES[-1]:
                part, meanwhile = gathered_sum(part, axis, masks, meanwhile)
            else:
                part, _ = gathered_sum(part, axis, masks, ())
            bit *= len(masks) + 1
    part, done = lax.optimization_barrier((part, work(meanwhile)))
    other = swap(part, "depth", 1)
    return jnp.where(first, part, other), jnp.where(first, other, part), done


def local(inputs, weight, bias, cotangent):
    cubes, ci, depth, height, width = inputs.shape
    co = cotangent.shape[1]
    payload_rows = 9 * ci + 9 * ci // 2 + 16
    payload_shape = jax.ShapeDtypeStruct((payload_rows, 2 * co), F32)
    flops = 4 * width * 27 * ci * co
    total = None
    deltas, fields = [], []
    fields_in = [inputs[cube].transpose(1, 2, 0, 3) for cube in range(cubes)]
    rows = [(x[:, 0], x[:, -1]) for x in fields_in]
    rows, fields_in, weight, bias, cotangent = lax.optimization_barrier(
        (rows, fields_in, weight, bias, cotangent)
    )
    taps, bias_row, cotangent = loaded(weight.transpose(2, 3, 4, 1, 0), bias[None], cotangent)
    w1 = taps.transpose(2, 4, 0, 1, 3).reshape(3 * co, 9 * ci)
    w2 = jnp.flip(taps, (0, 1)).transpose(2, 3, 0, 1, 4).reshape(3 * ci, 9 * co)
    w1, w2 = lax.optimization_barrier((w1, w2))
    for cube in range(cubes):
        x = fields_in[cube]
        cot = cotangent[cube].transpose(1, 2, 0, 3)
        parts = parts_of(depth, height)

        def forward(which, halos, so_far):
            count = len(parts[which])
            return call(
                functools.partial(forward_kernel, parts[which], len(halos)),
                (jax.ShapeDtypeStruct((count, co, width), BF16), payload_shape),
                [
                    pltpu.VMEM((9 * ci, count * width), BF16),
                    pltpu.VMEM((3 * co, count * width), F32),
                    pltpu.VMEM((3 * co, count * width), BF16),
                    pltpu.VMEM((9 * ci, 3 * co), F32),
                ],
                flops * count,
                x,
                *halos,
                w1,
                bias_row,
                cot,
                *so_far,
            )

        inner, part = forward(0, (), ())
        left, right = exchange(*rows[cube], "height")
        part, left, right = lax.optimization_barrier((part, left, right))

        def layer(at):
            return jnp.concatenate([left[at][None], x[at], right[at][None]], axis=0)

        low, high = exchange(layer(0), layer(-1), "depth")
        sides, part = forward(1, (left, right), (part,))
        ends, part = forward(2, (left, right, low, high), (part,))
        total = part if total is None else total + part
        deltas.append((inner, sides, ends))
    even = paired("depth")
    part, edges = halved(
        total, [jnp.where(even, ends[height:], ends[:height]) for _, _, ends in deltas]
    )
    for (inner, sides, ends), edge in zip(deltas, edges):
        below, above = exchange(ends[:height], ends[height:], "depth", edge)
        first_row = jnp.concatenate([ends[:1], sides[: depth - 2], ends[height : height + 1]], axis=0)
        last_row = jnp.concatenate([ends[height - 1 : height], sides[depth - 2 :], ends[-1:]], axis=0)
        around = exchange(*columns(first_row, last_row, below, above), "height")
        fields.append((inner, sides, ends, below, above, *around))

    def input_gradients(fields):
        grads = []
        for field in fields:
            (grad,) = call(
                input_kernel,
                (jax.ShapeDtypeStruct((depth, height, ci, width), BF16),),
                [pltpu.VMEM(((depth + 2) * 3 * co, height * width), BF16)],
                flops // 2 * depth * height,
                *field,
                w2,
            )
            grads.append(grad.transpose(2, 0, 1, 3))
        return jnp.stack(grads)

    low, high, grads = summed(part, fields, input_gradients)
    voxels = cubes * depth * height * width
    for axis in AXES:
        voxels *= lax.axis_size(axis)
    scale = float(voxels) ** -0.5
    grad_taps, grad_bias = call(
        lambda *refs: unpack_kernel(scale, *refs),
        (jax.ShapeDtypeStruct((27 * ci, co), F32), jax.ShapeDtypeStruct((1, co), F32)),
        [pltpu.VMEM((payload_rows, 2 * co), F32)],
        payload_rows * 2 * co,
        low,
        high,
    )
    grad_weight = grad_taps.reshape(3, 3, 3, ci, co).transpose(4, 3, 0, 1, 2)
    return grads, grad_weight, grad_bias.reshape(co)


def solution(mesh):
    voxels = P("dp", None, "depth", "height", None)
    return jax.shard_map(
        local,
        mesh=mesh,
        in_specs=(voxels, P(), P(), voxels),
        out_specs=(voxels, P(), P()),
        check_vma=False,
    )
```

```python
import functools

import jax
import jax.numpy as jnp
from jax import lax
from jax.experimental import pallas as pl
from jax.experimental.pallas import tpu as pltpu
from jax.sharding import PartitionSpec as P

F32 = jnp.float32
BF16 = jnp.bfloat16
GROUP = 4
AXES = ("depth", "height", "dp")
WAYS = {"depth": (1, 2, 3), "height": (1, 2, 3), "dp": (1, 2, 3)}


def paired(axis):
    return lax.axis_index(axis) % 2 == 0 if lax.axis_size(axis) % 2 == 0 else jnp.bool_(True)


def meet(low_edge, high_edge, axis):
    count = lax.axis_size(axis)
    none = jnp.zeros_like(low_edge)
    if count == 1:
        return none, none
    if count % 2:
        up = [(i, i + 1) for i in range(count - 1)]
        down = [(i + 1, i) for i in range(count - 1)]
        return lax.ppermute(high_edge, axis, up), lax.ppermute(low_edge, axis, down)
    at, even = lax.axis_index(axis), paired(axis)
    inner = [(i, i ^ 1) for i in range(count)]
    first = lax.ppermute(jnp.where(even, high_edge, low_edge), axis, inner)
    if count == 2:
        return none, first
    outer = [(i, (i - 1 if i % 2 == 0 else i + 1) % count) for i in range(count)]
    second = lax.ppermute(jnp.where(even, low_edge, high_edge), axis, outer)
    return jnp.where((at == 0) | (at == count - 1), none, second), first


def exchange(low_edge, high_edge, axis):
    second, first = meet(low_edge, high_edge, axis)
    even = paired(axis)
    return jnp.where(even, second, first), jnp.where(even, first, second)


def columns(first_row, last_row, below, above):
    def column(rows, at):
        return jnp.concatenate([below[at][None], rows, above[at][None]], axis=0)

    return column(first_row, 0), column(last_row, -1)


def swap(array, axis, mask):
    return lax.ppermute(array, axis, [(i, i ^ mask) for i in range(lax.axis_size(axis))])


def fill_patches(row_of, depth, rows, patches):
    chans, width = row_of(1, 1).shape
    for d in range(depth + 2):
        for at, h in enumerate(rows):
            for b in range(3):
                patches[pl.ds((d * 3 + b) * chans, chans), pl.ds(at * width, width)] = row_of(d, h + b)


def shifted(value, step):
    if step == 0:
        return value
    width = value.shape[1]
    lane = lax.broadcasted_iota(jnp.int32, value.shape, 1)
    edge = width - 1 if step == 1 else 0
    return jnp.where(lane == edge, 0.0, pltpu.roll(value, (-step) % width, 1))


def rowwise(value, width):
    return [value[:, at : at + width] for at in range(0, value.shape[1], width)]


def beside(rows):
    return rows[0] if len(rows) == 1 else jnp.concatenate(rows, axis=1)


def forward_rows(positions, row_of, w1, bias, cot, delta, before, payload, patches, taps, slopes, grad):
    co, width = bias.shape[1], cot.shape[3]
    ci = patches.shape[0] // 9
    for at, (d, h) in enumerate(positions):
        for a in range(3):
            for b in range(3):
                patches[pl.ds((a * 3 + b) * ci, ci), pl.ds(at * width, width)] = row_of(d + a, h + b)
    taps[...] = jnp.dot(w1[...], patches[...], preferred_element_type=F32)
    shift_bias = jnp.broadcast_to(bias[...], (width, co)).T
    bias_acc = jnp.zeros((co, width), F32)
    starts = range(0, len(positions), GROUP)
    per_group = len(starts) > 2
    product = functools.partial(
        lax.dot_general,
        dimension_numbers=(((1,), (1,)), ((), ())),
        preferred_element_type=F32,
    )
    for start in starts:
        group = positions[start : start + GROUP]
        lanes = pl.ds(start * width, len(group) * width)
        low, middle, high = (rowwise(taps[i * co : (i + 1) * co, lanes], width) for i in range(3))
        linear = beside(
            [
                m + shift_bias + shifted(l, -1) + shifted(h, 1)
                for l, m, h in zip(low, middle, high)
            ]
        )
        sigma = 1.0 / (1.0 + jnp.exp(-linear))
        incoming = beside([cot[d, h].astype(F32) for d, h in group])
        rounded = (incoming * sigma * (1.0 + linear * (1.0 - sigma))).astype(BF16)
        wide = rowwise(rounded.astype(F32), width)
        for at, row in enumerate(rowwise(rounded, width)):
            delta[start + at] = row
            bias_acc = bias_acc + wide[at]
        before_it = beside([shifted(row, 1) for row in wide]).astype(BF16)
        after_it = beside([shifted(row, -1) for row in wide]).astype(BF16)
        if per_group:
            term = product(patches[:, lanes], jnp.concatenate([before_it, rounded, after_it], axis=0))
            grad[...] = term if start == 0 else grad[...] + term
        else:
            slopes[:co, lanes] = before_it
            slopes[co : 2 * co, lanes] = rounded
            slopes[2 * co :, lanes] = after_it
    if not per_group:
        grad[...] = product(patches[...], slopes[...])
    rows = grad.shape[0]
    tail = rows + rows // 2
    total = jnp.sum(bias_acc.T, axis=0, keepdims=True)
    left_over = payload.shape[0] - tail
    row_at = lax.broadcasted_iota(jnp.int32, (left_over, co), 0)
    bias_rows = jnp.where(row_at == 0, jnp.broadcast_to(total, (left_over, co)), 0.0)
    zeros = jnp.zeros((left_over, payload.shape[1] - co), F32)
    for at, value in (
        (pl.ds(0, rows), grad[:, : 2 * co]),
        (
            pl.ds(rows, rows // 2),
            jnp.concatenate([grad[: rows // 2, 2 * co :], grad[rows // 2 :, 2 * co :]], axis=1),
        ),
        (pl.ds(tail, left_over), jnp.concatenate([bias_rows, zeros], axis=1)),
    ):
        payload[at, :] = value if before is None else before[at, :] + value


def parts_of(depth, height):
    layers, rows = range(1, depth - 1), range(1, height - 1)
    return (
        [(d, h) for d in layers for h in rows],
        [(d, h) for h in (0, height - 1) for d in layers],
        [(d, h) for d in (0, depth - 1) for h in range(height)],
    )


def forward_kernel(positions, halos, x, *refs):
    left, right, low, high = (*refs[:halos], None, None, None, None)[:4]
    w1, bias, cot, *refs = refs[halos:]
    before, *refs = refs if halos else (None, *refs)
    depth, height = x.shape[:2]

    def row_of(d, h):
        if d == 0:
            return low[h]
        if d == depth + 1:
            return high[h]
        return left[d - 1] if h == 0 else right[d - 1] if h == height + 1 else x[d - 1, h - 1]

    delta, *refs = refs
    forward_rows(positions, row_of, w1, bias, cot, delta, before, *refs)


def input_kernel(inner, sides, ends, below, above, left, right, w2, out, patches):
    depth, height, ci, width = out.shape
    co = inner.shape[1]
    place = {}
    for ref, positions in zip((inner, sides, ends), parts_of(depth, height)):
        place.update({position: (ref, at) for at, position in enumerate(positions)})

    def row_of(d, h):
        if h == 0:
            return left[d]
        if h == height + 1:
            return right[d]
        if d == 0:
            return below[h - 1]
        if d == depth + 1:
            return above[h - 1]
        ref, at = place[d - 1, h - 1]
        return ref[at]

    fill_patches(row_of, depth, range(height), patches)
    for d in range(depth):
        taps = jnp.dot(w2[...], patches[pl.ds(d * 3 * co, 9 * co), :], preferred_element_type=F32)
        for h in range(height):
            lanes = slice(h * width, (h + 1) * width)
            total = taps[ci : 2 * ci, lanes]
            total = total + shifted(taps[:ci, lanes], 1) + shifted(taps[2 * ci :, lanes], -1)
            out[d, h] = total.astype(BF16)


def unpack_kernel(scale, low, high, weight_out, bias_out, full):
    half = low.shape[0]
    co = bias_out.shape[1]
    full[:half, :] = low[...] * scale
    full[half:, :] = high[...] * scale
    rows = weight_out.shape[0] // 3
    ci = rows // 9
    step = ci // 2
    for j in range(9):
        for part in range(2):
            source = j * ci + part * step
            to = 3 * j * ci + part * step
            weight_out[pl.ds(to, step), :] = full[pl.ds(source, step), :co]
            weight_out[pl.ds(to + ci, step), :] = full[pl.ds(source, step), co:]
            at = rows + source % (rows // 2)
            lanes = slice(0, co) if source < rows // 2 else slice(co, 2 * co)
            weight_out[pl.ds(to + 2 * ci, step), :] = full[pl.ds(at, step), lanes]
    bias_out[...] = full[rows + rows // 2 : rows + rows // 2 + 1, :co]


def load_kernel(*refs):
    count = len(refs) // 2
    done = refs[-1]
    copies = [pltpu.make_async_copy(refs[i], refs[count + i], done.at[i]) for i in range(count)]
    for copy in copies:
        copy.start()
    for copy in copies:
        copy.wait()


def loaded(*arrays):
    return pl.pallas_call(
        load_kernel,
        out_shape=[jax.ShapeDtypeStruct(a.shape, a.dtype) for a in arrays],
        in_specs=[pl.BlockSpec(memory_space=pltpu.HBM) for a in arrays],
        out_specs=[pl.BlockSpec(memory_space=pltpu.VMEM) for a in arrays],
        scratch_shapes=[pltpu.SemaphoreType.DMA((len(arrays),))],
        compiler_params=pltpu.CompilerParams(vmem_limit_bytes=16 << 20),
    )(*(pltpu.with_memory_space_constraint(a, pltpu.HBM) for a in arrays))


def call(kernel, outs, scratch, flops, *args):
    size = sum(a.size * a.dtype.itemsize for a in args) + sum(o.size * o.dtype.itemsize for o in outs)
    return pl.pallas_call(
        kernel,
        out_shape=outs,
        scratch_shapes=scratch,
        compiler_params=pltpu.CompilerParams(vmem_limit_bytes=40 << 20),
        cost_estimate=pl.CostEstimate(flops=flops, bytes_accessed=size, transcendentals=0),
    )(*args)


def gathered_sum(part, axis, masks):
    own = lax.reduce_precision(part, 8, 7)
    sent = own.astype(BF16)
    terms = [own] + [swap(sent, axis, mask).astype(F32) for mask in masks]
    while len(terms) > 1:
        terms = [terms[i] + terms[i + 1] for i in range(0, len(terms), 2)]
    return terms[0]


def summed(total, meanwhile, work):
    half = total.shape[0] // 2
    low, high = total[:half], total[half:]
    first = lax.axis_index("depth") % 2 == 0
    got = swap(jnp.where(first, high, low), "depth", 1)
    part = jnp.where(first, low, high) + got
    for axis in AXES:
        count = lax.axis_size(axis)
        assert count & (count - 1) == 0
        bit = 2 if axis == "depth" else 1
        while bit < count:
            masks = [bit * way for way in WAYS[axis]] if 2 * bit < count else [bit]
            part = gathered_sum(part, axis, masks)
            bit *= len(masks) + 1
    part, done = lax.optimization_barrier((part, work(meanwhile)))
    other = swap(part, "depth", 1)
    return jnp.where(first, part, other), jnp.where(first, other, part), done


def local(inputs, weight, bias, cotangent):
    cubes, ci, depth, height, width = inputs.shape
    co = cotangent.shape[1]
    payload_rows = 9 * ci + 9 * ci // 2 + 16
    payload_shape = jax.ShapeDtypeStruct((payload_rows, 2 * co), F32)
    flops = 4 * width * 27 * ci * co
    total = None
    fields = []
    fields_in = [inputs[cube].transpose(1, 2, 0, 3) for cube in range(cubes)]
    rows = [(x[:, 0], x[:, -1]) for x in fields_in]
    rows, fields_in, weight, bias, cotangent = lax.optimization_barrier(
        (rows, fields_in, weight, bias, cotangent)
    )
    taps, bias_row, cotangent = loaded(weight.transpose(2, 3, 4, 1, 0), bias[None], cotangent)
    w1 = taps.transpose(2, 4, 0, 1, 3).reshape(3 * co, 9 * ci)
    for cube in range(cubes):
        x = fields_in[cube]
        cot = cotangent[cube].transpose(1, 2, 0, 3)
        parts = parts_of(depth, height)

        def forward(which, halos, so_far):
            count = len(parts[which])
            return call(
                functools.partial(forward_kernel, parts[which], len(halos)),
                (jax.ShapeDtypeStruct((count, co, width), BF16), payload_shape),
                [
                    pltpu.VMEM((9 * ci, count * width), BF16),
                    pltpu.VMEM((3 * co, count * width), F32),
                    pltpu.VMEM((3 * co, count * width), BF16),
                    pltpu.VMEM((9 * ci, 3 * co), F32),
                ],
                flops * count,
                x,
                *halos,
                w1,
                bias_row,
                cot,
                *so_far,
            )

        inner, part = forward(0, (), ())
        left, right = exchange(*rows[cube], "height")
        part, left, right = lax.optimization_barrier((part, left, right))

        def layer(at):
            return jnp.concatenate([left[at][None], x[at], right[at][None]], axis=0)

        low, high = exchange(layer(0), layer(-1), "depth")
        sides, part = forward(1, (left, right), (part,))
        ends, part = forward(2, (left, right, low, high), (part,))
        total = part if total is None else total + part
        below, above = exchange(ends[:height], ends[height:], "depth")
        below, above, taps = lax.optimization_barrier((below, above, taps))
        first_row = jnp.concatenate([ends[:1], sides[: depth - 2], ends[height : height + 1]], axis=0)
        last_row = jnp.concatenate([ends[height - 1 : height], sides[depth - 2 :], ends[-1:]], axis=0)
        around = exchange(*columns(first_row, last_row, below, above), "height")
        fields.append((inner, sides, ends, below, above, *around))
    w2 = jnp.flip(taps, (0, 1)).transpose(2, 3, 0, 1, 4).reshape(3 * ci, 9 * co)

    def input_gradients(fields):
        grads = []
        for field in fields:
            (grad,) = call(
                input_kernel,
                (jax.ShapeDtypeStruct((depth, height, ci, width), BF16),),
                [pltpu.VMEM(((depth + 2) * 3 * co, height * width), BF16)],
                flops // 2 * depth * height,
                *field,
                w2,
            )
            grads.append(grad.transpose(2, 0, 1, 3))
        return jnp.stack(grads)

    low, high, grads = summed(total, fields, input_gradients)
    voxels = cubes * depth * height * width
    for axis in AXES:
        voxels *= lax.axis_size(axis)
    scale = float(voxels) ** -0.5
    grad_taps, grad_bias = call(
        lambda *refs: unpack_kernel(scale, *refs),
        (jax.ShapeDtypeStruct((27 * ci, co), F32), jax.ShapeDtypeStruct((1, co), F32)),
        [pltpu.VMEM((payload_rows, 2 * co), F32)],
        payload_rows * 2 * co,
        low,
        high,
    )
    grad_weight = grad_taps.reshape(3, 3, 3, ci, co).transpose(4, 3, 0, 1, 2)
    return grads, grad_weight, grad_bias.reshape(co)


def solution(mesh):
    voxels = P("dp", None, "depth", "height", None)
    return jax.shard_map(
        local,
        mesh=mesh,
        in_specs=(voxels, P(), P(), voxels),
        out_specs=(voxels, P(), P()),
        check_vma=False,
    )
```

```python
import functools

import jax
import jax.numpy as jnp
from jax import lax
from jax.experimental import pallas as pl
from jax.experimental.pallas import tpu as pltpu
from jax.sharding import PartitionSpec as P

F32 = jnp.float32
BF16 = jnp.bfloat16
GROUP = 4
AXES = ("depth", "height", "dp")
WAYS = {"depth": (1, 2, 3), "height": (1, 2, 3), "dp": (1, 2, 3)}


def paired(axis):
    return lax.axis_index(axis) % 2 == 0 if lax.axis_size(axis) % 2 == 0 else jnp.bool_(True)


def meet(low_edge, high_edge, axis):
    count = lax.axis_size(axis)
    none = jnp.zeros_like(low_edge)
    if count == 1:
        return none, none
    if count % 2:
        up = [(i, i + 1) for i in range(count - 1)]
        down = [(i + 1, i) for i in range(count - 1)]
        return lax.ppermute(high_edge, axis, up), lax.ppermute(low_edge, axis, down)
    at, even = lax.axis_index(axis), paired(axis)
    inner = [(i, i ^ 1) for i in range(count)]
    first = lax.ppermute(jnp.where(even, high_edge, low_edge), axis, inner)
    if count == 2:
        return none, first
    outer = [(i, (i - 1 if i % 2 == 0 else i + 1) % count) for i in range(count)]
    second = lax.ppermute(jnp.where(even, low_edge, high_edge), axis, outer)
    return jnp.where((at == 0) | (at == count - 1), none, second), first


def exchange(low_edge, high_edge, axis):
    second, first = meet(low_edge, high_edge, axis)
    even = paired(axis)
    return jnp.where(even, second, first), jnp.where(even, first, second)


def columns(first_row, last_row, below, above):
    def column(rows, at):
        return jnp.concatenate([below[at][None], rows, above[at][None]], axis=0)

    return column(first_row, 0), column(last_row, -1)


def swap(array, axis, mask):
    return lax.ppermute(array, axis, [(i, i ^ mask) for i in range(lax.axis_size(axis))])


def fill_patches(row_of, depth, rows, patches):
    chans, width = row_of(1, 1).shape
    for d in range(depth + 2):
        for at, h in enumerate(rows):
            for b in range(3):
                patches[pl.ds((d * 3 + b) * chans, chans), pl.ds(at * width, width)] = row_of(d, h + b)


def shifted(value, step):
    if step == 0:
        return value
    width = value.shape[1]
    lane = lax.broadcasted_iota(jnp.int32, value.shape, 1)
    edge = width - 1 if step == 1 else 0
    return jnp.where(lane == edge, 0.0, pltpu.roll(value, (-step) % width, 1))


def rowwise(value, width):
    return [value[:, at : at + width] for at in range(0, value.shape[1], width)]


def beside(rows):
    return rows[0] if len(rows) == 1 else jnp.concatenate(rows, axis=1)


def forward_rows(positions, row_of, w1, bias, cot, delta, before, payload, patches, taps, slopes, grad):
    co, width = bias.shape[1], cot.shape[3]
    ci = patches.shape[0] // 9
    for at, (d, h) in enumerate(positions):
        for a in range(3):
            for b in range(3):
                patches[pl.ds((a * 3 + b) * ci, ci), pl.ds(at * width, width)] = row_of(d + a, h + b)
    taps[...] = jnp.dot(w1[...], patches[...], preferred_element_type=F32)
    shift_bias = jnp.broadcast_to(bias[...], (width, co)).T
    bias_acc = jnp.zeros((co, width), F32)
    starts = range(0, len(positions), GROUP)
    per_group = len(starts) > 2
    product = functools.partial(
        lax.dot_general,
        dimension_numbers=(((1,), (1,)), ((), ())),
        preferred_element_type=F32,
    )
    for start in starts:
        group = positions[start : start + GROUP]
        lanes = pl.ds(start * width, len(group) * width)
        low, middle, high = (rowwise(taps[i * co : (i + 1) * co, lanes], width) for i in range(3))
        linear = beside(
            [
                m + shift_bias + shifted(l, -1) + shifted(h, 1)
                for l, m, h in zip(low, middle, high)
            ]
        )
        sigma = 1.0 / (1.0 + jnp.exp(-linear))
        incoming = beside([cot[d, h].astype(F32) for d, h in group])
        rounded = (incoming * sigma * (1.0 + linear * (1.0 - sigma))).astype(BF16)
        wide = rowwise(rounded.astype(F32), width)
        for at, row in enumerate(rowwise(rounded, width)):
            delta[start + at] = row
            bias_acc = bias_acc + wide[at]
        before_it = beside([shifted(row, 1) for row in wide]).astype(BF16)
        after_it = beside([shifted(row, -1) for row in wide]).astype(BF16)
        if per_group:
            term = product(patches[:, lanes], jnp.concatenate([before_it, rounded, after_it], axis=0))
            grad[...] = term if start == 0 else grad[...] + term
        else:
            slopes[:co, lanes] = before_it
            slopes[co : 2 * co, lanes] = rounded
            slopes[2 * co :, lanes] = after_it
    if not per_group:
        grad[...] = product(patches[...], slopes[...])
    rows = grad.shape[0]
    tail = rows + rows // 2
    total = jnp.sum(bias_acc.T, axis=0, keepdims=True)
    left_over = payload.shape[0] - tail
    row_at = lax.broadcasted_iota(jnp.int32, (left_over, co), 0)
    bias_rows = jnp.where(row_at == 0, jnp.broadcast_to(total, (left_over, co)), 0.0)
    zeros = jnp.zeros((left_over, payload.shape[1] - co), F32)
    for at, value in (
        (pl.ds(0, rows), grad[:, : 2 * co]),
        (
            pl.ds(rows, rows // 2),
            jnp.concatenate([grad[: rows // 2, 2 * co :], grad[rows // 2 :, 2 * co :]], axis=1),
        ),
        (pl.ds(tail, left_over), jnp.concatenate([bias_rows, zeros], axis=1)),
    ):
        payload[at, :] = value if before is None else before[at, :] + value


def parts_of(depth, height):
    layers, rows = range(1, depth - 1), range(1, height - 1)
    return (
        [(d, h) for d in layers for h in rows],
        [(d, h) for h in (0, height - 1) for d in layers],
        [(d, h) for d in (0, depth - 1) for h in range(height)],
    )


def forward_kernel(positions, halos, x, *refs):
    left, right, low, high = (*refs[:halos], None, None, None, None)[:4]
    w1, bias, cot, *refs = refs[halos:]
    before, *refs = refs if halos else (None, *refs)
    depth, height = x.shape[:2]

    def row_of(d, h):
        if d == 0:
            return low[h]
        if d == depth + 1:
            return high[h]
        return left[d - 1] if h == 0 else right[d - 1] if h == height + 1 else x[d - 1, h - 1]

    delta, *refs = refs
    forward_rows(positions, row_of, w1, bias, cot, delta, before, *refs)


def input_kernel(inner, sides, ends, below, above, left, right, w2, out, patches):
    depth, height, ci, width = out.shape
    co = inner.shape[1]
    place = {}
    for ref, positions in zip((inner, sides, ends), parts_of(depth, height)):
        place.update({position: (ref, at) for at, position in enumerate(positions)})

    def row_of(d, h):
        if h == 0:
            return left[d]
        if h == height + 1:
            return right[d]
        if d == 0:
            return below[h - 1]
        if d == depth + 1:
            return above[h - 1]
        ref, at = place[d - 1, h - 1]
        return ref[at]

    fill_patches(row_of, depth, range(height), patches)
    for d in range(depth):
        taps = jnp.dot(w2[...], patches[pl.ds(d * 3 * co, 9 * co), :], preferred_element_type=F32)
        for h in range(height):
            lanes = slice(h * width, (h + 1) * width)
            total = taps[ci : 2 * ci, lanes]
            total = total + shifted(taps[:ci, lanes], 1) + shifted(taps[2 * ci :, lanes], -1)
            out[d, h] = total.astype(BF16)


def unpack_kernel(scale, low, high, weight_out, bias_out, full):
    half = low.shape[0]
    co = bias_out.shape[1]
    full[:half, :] = low[...] * scale
    full[half:, :] = high[...] * scale
    rows = weight_out.shape[0] // 3
    ci = rows // 9
    step = ci // 2
    for j in range(9):
        for part in range(2):
            source = j * ci + part * step
            to = 3 * j * ci + part * step
            weight_out[pl.ds(to, step), :] = full[pl.ds(source, step), :co]
            weight_out[pl.ds(to + ci, step), :] = full[pl.ds(source, step), co:]
            at = rows + source % (rows // 2)
            lanes = slice(0, co) if source < rows // 2 else slice(co, 2 * co)
            weight_out[pl.ds(to + 2 * ci, step), :] = full[pl.ds(at, step), lanes]
    bias_out[...] = full[rows + rows // 2 : rows + rows // 2 + 1, :co]


def load_kernel(*refs):
    count = len(refs) // 2
    done = refs[-1]
    copies = [pltpu.make_async_copy(refs[i], refs[count + i], done.at[i]) for i in range(count)]
    for copy in copies:
        copy.start()
    for copy in copies:
        copy.wait()


def loaded(*arrays):
    return pl.pallas_call(
        load_kernel,
        out_shape=[jax.ShapeDtypeStruct(a.shape, a.dtype) for a in arrays],
        in_specs=[pl.BlockSpec(memory_space=pltpu.HBM) for a in arrays],
        out_specs=[pl.BlockSpec(memory_space=pltpu.VMEM) for a in arrays],
        scratch_shapes=[pltpu.SemaphoreType.DMA((len(arrays),))],
        compiler_params=pltpu.CompilerParams(vmem_limit_bytes=16 << 20),
    )(*(pltpu.with_memory_space_constraint(a, pltpu.HBM) for a in arrays))


def call(kernel, outs, scratch, flops, *args):
    size = sum(a.size * a.dtype.itemsize for a in args) + sum(o.size * o.dtype.itemsize for o in outs)
    return pl.pallas_call(
        kernel,
        out_shape=outs,
        scratch_shapes=scratch,
        compiler_params=pltpu.CompilerParams(vmem_limit_bytes=40 << 20),
        cost_estimate=pl.CostEstimate(flops=flops, bytes_accessed=size, transcendentals=0),
    )(*args)


def gathered_sum(part, axis, masks):
    own = lax.reduce_precision(part, 8, 7)
    sent = own.astype(BF16)
    terms = [own] + [swap(sent, axis, mask).astype(F32) for mask in masks]
    while len(terms) > 1:
        terms = [terms[i] + terms[i + 1] for i in range(0, len(terms), 2)]
    return terms[0]


def summed(total, meanwhile, work):
    half = total.shape[0] // 2
    low, high = total[:half], total[half:]
    first = lax.axis_index("depth") % 2 == 0
    got = swap(jnp.where(first, high, low), "depth", 1)
    part = jnp.where(first, low, high) + got
    for axis in AXES:
        count = lax.axis_size(axis)
        assert count & (count - 1) == 0
        bit = 2 if axis == "depth" else 1
        while bit < count:
            masks = [bit * way for way in WAYS[axis]] if 2 * bit < count else [bit]
            part = gathered_sum(part, axis, masks)
            bit *= len(masks) + 1
    part, done = lax.optimization_barrier((part, work(meanwhile)))
    other = swap(part, "depth", 1)
    return jnp.where(first, part, other), jnp.where(first, other, part), done


def local(inputs, weight, bias, cotangent):
    cubes, ci, depth, height, width = inputs.shape
    co = cotangent.shape[1]
    payload_rows = 9 * ci + 9 * ci // 2 + 16
    payload_shape = jax.ShapeDtypeStruct((payload_rows, 2 * co), F32)
    flops = 4 * width * 27 * ci * co
    total = None
    fields = []
    (inputs,) = loaded(inputs)
    fields_in = [inputs[cube].transpose(1, 2, 0, 3) for cube in range(cubes)]
    rows = [(x[:, 0], x[:, -1]) for x in fields_in]
    rows, fields_in, weight, bias, cotangent = lax.optimization_barrier(
        (rows, fields_in, weight, bias, cotangent)
    )
    taps, bias_row, cotangent = loaded(weight.transpose(2, 3, 4, 1, 0), bias[None], cotangent)
    w1 = taps.transpose(2, 4, 0, 1, 3).reshape(3 * co, 9 * ci)
    for cube in range(cubes):
        x = fields_in[cube]
        cot = cotangent[cube].transpose(1, 2, 0, 3)
        parts = parts_of(depth, height)

        def forward(which, halos, so_far):
            count = len(parts[which])
            return call(
                functools.partial(forward_kernel, parts[which], len(halos)),
                (jax.ShapeDtypeStruct((count, co, width), BF16), payload_shape),
                [
                    pltpu.VMEM((9 * ci, count * width), BF16),
                    pltpu.VMEM((3 * co, count * width), F32),
                    pltpu.VMEM((3 * co, count * width), BF16),
                    pltpu.VMEM((9 * ci, 3 * co), F32),
                ],
                flops * count,
                x,
                *halos,
                w1,
                bias_row,
                cot,
                *so_far,
            )

        inner, part = forward(0, (), ())
        left, right = exchange(*rows[cube], "height")
        part, left, right = lax.optimization_barrier((part, left, right))

        def layer(at):
            return jnp.concatenate([left[at][None], x[at], right[at][None]], axis=0)

        low, high = exchange(layer(0), layer(-1), "depth")
        sides, part = forward(1, (left, right), (part,))
        ends, part = forward(2, (left, right, low, high), (part,))
        total = part if total is None else total + part
        below, above = exchange(ends[:height], ends[height:], "depth")
        below, above, taps = lax.optimization_barrier((below, above, taps))
        first_row = jnp.concatenate([ends[:1], sides[: depth - 2], ends[height : height + 1]], axis=0)
        last_row = jnp.concatenate([ends[height - 1 : height], sides[depth - 2 :], ends[-1:]], axis=0)
        around = exchange(*columns(first_row, last_row, below, above), "height")
        fields.append((inner, sides, ends, below, above, *around))
    w2 = jnp.flip(taps, (0, 1)).transpose(2, 3, 0, 1, 4).reshape(3 * ci, 9 * co)

    def input_gradients(fields):
        grads = []
        for field in fields:
            (grad,) = call(
                input_kernel,
                (jax.ShapeDtypeStruct((depth, height, ci, width), BF16),),
                [pltpu.VMEM(((depth + 2) * 3 * co, height * width), BF16)],
                flops // 2 * depth * height,
                *field,
                w2,
            )
            grads.append(grad.transpose(2, 0, 1, 3))
        return jnp.stack(grads)

    low, high, grads = summed(total, fields, input_gradients)
    voxels = cubes * depth * height * width
    for axis in AXES:
        voxels *= lax.axis_size(axis)
    scale = float(voxels) ** -0.5
    grad_taps, grad_bias = call(
        lambda *refs: unpack_kernel(scale, *refs),
        (jax.ShapeDtypeStruct((27 * ci, co), F32), jax.ShapeDtypeStruct((1, co), F32)),
        [pltpu.VMEM((payload_rows, 2 * co), F32)],
        payload_rows * 2 * co,
        low,
        high,
    )
    grad_weight = grad_taps.reshape(3, 3, 3, ci, co).transpose(4, 3, 0, 1, 2)
    return grads, grad_weight, grad_bias.reshape(co)


def solution(mesh):
    voxels = P("dp", None, "depth", "height", None)
    return jax.shard_map(
        local,
        mesh=mesh,
        in_specs=(voxels, P(), P(), voxels),
        out_specs=(voxels, P(), P()),
        check_vma=False,
    )
```

```python
import functools

import jax
import jax.numpy as jnp
from jax import lax
from jax.experimental import pallas as pl
from jax.experimental.pallas import tpu as pltpu
from jax.sharding import PartitionSpec as P

F32 = jnp.float32
BF16 = jnp.bfloat16
GROUP = 4
AXES = ("depth", "height", "dp")
WAYS = {"depth": (1, 2, 3), "height": (1, 2, 3), "dp": (1, 2, 3)}


def paired(axis):
    return lax.axis_index(axis) % 2 == 0 if lax.axis_size(axis) % 2 == 0 else jnp.bool_(True)


def meet(low_edge, high_edge, axis, first=None):
    count = lax.axis_size(axis)
    none = jnp.zeros_like(low_edge)
    if count == 1:
        return none, none
    if count % 2:
        up = [(i, i + 1) for i in range(count - 1)]
        down = [(i + 1, i) for i in range(count - 1)]
        return lax.ppermute(high_edge, axis, up), lax.ppermute(low_edge, axis, down)
    at, even = lax.axis_index(axis), paired(axis)
    inner = [(i, i ^ 1) for i in range(count)]
    if first is None:
        first = lax.ppermute(jnp.where(even, high_edge, low_edge), axis, inner)
    if count == 2:
        return none, first
    outer = [(i, (i - 1 if i % 2 == 0 else i + 1) % count) for i in range(count)]
    second = lax.ppermute(jnp.where(even, low_edge, high_edge), axis, outer)
    return jnp.where((at == 0) | (at == count - 1), none, second), first


def exchange(low_edge, high_edge, axis, first=None):
    second, first = meet(low_edge, high_edge, axis, first)
    even = paired(axis)
    return jnp.where(even, second, first), jnp.where(even, first, second)


def columns(first_row, last_row, below, above):
    def column(rows, at):
        return jnp.concatenate([below[at][None], rows, above[at][None]], axis=0)

    return column(first_row, 0), column(last_row, -1)


def swap(array, axis, mask):
    return lax.ppermute(array, axis, [(i, i ^ mask) for i in range(lax.axis_size(axis))])


def fill_patches(row_of, depth, rows, patches):
    chans, width = row_of(1, 1).shape
    for d in range(depth + 2):
        for at, h in enumerate(rows):
            for b in range(3):
                patches[pl.ds((d * 3 + b) * chans, chans), pl.ds(at * width, width)] = row_of(d, h + b)


def shifted(value, step):
    if step == 0:
        return value
    width = value.shape[1]
    lane = lax.broadcasted_iota(jnp.int32, value.shape, 1)
    edge = width - 1 if step == 1 else 0
    return jnp.where(lane == edge, 0.0, pltpu.roll(value, (-step) % width, 1))


def rowwise(value, width):
    return [value[:, at : at + width] for at in range(0, value.shape[1], width)]


def beside(rows):
    return rows[0] if len(rows) == 1 else jnp.concatenate(rows, axis=1)


def forward_rows(positions, row_of, w1, bias, cot, delta, before, payload, patches, taps, slopes, grad):
    co, width = bias.shape[1], cot.shape[3]
    ci = patches.shape[0] // 9
    for at, (d, h) in enumerate(positions):
        for a in range(3):
            for b in range(3):
                patches[pl.ds((a * 3 + b) * ci, ci), pl.ds(at * width, width)] = row_of(d + a, h + b)
    taps[...] = jnp.dot(w1[...], patches[...], preferred_element_type=F32)
    shift_bias = jnp.broadcast_to(bias[...], (width, co)).T
    bias_acc = jnp.zeros((co, width), F32)
    starts = range(0, len(positions), GROUP)
    per_group = len(starts) > 2
    product = functools.partial(
        lax.dot_general,
        dimension_numbers=(((1,), (1,)), ((), ())),
        preferred_element_type=F32,
    )
    for start in starts:
        group = positions[start : start + GROUP]
        lanes = pl.ds(start * width, len(group) * width)
        low, middle, high = (rowwise(taps[i * co : (i + 1) * co, lanes], width) for i in range(3))
        linear = beside(
            [
                m + shift_bias + shifted(l, -1) + shifted(h, 1)
                for l, m, h in zip(low, middle, high)
            ]
        )
        sigma = 1.0 / (1.0 + jnp.exp(-linear))
        incoming = beside([cot[d, h].astype(F32) for d, h in group])
        rounded = (incoming * sigma * (1.0 + linear * (1.0 - sigma))).astype(BF16)
        wide = rowwise(rounded.astype(F32), width)
        for at, row in enumerate(rowwise(rounded, width)):
            delta[start + at] = row
            bias_acc = bias_acc + wide[at]
        before_it = beside([shifted(row, 1) for row in wide]).astype(BF16)
        after_it = beside([shifted(row, -1) for row in wide]).astype(BF16)
        if per_group:
            term = product(patches[:, lanes], jnp.concatenate([before_it, rounded, after_it], axis=0))
            grad[...] = term if start == 0 else grad[...] + term
        else:
            slopes[:co, lanes] = before_it
            slopes[co : 2 * co, lanes] = rounded
            slopes[2 * co :, lanes] = after_it
    if not per_group:
        grad[...] = product(patches[...], slopes[...])
    rows = grad.shape[0]
    tail = rows + rows // 2
    total = jnp.sum(bias_acc.T, axis=0, keepdims=True)
    left_over = payload.shape[0] - tail
    row_at = lax.broadcasted_iota(jnp.int32, (left_over, co), 0)
    bias_rows = jnp.where(row_at == 0, jnp.broadcast_to(total, (left_over, co)), 0.0)
    zeros = jnp.zeros((left_over, payload.shape[1] - co), F32)
    for at, value in (
        (pl.ds(0, rows), grad[:, : 2 * co]),
        (
            pl.ds(rows, rows // 2),
            jnp.concatenate([grad[: rows // 2, 2 * co :], grad[rows // 2 :, 2 * co :]], axis=1),
        ),
        (pl.ds(tail, left_over), jnp.concatenate([bias_rows, zeros], axis=1)),
    ):
        payload[at, :] = value if before is None else before[at, :] + value


def parts_of(depth, height):
    layers, rows = range(1, depth - 1), range(1, height - 1)
    return (
        [(d, h) for d in layers for h in rows],
        [(d, h) for h in (0, height - 1) for d in layers],
        [(d, h) for d in (0, depth - 1) for h in range(height)],
    )


def forward_kernel(positions, halos, x, *refs):
    left, right, low, high = (*refs[:halos], None, None, None, None)[:4]
    w1, bias, cot, *refs = refs[halos:]
    before, *refs = refs if halos else (None, *refs)
    depth, height = x.shape[:2]

    def row_of(d, h):
        if d == 0:
            return low[h]
        if d == depth + 1:
            return high[h]
        return left[d - 1] if h == 0 else right[d - 1] if h == height + 1 else x[d - 1, h - 1]

    delta, *refs = refs
    forward_rows(positions, row_of, w1, bias, cot, delta, before, *refs)


def input_kernel(inner, sides, ends, below, above, left, right, w2, out, patches):
    depth, height, ci, width = out.shape
    co = inner.shape[1]
    place = {}
    for ref, positions in zip((inner, sides, ends), parts_of(depth, height)):
        place.update({position: (ref, at) for at, position in enumerate(positions)})

    def row_of(d, h):
        if h == 0:
            return left[d]
        if h == height + 1:
            return right[d]
        if d == 0:
            return below[h - 1]
        if d == depth + 1:
            return above[h - 1]
        ref, at = place[d - 1, h - 1]
        return ref[at]

    fill_patches(row_of, depth, range(height), patches)
    for d in range(depth):
        taps = jnp.dot(w2[...], patches[pl.ds(d * 3 * co, 9 * co), :], preferred_element_type=F32)
        for h in range(height):
            lanes = slice(h * width, (h + 1) * width)
            total = taps[ci : 2 * ci, lanes]
            total = total + shifted(taps[:ci, lanes], 1) + shifted(taps[2 * ci :, lanes], -1)
            out[d, h] = total.astype(BF16)


def unpack_kernel(scale, low, high, weight_out, bias_out, full):
    half = low.shape[0]
    co = bias_out.shape[1]
    full[:half, :] = low[...] * scale
    full[half:, :] = high[...] * scale
    rows = weight_out.shape[0] // 3
    ci = rows // 9
    step = ci // 2
    for j in range(9):
        for part in range(2):
            source = j * ci + part * step
            to = 3 * j * ci + part * step
            weight_out[pl.ds(to, step), :] = full[pl.ds(source, step), :co]
            weight_out[pl.ds(to + ci, step), :] = full[pl.ds(source, step), co:]
            at = rows + source % (rows // 2)
            lanes = slice(0, co) if source < rows // 2 else slice(co, 2 * co)
            weight_out[pl.ds(to + 2 * ci, step), :] = full[pl.ds(at, step), lanes]
    bias_out[...] = full[rows + rows // 2 : rows + rows // 2 + 1, :co]


def load_kernel(*refs):
    count = len(refs) // 2
    done = refs[-1]
    copies = [pltpu.make_async_copy(refs[i], refs[count + i], done.at[i]) for i in range(count)]
    for copy in copies:
        copy.start()
    for copy in copies:
        copy.wait()


def loaded(*arrays):
    return pl.pallas_call(
        load_kernel,
        out_shape=[jax.ShapeDtypeStruct(a.shape, a.dtype) for a in arrays],
        in_specs=[pl.BlockSpec(memory_space=pltpu.HBM) for a in arrays],
        out_specs=[pl.BlockSpec(memory_space=pltpu.VMEM) for a in arrays],
        scratch_shapes=[pltpu.SemaphoreType.DMA((len(arrays),))],
        compiler_params=pltpu.CompilerParams(vmem_limit_bytes=16 << 20),
    )(*(pltpu.with_memory_space_constraint(a, pltpu.HBM) for a in arrays))


def call(kernel, outs, scratch, flops, *args):
    size = sum(a.size * a.dtype.itemsize for a in args) + sum(o.size * o.dtype.itemsize for o in outs)
    return pl.pallas_call(
        kernel,
        out_shape=outs,
        scratch_shapes=scratch,
        compiler_params=pltpu.CompilerParams(vmem_limit_bytes=40 << 20),
        cost_estimate=pl.CostEstimate(flops=flops, bytes_accessed=size, transcendentals=0),
    )(*args)


def gathered_sum(part, axis, masks, meanwhile):
    own = lax.reduce_precision(part, 8, 7)
    sent = own.astype(BF16)
    near, meanwhile = lax.optimization_barrier((sent, meanwhile))
    terms = [own]
    for mask in masks:
        terms.append(swap(near if mask == min(masks) else sent, axis, mask).astype(F32))
    while len(terms) > 1:
        terms = [terms[i] + terms[i + 1] for i in range(0, len(terms), 2)]
    return terms[0], meanwhile


def halved(total, edges):
    half, lanes = total.shape[0] // 2, total.shape[1]
    first = lax.axis_index("depth") % 2 == 0
    low, high = total[:half], total[half:]
    flat = [edge.astype(F32).reshape(-1, lanes) for edge in edges]
    got = swap(jnp.concatenate([jnp.where(first, high, low), *flat], axis=0), "depth", 1)
    part = jnp.where(first, low, high) + got[:half]
    received, at = [], half
    for edge, rows in zip(edges, flat):
        received.append(got[at : at + rows.shape[0]].reshape(edge.shape).astype(BF16))
        at += rows.shape[0]
    return part, received


def summed(part, first_halos, meanwhile, work):
    first = lax.axis_index("depth") % 2 == 0
    for axis in AXES:
        count = lax.axis_size(axis)
        assert count & (count - 1) == 0
        bit = 2 if axis == "depth" else 1
        while bit < count:
            masks = [bit * way for way in WAYS[axis]] if 2 * bit < count else [bit]
            if axis == AXES[-1]:
                part, _ = gathered_sum(part, axis, masks, first_halos)
            else:
                part, _ = gathered_sum(part, axis, masks, ())
            bit *= len(masks) + 1
    part, done = lax.optimization_barrier((part, work(meanwhile)))
    other = swap(part, "depth", 1)
    return jnp.where(first, part, other), jnp.where(first, other, part), done


def local(inputs, weight, bias, cotangent):
    cubes, ci, depth, height, width = inputs.shape
    co = cotangent.shape[1]
    payload_rows = 9 * ci + 9 * ci // 2 + 16
    payload_shape = jax.ShapeDtypeStruct((payload_rows, 2 * co), F32)
    flops = 4 * width * 27 * ci * co
    total = None
    deltas, fields = [], []
    fields_in = [inputs[cube].transpose(1, 2, 0, 3) for cube in range(cubes)]
    rows = [(x[:, 0], x[:, -1]) for x in fields_in]
    rows, fields_in, weight, bias, cotangent = lax.optimization_barrier(
        (rows, fields_in, weight, bias, cotangent)
    )
    taps, bias_row, cotangent = loaded(weight.transpose(2, 3, 4, 1, 0), bias[None], cotangent)
    w1 = taps.transpose(2, 4, 0, 1, 3).reshape(3 * co, 9 * ci)
    for cube in range(cubes):
        x = fields_in[cube]
        cot = cotangent[cube].transpose(1, 2, 0, 3)
        parts = parts_of(depth, height)

        def forward(which, halos, so_far):
            count = len(parts[which])
            return call(
                functools.partial(forward_kernel, parts[which], len(halos)),
                (jax.ShapeDtypeStruct((count, co, width), BF16), payload_shape),
                [
                    pltpu.VMEM((9 * ci, count * width), BF16),
                    pltpu.VMEM((3 * co, count * width), F32),
                    pltpu.VMEM((3 * co, count * width), BF16),
                    pltpu.VMEM((9 * ci, 3 * co), F32),
                ],
                flops * count,
                x,
                *halos,
                w1,
                bias_row,
                cot,
                *so_far,
            )

        inner, part = forward(0, (), ())
        left, right = exchange(*rows[cube], "height")
        part, left, right = lax.optimization_barrier((part, left, right))

        def layer(at):
            return jnp.concatenate([left[at][None], x[at], right[at][None]], axis=0)

        low, high = exchange(layer(0), layer(-1), "depth")
        sides, part = forward(1, (left, right), (part,))
        ends, part = forward(2, (left, right, low, high), (part,))
        total = part if total is None else total + part
        deltas.append((inner, sides, ends))
    even = paired("depth")
    part, edges = halved(
        total, [jnp.where(even, ends[height:], ends[:height]) for _, _, ends in deltas]
    )
    first_halos = []
    for (inner, sides, ends), edge in zip(deltas, edges):
        below, above = exchange(ends[:height], ends[height:], "depth", edge)
        below, above, taps = lax.optimization_barrier((below, above, taps))
        first_row = jnp.concatenate([ends[:1], sides[: depth - 2], ends[height : height + 1]], axis=0)
        last_row = jnp.concatenate([ends[height - 1 : height], sides[depth - 2 :], ends[-1:]], axis=0)
        second, first = meet(*columns(first_row, last_row, below, above), "height")
        first = lax.optimization_barrier(first)
        first_halos.append(first)
        up = paired("height")
        around = jnp.where(up, second, first), jnp.where(up, first, second)
        fields.append((inner, sides, ends, below, above, *around))
    w2 = jnp.flip(taps, (0, 1)).transpose(2, 3, 0, 1, 4).reshape(3 * ci, 9 * co)

    def input_gradients(fields):
        grads = []
        for field in fields:
            (grad,) = call(
                input_kernel,
                (jax.ShapeDtypeStruct((depth, height, ci, width), BF16),),
                [pltpu.VMEM(((depth + 2) * 3 * co, height * width), BF16)],
                flops // 2 * depth * height,
                *field,
                w2,
            )
            grads.append(grad.transpose(2, 0, 1, 3))
        return jnp.stack(grads)

    low, high, grads = summed(part, first_halos, fields, input_gradients)
    voxels = cubes * depth * height * width
    for axis in AXES:
        voxels *= lax.axis_size(axis)
    scale = float(voxels) ** -0.5
    grad_taps, grad_bias = call(
        lambda *refs: unpack_kernel(scale, *refs),
        (jax.ShapeDtypeStruct((27 * ci, co), F32), jax.ShapeDtypeStruct((1, co), F32)),
        [pltpu.VMEM((payload_rows, 2 * co), F32)],
        payload_rows * 2 * co,
        low,
        high,
    )
    grad_weight = grad_taps.reshape(3, 3, 3, ci, co).transpose(4, 3, 0, 1, 2)
    return grads, grad_weight, grad_bias.reshape(co)


def solution(mesh):
    voxels = P("dp", None, "depth", "height", None)
    return jax.shard_map(
        local,
        mesh=mesh,
        in_specs=(voxels, P(), P(), voxels),
        out_specs=(voxels, P(), P()),
        check_vma=False,
    )
```

```python
import functools

import jax
import jax.numpy as jnp
from jax import lax
from jax.experimental import pallas as pl
from jax.experimental.pallas import tpu as pltpu
from jax.sharding import PartitionSpec as P

F32 = jnp.float32
BF16 = jnp.bfloat16
GROUP = 4
AXES = ("depth", "height", "dp")
WAYS = {"depth": (1, 2, 3), "height": (1, 2, 3), "dp": (1, 2, 3)}


def paired(axis):
    return lax.axis_index(axis) % 2 == 0 if lax.axis_size(axis) % 2 == 0 else jnp.bool_(True)


def meet(low_edge, high_edge, axis):
    count = lax.axis_size(axis)
    none = jnp.zeros_like(low_edge)
    if count == 1:
        return none, none
    if count % 2:
        up = [(i, i + 1) for i in range(count - 1)]
        down = [(i + 1, i) for i in range(count - 1)]
        return lax.ppermute(high_edge, axis, up), lax.ppermute(low_edge, axis, down)
    at, even = lax.axis_index(axis), paired(axis)
    inner = [(i, i ^ 1) for i in range(count)]
    first = lax.ppermute(jnp.where(even, high_edge, low_edge), axis, inner)
    if count == 2:
        return none, first
    outer = [(i, (i - 1 if i % 2 == 0 else i + 1) % count) for i in range(count)]
    second = lax.ppermute(jnp.where(even, low_edge, high_edge), axis, outer)
    return jnp.where((at == 0) | (at == count - 1), none, second), first


def exchange(low_edge, high_edge, axis):
    second, first = meet(low_edge, high_edge, axis)
    even = paired(axis)
    return jnp.where(even, second, first), jnp.where(even, first, second)


def columns(first_row, last_row, below, above):
    def column(rows, at):
        return jnp.concatenate([below[at][None], rows, above[at][None]], axis=0)

    return column(first_row, 0), column(last_row, -1)


def swap(array, axis, mask):
    return lax.ppermute(array, axis, [(i, i ^ mask) for i in range(lax.axis_size(axis))])


def fill_patches(row_of, depth, rows, patches):
    chans, width = row_of(1, 1).shape
    for d in range(depth + 2):
        for at, h in enumerate(rows):
            for b in range(3):
                patches[pl.ds((d * 3 + b) * chans, chans), pl.ds(at * width, width)] = row_of(d, h + b)


def shifted(value, step):
    if step == 0:
        return value
    width = value.shape[1]
    lane = lax.broadcasted_iota(jnp.int32, value.shape, 1)
    edge = width - 1 if step == 1 else 0
    return jnp.where(lane == edge, 0.0, pltpu.roll(value, (-step) % width, 1))


def rowwise(value, width):
    return [value[:, at : at + width] for at in range(0, value.shape[1], width)]


def beside(rows):
    return rows[0] if len(rows) == 1 else jnp.concatenate(rows, axis=1)


def forward_rows(positions, row_of, w1, bias, cot, delta, before, payload, patches, taps, slopes, grad):
    co, width = bias.shape[1], cot.shape[3]
    ci = patches.shape[0] // 9
    for at, (d, h) in enumerate(positions):
        for a in range(3):
            for b in range(3):
                patches[pl.ds((a * 3 + b) * ci, ci), pl.ds(at * width, width)] = row_of(d + a, h + b)
    taps[...] = jnp.dot(w1[...], patches[...], preferred_element_type=F32)
    shift_bias = jnp.broadcast_to(bias[...], (width, co)).T
    bias_acc = jnp.zeros((co, width), F32)
    starts = range(0, len(positions), GROUP)
    per_group = len(starts) > 2
    product = functools.partial(
        lax.dot_general,
        dimension_numbers=(((1,), (1,)), ((), ())),
        preferred_element_type=F32,
    )
    for start in starts:
        group = positions[start : start + GROUP]
        lanes = pl.ds(start * width, len(group) * width)
        low, middle, high = (rowwise(taps[i * co : (i + 1) * co, lanes], width) for i in range(3))
        linear = beside(
            [
                m + shift_bias + shifted(l, -1) + shifted(h, 1)
                for l, m, h in zip(low, middle, high)
            ]
        )
        sigma = 1.0 / (1.0 + jnp.exp(-linear))
        incoming = beside([cot[d, h].astype(F32) for d, h in group])
        rounded = (incoming * sigma * (1.0 + linear * (1.0 - sigma))).astype(BF16)
        wide = rowwise(rounded.astype(F32), width)
        for at, row in enumerate(rowwise(rounded, width)):
            delta[start + at] = row
            bias_acc = bias_acc + wide[at]
        before_it = beside([shifted(row, 1) for row in wide]).astype(BF16)
        after_it = beside([shifted(row, -1) for row in wide]).astype(BF16)
        if per_group:
            term = product(patches[:, lanes], jnp.concatenate([before_it, rounded, after_it], axis=0))
            grad[...] = term if start == 0 else grad[...] + term
        else:
            slopes[:co, lanes] = before_it
            slopes[co : 2 * co, lanes] = rounded
            slopes[2 * co :, lanes] = after_it
    if not per_group:
        grad[...] = product(patches[...], slopes[...])
    rows = grad.shape[0]
    tail = rows + rows // 2
    total = jnp.sum(bias_acc.T, axis=0, keepdims=True)
    left_over = payload.shape[0] - tail
    row_at = lax.broadcasted_iota(jnp.int32, (left_over, co), 0)
    bias_rows = jnp.where(row_at == 0, jnp.broadcast_to(total, (left_over, co)), 0.0)
    zeros = jnp.zeros((left_over, payload.shape[1] - co), F32)
    for at, value in (
        (pl.ds(0, rows), grad[:, : 2 * co]),
        (
            pl.ds(rows, rows // 2),
            jnp.concatenate([grad[: rows // 2, 2 * co :], grad[rows // 2 :, 2 * co :]], axis=1),
        ),
        (pl.ds(tail, left_over), jnp.concatenate([bias_rows, zeros], axis=1)),
    ):
        payload[at, :] = value if before is None else before[at, :] + value


def parts_of(depth, height):
    layers, rows = range(1, depth - 1), range(1, height - 1)
    return (
        [(d, h) for d in layers for h in rows],
        [(d, h) for h in (0, height - 1) for d in layers],
        [(d, h) for d in (0, depth - 1) for h in range(height)],
    )


def forward_kernel(positions, halos, x, *refs):
    left, right, low, high = (*refs[:halos], None, None, None, None)[:4]
    w1, bias, cot, *refs = refs[halos:]
    before, *refs = refs if halos else (None, *refs)
    depth, height = x.shape[:2]

    def row_of(d, h):
        if d == 0:
            return low[h]
        if d == depth + 1:
            return high[h]
        return left[d - 1] if h == 0 else right[d - 1] if h == height + 1 else x[d - 1, h - 1]

    delta, *refs = refs
    forward_rows(positions, row_of, w1, bias, cot, delta, before, *refs)


def input_kernel(inner, sides, ends, below, above, left, right, w2, out, patches):
    depth, height, ci, width = out.shape
    co = inner.shape[1]
    place = {}
    for ref, positions in zip((inner, sides, ends), parts_of(depth, height)):
        place.update({position: (ref, at) for at, position in enumerate(positions)})

    def row_of(d, h):
        if h == 0:
            return left[d]
        if h == height + 1:
            return right[d]
        if d == 0:
            return below[h - 1]
        if d == depth + 1:
            return above[h - 1]
        ref, at = place[d - 1, h - 1]
        return ref[at]

    fill_patches(row_of, depth, range(height), patches)
    for d in range(depth):
        taps = jnp.dot(w2[...], patches[pl.ds(d * 3 * co, 9 * co), :], preferred_element_type=F32)
        for h in range(height):
            lanes = slice(h * width, (h + 1) * width)
            total = taps[ci : 2 * ci, lanes]
            total = total + shifted(taps[:ci, lanes], 1) + shifted(taps[2 * ci :, lanes], -1)
            out[d, h] = total.astype(BF16)


def unpack_kernel(scale, low, high, weight_out, bias_out, full):
    half = low.shape[0]
    co = bias_out.shape[1]
    full[:half, :] = low[...] * scale
    full[half:, :] = high[...] * scale
    rows = weight_out.shape[0] // 3
    ci = rows // 9
    step = ci // 2
    for j in range(9):
        for part in range(2):
            source = j * ci + part * step
            to = 3 * j * ci + part * step
            weight_out[pl.ds(to, step), :] = full[pl.ds(source, step), :co]
            weight_out[pl.ds(to + ci, step), :] = full[pl.ds(source, step), co:]
            at = rows + source % (rows // 2)
            lanes = slice(0, co) if source < rows // 2 else slice(co, 2 * co)
            weight_out[pl.ds(to + 2 * ci, step), :] = full[pl.ds(at, step), lanes]
    bias_out[...] = full[rows + rows // 2 : rows + rows // 2 + 1, :co]


def load_kernel(*refs):
    count = len(refs) // 2
    done = refs[-1]
    copies = [pltpu.make_async_copy(refs[i], refs[count + i], done.at[i]) for i in range(count)]
    for copy in copies:
        copy.start()
    for copy in copies:
        copy.wait()


def loaded(*arrays):
    return pl.pallas_call(
        load_kernel,
        out_shape=[jax.ShapeDtypeStruct(a.shape, a.dtype) for a in arrays],
        in_specs=[pl.BlockSpec(memory_space=pltpu.HBM) for a in arrays],
        out_specs=[pl.BlockSpec(memory_space=pltpu.VMEM) for a in arrays],
        scratch_shapes=[pltpu.SemaphoreType.DMA((len(arrays),))],
        compiler_params=pltpu.CompilerParams(vmem_limit_bytes=16 << 20),
    )(*(pltpu.with_memory_space_constraint(a, pltpu.HBM) for a in arrays))


def call(kernel, outs, scratch, flops, *args):
    size = sum(a.size * a.dtype.itemsize for a in args) + sum(o.size * o.dtype.itemsize for o in outs)
    return pl.pallas_call(
        kernel,
        out_shape=outs,
        scratch_shapes=scratch,
        compiler_params=pltpu.CompilerParams(vmem_limit_bytes=40 << 20),
        cost_estimate=pl.CostEstimate(flops=flops, bytes_accessed=size, transcendentals=0),
    )(*args)


def gathered_sum(part, axis, masks):
    own = lax.reduce_precision(part, 8, 7)
    sent = own.astype(BF16)
    terms = [own] + [swap(sent, axis, mask).astype(F32) for mask in masks]
    while len(terms) > 1:
        terms = [terms[i] + terms[i + 1] for i in range(0, len(terms), 2)]
    return terms[0]


def summed(total, meanwhile, work):
    half = total.shape[0] // 2
    low, high = total[:half], total[half:]
    first = lax.axis_index("depth") % 2 == 0
    got = swap(jnp.where(first, high, low), "depth", 1)
    part = jnp.where(first, low, high) + got
    for axis in AXES:
        count = lax.axis_size(axis)
        assert count & (count - 1) == 0
        bit = 2 if axis == "depth" else 1
        while bit < count:
            masks = [bit * way for way in WAYS[axis]] if 2 * bit < count else [bit]
            part = gathered_sum(part, axis, masks)
            bit *= len(masks) + 1
    part, done = lax.optimization_barrier((part, work(meanwhile)))
    other = swap(part, "depth", 1)
    return jnp.where(first, part, other), jnp.where(first, other, part), done


def local(inputs, weight, bias, cotangent):
    cubes, ci, depth, height, width = inputs.shape
    co = cotangent.shape[1]
    payload_rows = 9 * ci + 9 * ci // 2 + 16
    payload_shape = jax.ShapeDtypeStruct((payload_rows, 2 * co), F32)
    flops = 4 * width * 27 * ci * co
    total = None
    fields = []
    fields_in = [inputs[cube].transpose(1, 2, 0, 3) for cube in range(cubes)]
    rows = [(x[:, 0], x[:, -1]) for x in fields_in]
    rows, fields_in, weight, bias, cotangent = lax.optimization_barrier(
        (rows, fields_in, weight, bias, cotangent)
    )
    taps, bias_row, cotangent = loaded(weight.transpose(2, 3, 4, 1, 0), bias[None], cotangent)
    w1 = taps.transpose(2, 4, 0, 1, 3).reshape(3 * co, 9 * ci)
    for cube in range(cubes):
        x = fields_in[cube]
        cot = cotangent[cube].transpose(1, 2, 0, 3)
        parts = parts_of(depth, height)

        def forward(which, halos, so_far):
            count = len(parts[which])
            return call(
                functools.partial(forward_kernel, parts[which], len(halos)),
                (jax.ShapeDtypeStruct((count, co, width), BF16), payload_shape),
                [
                    pltpu.VMEM((9 * ci, count * width), BF16),
                    pltpu.VMEM((3 * co, count * width), F32),
                    pltpu.VMEM((3 * co, count * width), BF16),
                    pltpu.VMEM((9 * ci, 3 * co), F32),
                ],
                flops * count,
                x,
                *halos,
                w1,
                bias_row,
                cot,
                *so_far,
            )

        inner, part = forward(0, (), ())
        left, right = exchange(*rows[cube], "height")
        part, left, right = lax.optimization_barrier((part, left, right))

        def layer(at):
            return jnp.concatenate([left[at][None], x[at], right[at][None]], axis=0)

        low, high = exchange(layer(0), layer(-1), "depth")
        sides, part = forward(1, (left, right), (part,))
        ends, part = forward(2, (left, right, low, high), (part,))
        total = part if total is None else total + part
        below, above = exchange(ends[:height], ends[height:], "depth")
        below, above, taps = lax.optimization_barrier((below, above, taps))
        first_row = jnp.concatenate([ends[:1], sides[: depth - 2], ends[height : height + 1]], axis=0)
        last_row = jnp.concatenate([ends[height - 1 : height], sides[depth - 2 :], ends[-1:]], axis=0)
        w2 = jnp.flip(taps, (0, 1)).transpose(2, 3, 0, 1, 4).reshape(3 * ci, 9 * co)
        first_row, last_row, below, above, w2 = lax.optimization_barrier(
            (first_row, last_row, below, above, w2)
        )
        around = exchange(*columns(first_row, last_row, below, above), "height")
        fields.append((inner, sides, ends, below, above, *around))

    def input_gradients(fields):
        grads = []
        for field in fields:
            (grad,) = call(
                input_kernel,
                (jax.ShapeDtypeStruct((depth, height, ci, width), BF16),),
                [pltpu.VMEM(((depth + 2) * 3 * co, height * width), BF16)],
                flops // 2 * depth * height,
                *field,
                w2,
            )
            grads.append(grad.transpose(2, 0, 1, 3))
        return jnp.stack(grads)

    low, high, grads = summed(total, fields, input_gradients)
    voxels = cubes * depth * height * width
    for axis in AXES:
        voxels *= lax.axis_size(axis)
    scale = float(voxels) ** -0.5
    grad_taps, grad_bias = call(
        lambda *refs: unpack_kernel(scale, *refs),
        (jax.ShapeDtypeStruct((27 * ci, co), F32), jax.ShapeDtypeStruct((1, co), F32)),
        [pltpu.VMEM((payload_rows, 2 * co), F32)],
        payload_rows * 2 * co,
        low,
        high,
    )
    grad_weight = grad_taps.reshape(3, 3, 3, ci, co).transpose(4, 3, 0, 1, 2)
    return grads, grad_weight, grad_bias.reshape(co)


def solution(mesh):
    voxels = P("dp", None, "depth", "height", None)
    return jax.shard_map(
        local,
        mesh=mesh,
        in_specs=(voxels, P(), P(), voxels),
        out_specs=(voxels, P(), P()),
        check_vma=False,
    )
```

```python
import functools

import jax
import jax.numpy as jnp
from jax import lax
from jax.experimental import pallas as pl
from jax.experimental.pallas import tpu as pltpu
from jax.sharding import PartitionSpec as P

F32 = jnp.float32
BF16 = jnp.bfloat16
GROUP = 4
AXES = ("depth", "height", "dp")
WAYS = {"depth": (1, 2, 3), "height": (1, 2, 3), "dp": (2, 1, 3)}


def paired(axis):
    return lax.axis_index(axis) % 2 == 0 if lax.axis_size(axis) % 2 == 0 else jnp.bool_(True)


def meet(low_edge, high_edge, axis):
    count = lax.axis_size(axis)
    none = jnp.zeros_like(low_edge)
    if count == 1:
        return none, none
    if count % 2:
        up = [(i, i + 1) for i in range(count - 1)]
        down = [(i + 1, i) for i in range(count - 1)]
        return lax.ppermute(high_edge, axis, up), lax.ppermute(low_edge, axis, down)
    at, even = lax.axis_index(axis), paired(axis)
    inner = [(i, i ^ 1) for i in range(count)]
    first = lax.ppermute(jnp.where(even, high_edge, low_edge), axis, inner)
    if count == 2:
        return none, first
    outer = [(i, (i - 1 if i % 2 == 0 else i + 1) % count) for i in range(count)]
    second = lax.ppermute(jnp.where(even, low_edge, high_edge), axis, outer)
    return jnp.where((at == 0) | (at == count - 1), none, second), first


def exchange(low_edge, high_edge, axis):
    second, first = meet(low_edge, high_edge, axis)
    even = paired(axis)
    return jnp.where(even, second, first), jnp.where(even, first, second)


def columns(first_row, last_row, below, above):
    def column(rows, at):
        return jnp.concatenate([below[at][None], rows, above[at][None]], axis=0)

    return column(first_row, 0), column(last_row, -1)


def swap(array, axis, mask):
    return lax.ppermute(array, axis, [(i, i ^ mask) for i in range(lax.axis_size(axis))])


def fill_patches(row_of, depth, rows, patches):
    chans, width = row_of(1, 1).shape
    for d in range(depth + 2):
        for at, h in enumerate(rows):
            for b in range(3):
                patches[pl.ds((d * 3 + b) * chans, chans), pl.ds(at * width, width)] = row_of(d, h + b)


def shifted(value, step):
    if step == 0:
        return value
    width = value.shape[1]
    lane = lax.broadcasted_iota(jnp.int32, value.shape, 1)
    edge = width - 1 if step == 1 else 0
    return jnp.where(lane == edge, 0.0, pltpu.roll(value, (-step) % width, 1))


def rowwise(value, width):
    return [value[:, at : at + width] for at in range(0, value.shape[1], width)]


def beside(rows):
    return rows[0] if len(rows) == 1 else jnp.concatenate(rows, axis=1)


def forward_rows(positions, row_of, w1, bias, cot, delta, before, payload, patches, taps, slopes, grad):
    co, width = bias.shape[1], cot.shape[3]
    ci = patches.shape[0] // 9
    for at, (d, h) in enumerate(positions):
        for a in range(3):
            for b in range(3):
                patches[pl.ds((a * 3 + b) * ci, ci), pl.ds(at * width, width)] = row_of(d + a, h + b)
    taps[...] = jnp.dot(w1[...], patches[...], preferred_element_type=F32)
    shift_bias = jnp.broadcast_to(bias[...], (width, co)).T
    bias_acc = jnp.zeros((co, width), F32)
    starts = range(0, len(positions), GROUP)
    per_group = len(starts) > 2
    product = functools.partial(
        lax.dot_general,
        dimension_numbers=(((1,), (1,)), ((), ())),
        preferred_element_type=F32,
    )
    for start in starts:
        group = positions[start : start + GROUP]
        lanes = pl.ds(start * width, len(group) * width)
        low, middle, high = (rowwise(taps[i * co : (i + 1) * co, lanes], width) for i in range(3))
        linear = beside(
            [
                m + shift_bias + shifted(l, -1) + shifted(h, 1)
                for l, m, h in zip(low, middle, high)
            ]
        )
        sigma = 1.0 / (1.0 + jnp.exp(-linear))
        incoming = beside([cot[d, h].astype(F32) for d, h in group])
        rounded = (incoming * sigma * (1.0 + linear * (1.0 - sigma))).astype(BF16)
        wide = rowwise(rounded.astype(F32), width)
        for at, row in enumerate(rowwise(rounded, width)):
            delta[start + at] = row
            bias_acc = bias_acc + wide[at]
        before_it = beside([shifted(row, 1) for row in wide]).astype(BF16)
        after_it = beside([shifted(row, -1) for row in wide]).astype(BF16)
        if per_group:
            term = product(patches[:, lanes], jnp.concatenate([before_it, rounded, after_it], axis=0))
            grad[...] = term if start == 0 else grad[...] + term
        else:
            slopes[:co, lanes] = before_it
            slopes[co : 2 * co, lanes] = rounded
            slopes[2 * co :, lanes] = after_it
    if not per_group:
        grad[...] = product(patches[...], slopes[...])
    rows = grad.shape[0]
    tail = rows + rows // 2
    total = jnp.sum(bias_acc.T, axis=0, keepdims=True)
    left_over = payload.shape[0] - tail
    row_at = lax.broadcasted_iota(jnp.int32, (left_over, co), 0)
    bias_rows = jnp.where(row_at == 0, jnp.broadcast_to(total, (left_over, co)), 0.0)
    zeros = jnp.zeros((left_over, payload.shape[1] - co), F32)
    for at, value in (
        (pl.ds(0, rows), grad[:, : 2 * co]),
        (
            pl.ds(rows, rows // 2),
            jnp.concatenate([grad[: rows // 2, 2 * co :], grad[rows // 2 :, 2 * co :]], axis=1),
        ),
        (pl.ds(tail, left_over), jnp.concatenate([bias_rows, zeros], axis=1)),
    ):
        payload[at, :] = value if before is None else before[at, :] + value


def parts_of(depth, height):
    layers, rows = range(1, depth - 1), range(1, height - 1)
    return (
        [(d, h) for d in layers for h in rows],
        [(d, h) for h in (0, height - 1) for d in layers],
        [(d, h) for d in (0, depth - 1) for h in range(height)],
    )


def forward_kernel(positions, halos, x, *refs):
    left, right, low, high = (*refs[:halos], None, None, None, None)[:4]
    w1, bias, cot, *refs = refs[halos:]
    before, *refs = refs if halos else (None, *refs)
    depth, height = x.shape[:2]

    def row_of(d, h):
        if d == 0:
            return low[h]
        if d == depth + 1:
            return high[h]
        return left[d - 1] if h == 0 else right[d - 1] if h == height + 1 else x[d - 1, h - 1]

    delta, *refs = refs
    forward_rows(positions, row_of, w1, bias, cot, delta, before, *refs)


def input_kernel(inner, sides, ends, below, above, left, right, w2, out, patches):
    depth, height, ci, width = out.shape
    co = inner.shape[1]
    place = {}
    for ref, positions in zip((inner, sides, ends), parts_of(depth, height)):
        place.update({position: (ref, at) for at, position in enumerate(positions)})

    def row_of(d, h):
        if h == 0:
            return left[d]
        if h == height + 1:
            return right[d]
        if d == 0:
            return below[h - 1]
        if d == depth + 1:
            return above[h - 1]
        ref, at = place[d - 1, h - 1]
        return ref[at]

    fill_patches(row_of, depth, range(height), patches)
    for d in range(depth):
        taps = jnp.dot(w2[...], patches[pl.ds(d * 3 * co, 9 * co), :], preferred_element_type=F32)
        for h in range(height):
            lanes = slice(h * width, (h + 1) * width)
            total = taps[ci : 2 * ci, lanes]
            total = total + shifted(taps[:ci, lanes], 1) + shifted(taps[2 * ci :, lanes], -1)
            out[d, h] = total.astype(BF16)


def unpack_kernel(scale, low, high, weight_out, bias_out, full):
    half = low.shape[0]
    co = bias_out.shape[1]
    full[:half, :] = low[...] * scale
    full[half:, :] = high[...] * scale
    rows = weight_out.shape[0] // 3
    ci = rows // 9
    step = ci // 2
    for j in range(9):
        for part in range(2):
            source = j * ci + part * step
            to = 3 * j * ci + part * step
            weight_out[pl.ds(to, step), :] = full[pl.ds(source, step), :co]
            weight_out[pl.ds(to + ci, step), :] = full[pl.ds(source, step), co:]
            at = rows + source % (rows // 2)
            lanes = slice(0, co) if source < rows // 2 else slice(co, 2 * co)
            weight_out[pl.ds(to + 2 * ci, step), :] = full[pl.ds(at, step), lanes]
    bias_out[...] = full[rows + rows // 2 : rows + rows // 2 + 1, :co]


def load_kernel(*refs):
    count = len(refs) // 2
    done = refs[-1]
    copies = [pltpu.make_async_copy(refs[i], refs[count + i], done.at[i]) for i in range(count)]
    for copy in copies:
        copy.start()
    for copy in copies:
        copy.wait()


def loaded(*arrays):
    return pl.pallas_call(
        load_kernel,
        out_shape=[jax.ShapeDtypeStruct(a.shape, a.dtype) for a in arrays],
        in_specs=[pl.BlockSpec(memory_space=pltpu.HBM) for a in arrays],
        out_specs=[pl.BlockSpec(memory_space=pltpu.VMEM) for a in arrays],
        scratch_shapes=[pltpu.SemaphoreType.DMA((len(arrays),))],
        compiler_params=pltpu.CompilerParams(vmem_limit_bytes=16 << 20),
    )(*(pltpu.with_memory_space_constraint(a, pltpu.HBM) for a in arrays))


def call(kernel, outs, scratch, flops, *args):
    size = sum(a.size * a.dtype.itemsize for a in args) + sum(o.size * o.dtype.itemsize for o in outs)
    return pl.pallas_call(
        kernel,
        out_shape=outs,
        scratch_shapes=scratch,
        compiler_params=pltpu.CompilerParams(vmem_limit_bytes=40 << 20),
        cost_estimate=pl.CostEstimate(flops=flops, bytes_accessed=size, transcendentals=0),
    )(*args)


def gathered_sum(part, axis, masks):
    own = lax.reduce_precision(part, 8, 7)
    sent = own.astype(BF16)
    terms = [own] + [swap(sent, axis, mask).astype(F32) for mask in masks]
    while len(terms) > 1:
        terms = [terms[i] + terms[i + 1] for i in range(0, len(terms), 2)]
    return terms[0]


def summed(total, meanwhile, work):
    half = total.shape[0] // 2
    low, high = total[:half], total[half:]
    first = lax.axis_index("depth") % 2 == 0
    got = swap(jnp.where(first, high, low), "depth", 1)
    part = jnp.where(first, low, high) + got
    for axis in AXES:
        count = lax.axis_size(axis)
        assert count & (count - 1) == 0
        bit = 2 if axis == "depth" else 1
        while bit < count:
            masks = [bit * way for way in WAYS[axis]] if 2 * bit < count else [bit]
            part = gathered_sum(part, axis, masks)
            bit *= len(masks) + 1
    part, done = lax.optimization_barrier((part, work(meanwhile)))
    other = swap(part, "depth", 1)
    return jnp.where(first, part, other), jnp.where(first, other, part), done


def local(inputs, weight, bias, cotangent):
    cubes, ci, depth, height, width = inputs.shape
    co = cotangent.shape[1]
    payload_rows = 9 * ci + 9 * ci // 2 + 16
    payload_shape = jax.ShapeDtypeStruct((payload_rows, 2 * co), F32)
    flops = 4 * width * 27 * ci * co
    total = None
    fields = []
    fields_in = [inputs[cube].transpose(1, 2, 0, 3) for cube in range(cubes)]
    rows = [(x[:, 0], x[:, -1]) for x in fields_in]
    rows, fields_in, weight, bias, cotangent = lax.optimization_barrier(
        (rows, fields_in, weight, bias, cotangent)
    )
    taps, bias_row, cotangent = loaded(weight.transpose(2, 3, 4, 1, 0), bias[None], cotangent)
    w1 = taps.transpose(2, 4, 0, 1, 3).reshape(3 * co, 9 * ci)
    for cube in range(cubes):
        x = fields_in[cube]
        cot = cotangent[cube].transpose(1, 2, 0, 3)
        parts = parts_of(depth, height)

        def forward(which, halos, so_far):
            count = len(parts[which])
            return call(
                functools.partial(forward_kernel, parts[which], len(halos)),
                (jax.ShapeDtypeStruct((count, co, width), BF16), payload_shape),
                [
                    pltpu.VMEM((9 * ci, count * width), BF16),
                    pltpu.VMEM((3 * co, count * width), F32),
                    pltpu.VMEM((3 * co, count * width), BF16),
                    pltpu.VMEM((9 * ci, 3 * co), F32),
                ],
                flops * count,
                x,
                *halos,
                w1,
                bias_row,
                cot,
                *so_far,
            )

        inner, part = forward(0, (), ())
        left, right = exchange(*rows[cube], "height")
        part, left, right = lax.optimization_barrier((part, left, right))

        def layer(at):
            return jnp.concatenate([left[at][None], x[at], right[at][None]], axis=0)

        low, high = exchange(layer(0), layer(-1), "depth")
        sides, part = forward(1, (left, right), (part,))
        ends, part = forward(2, (left, right, low, high), (part,))
        total = part if total is None else total + part
        below, above = exchange(ends[:height], ends[height:], "depth")
        below, above, taps = lax.optimization_barrier((below, above, taps))
        first_row = jnp.concatenate([ends[:1], sides[: depth - 2], ends[height : height + 1]], axis=0)
        last_row = jnp.concatenate([ends[height - 1 : height], sides[depth - 2 :], ends[-1:]], axis=0)
        around = exchange(*columns(first_row, last_row, below, above), "height")
        fields.append((inner, sides, ends, below, above, *around))
    w2 = jnp.flip(taps, (0, 1)).transpose(2, 3, 0, 1, 4).reshape(3 * ci, 9 * co)

    def input_gradients(fields):
        grads = []
        for field in fields:
            (grad,) = call(
                input_kernel,
                (jax.ShapeDtypeStruct((depth, height, ci, width), BF16),),
                [pltpu.VMEM(((depth + 2) * 3 * co, height * width), BF16)],
                flops // 2 * depth * height,
                *field,
                w2,
            )
            grads.append(grad.transpose(2, 0, 1, 3))
        return jnp.stack(grads)

    low, high, grads = summed(total, fields, input_gradients)
    voxels = cubes * depth * height * width
    for axis in AXES:
        voxels *= lax.axis_size(axis)
    scale = float(voxels) ** -0.5
    grad_taps, grad_bias = call(
        lambda *refs: unpack_kernel(scale, *refs),
        (jax.ShapeDtypeStruct((27 * ci, co), F32), jax.ShapeDtypeStruct((1, co), F32)),
        [pltpu.VMEM((payload_rows, 2 * co), F32)],
        payload_rows * 2 * co,
        low,
        high,
    )
    grad_weight = grad_taps.reshape(3, 3, 3, ci, co).transpose(4, 3, 0, 1, 2)
    return grads, grad_weight, grad_bias.reshape(co)


def solution(mesh):
    voxels = P("dp", None, "depth", "height", None)
    return jax.shard_map(
        local,
        mesh=mesh,
        in_specs=(voxels, P(), P(), voxels),
        out_specs=(voxels, P(), P()),
        check_vma=False,
    )
```

```python
import functools

import jax
import jax.numpy as jnp
from jax import lax
from jax.experimental import pallas as pl
from jax.experimental.pallas import tpu as pltpu
from jax.sharding import PartitionSpec as P

F32 = jnp.float32
BF16 = jnp.bfloat16
GROUP = 6
AXES = ("depth", "height", "dp")
WAYS = {"depth": (1, 2, 3), "height": (1, 2, 3), "dp": (1, 2, 3)}


def paired(axis):
    return lax.axis_index(axis) % 2 == 0 if lax.axis_size(axis) % 2 == 0 else jnp.bool_(True)


def meet(low_edge, high_edge, axis):
    count = lax.axis_size(axis)
    none = jnp.zeros_like(low_edge)
    if count == 1:
        return none, none
    if count % 2:
        up = [(i, i + 1) for i in range(count - 1)]
        down = [(i + 1, i) for i in range(count - 1)]
        return lax.ppermute(high_edge, axis, up), lax.ppermute(low_edge, axis, down)
    at, even = lax.axis_index(axis), paired(axis)
    inner = [(i, i ^ 1) for i in range(count)]
    first = lax.ppermute(jnp.where(even, high_edge, low_edge), axis, inner)
    if count == 2:
        return none, first
    outer = [(i, (i - 1 if i % 2 == 0 else i + 1) % count) for i in range(count)]
    second = lax.ppermute(jnp.where(even, low_edge, high_edge), axis, outer)
    return jnp.where((at == 0) | (at == count - 1), none, second), first


def exchange(low_edge, high_edge, axis):
    second, first = meet(low_edge, high_edge, axis)
    even = paired(axis)
    return jnp.where(even, second, first), jnp.where(even, first, second)


def columns(first_row, last_row, below, above):
    def column(rows, at):
        return jnp.concatenate([below[at][None], rows, above[at][None]], axis=0)

    return column(first_row, 0), column(last_row, -1)


def swap(array, axis, mask):
    return lax.ppermute(array, axis, [(i, i ^ mask) for i in range(lax.axis_size(axis))])


def fill_patches(row_of, depth, rows, patches):
    chans, width = row_of(1, 1).shape
    for d in range(depth + 2):
        for at, h in enumerate(rows):
            for b in range(3):
                patches[pl.ds((d * 3 + b) * chans, chans), pl.ds(at * width, width)] = row_of(d, h + b)


def shifted(value, step):
    if step == 0:
        return value
    width = value.shape[1]
    lane = lax.broadcasted_iota(jnp.int32, value.shape, 1)
    edge = width - 1 if step == 1 else 0
    return jnp.where(lane == edge, 0.0, pltpu.roll(value, (-step) % width, 1))


def rowwise(value, width):
    return [value[:, at : at + width] for at in range(0, value.shape[1], width)]


def beside(rows):
    return rows[0] if len(rows) == 1 else jnp.concatenate(rows, axis=1)


def forward_rows(positions, row_of, w1, bias, cot, delta, before, payload, patches, taps, slopes, grad):
    co, width = bias.shape[1], cot.shape[3]
    ci = patches.shape[0] // 9
    for at, (d, h) in enumerate(positions):
        for a in range(3):
            for b in range(3):
                patches[pl.ds((a * 3 + b) * ci, ci), pl.ds(at * width, width)] = row_of(d + a, h + b)
    taps[...] = jnp.dot(w1[...], patches[...], preferred_element_type=F32)
    shift_bias = jnp.broadcast_to(bias[...], (width, co)).T
    bias_acc = jnp.zeros((co, width), F32)
    starts = range(0, len(positions), GROUP)
    per_group = len(starts) > 2
    product = functools.partial(
        lax.dot_general,
        dimension_numbers=(((1,), (1,)), ((), ())),
        preferred_element_type=F32,
    )
    for start in starts:
        group = positions[start : start + GROUP]
        lanes = pl.ds(start * width, len(group) * width)
        low, middle, high = (rowwise(taps[i * co : (i + 1) * co, lanes], width) for i in range(3))
        linear = beside(
            [
                m + shift_bias + shifted(l, -1) + shifted(h, 1)
                for l, m, h in zip(low, middle, high)
            ]
        )
        sigma = 1.0 / (1.0 + jnp.exp(-linear))
        incoming = beside([cot[d, h].astype(F32) for d, h in group])
        rounded = (incoming * sigma * (1.0 + linear * (1.0 - sigma))).astype(BF16)
        wide = rowwise(rounded.astype(F32), width)
        for at, row in enumerate(rowwise(rounded, width)):
            delta[start + at] = row
            bias_acc = bias_acc + wide[at]
        before_it = beside([shifted(row, 1) for row in wide]).astype(BF16)
        after_it = beside([shifted(row, -1) for row in wide]).astype(BF16)
        if per_group:
            term = product(patches[:, lanes], jnp.concatenate([before_it, rounded, after_it], axis=0))
            grad[...] = term if start == 0 else grad[...] + term
        else:
            slopes[:co, lanes] = before_it
            slopes[co : 2 * co, lanes] = rounded
            slopes[2 * co :, lanes] = after_it
    if not per_group:
        grad[...] = product(patches[...], slopes[...])
    rows = grad.shape[0]
    tail = rows + rows // 2
    total = jnp.sum(bias_acc.T, axis=0, keepdims=True)
    left_over = payload.shape[0] - tail
    row_at = lax.broadcasted_iota(jnp.int32, (left_over, co), 0)
    bias_rows = jnp.where(row_at == 0, jnp.broadcast_to(total, (left_over, co)), 0.0)
    zeros = jnp.zeros((left_over, payload.shape[1] - co), F32)
    for at, value in (
        (pl.ds(0, rows), grad[:, : 2 * co]),
        (
            pl.ds(rows, rows // 2),
            jnp.concatenate([grad[: rows // 2, 2 * co :], grad[rows // 2 :, 2 * co :]], axis=1),
        ),
        (pl.ds(tail, left_over), jnp.concatenate([bias_rows, zeros], axis=1)),
    ):
        payload[at, :] = value if before is None else before[at, :] + value


def parts_of(depth, height):
    layers, rows = range(1, depth - 1), range(1, height - 1)
    return (
        [(d, h) for d in layers for h in rows],
        [(d, h) for h in (0, height - 1) for d in layers],
        [(d, h) for d in (0, depth - 1) for h in range(height)],
    )


def forward_kernel(positions, halos, x, *refs):
    left, right, low, high = (*refs[:halos], None, None, None, None)[:4]
    w1, bias, cot, *refs = refs[halos:]
    before, *refs = refs if halos else (None, *refs)
    depth, height = x.shape[:2]

    def row_of(d, h):
        if d == 0:
            return low[h]
        if d == depth + 1:
            return high[h]
        return left[d - 1] if h == 0 else right[d - 1] if h == height + 1 else x[d - 1, h - 1]

    delta, *refs = refs
    forward_rows(positions, row_of, w1, bias, cot, delta, before, *refs)


def input_kernel(inner, sides, ends, below, above, left, right, w2, out, patches):
    depth, height, ci, width = out.shape
    co = inner.shape[1]
    place = {}
    for ref, positions in zip((inner, sides, ends), parts_of(depth, height)):
        place.update({position: (ref, at) for at, position in enumerate(positions)})

    def row_of(d, h):
        if h == 0:
            return left[d]
        if h == height + 1:
            return right[d]
        if d == 0:
            return below[h - 1]
        if d == depth + 1:
            return above[h - 1]
        ref, at = place[d - 1, h - 1]
        return ref[at]

    fill_patches(row_of, depth, range(height), patches)
    for d in range(depth):
        taps = jnp.dot(w2[...], patches[pl.ds(d * 3 * co, 9 * co), :], preferred_element_type=F32)
        for h in range(height):
            lanes = slice(h * width, (h + 1) * width)
            total = taps[ci : 2 * ci, lanes]
            total = total + shifted(taps[:ci, lanes], 1) + shifted(taps[2 * ci :, lanes], -1)
            out[d, h] = total.astype(BF16)


def unpack_kernel(scale, low, high, weight_out, bias_out, full):
    half = low.shape[0]
    co = bias_out.shape[1]
    full[:half, :] = low[...] * scale
    full[half:, :] = high[...] * scale
    rows = weight_out.shape[0] // 3
    ci = rows // 9
    step = ci // 2
    for j in range(9):
        for part in range(2):
            source = j * ci + part * step
            to = 3 * j * ci + part * step
            weight_out[pl.ds(to, step), :] = full[pl.ds(source, step), :co]
            weight_out[pl.ds(to + ci, step), :] = full[pl.ds(source, step), co:]
            at = rows + source % (rows // 2)
            lanes = slice(0, co) if source < rows // 2 else slice(co, 2 * co)
            weight_out[pl.ds(to + 2 * ci, step), :] = full[pl.ds(at, step), lanes]
    bias_out[...] = full[rows + rows // 2 : rows + rows // 2 + 1, :co]


def load_kernel(*refs):
    count = len(refs) // 2
    done = refs[-1]
    copies = [pltpu.make_async_copy(refs[i], refs[count + i], done.at[i]) for i in range(count)]
    for copy in copies:
        copy.start()
    for copy in copies:
        copy.wait()


def loaded(*arrays):
    return pl.pallas_call(
        load_kernel,
        out_shape=[jax.ShapeDtypeStruct(a.shape, a.dtype) for a in arrays],
        in_specs=[pl.BlockSpec(memory_space=pltpu.HBM) for a in arrays],
        out_specs=[pl.BlockSpec(memory_space=pltpu.VMEM) for a in arrays],
        scratch_shapes=[pltpu.SemaphoreType.DMA((len(arrays),))],
        compiler_params=pltpu.CompilerParams(vmem_limit_bytes=16 << 20),
    )(*(pltpu.with_memory_space_constraint(a, pltpu.HBM) for a in arrays))


def call(kernel, outs, scratch, flops, *args):
    size = sum(a.size * a.dtype.itemsize for a in args) + sum(o.size * o.dtype.itemsize for o in outs)
    return pl.pallas_call(
        kernel,
        out_shape=outs,
        scratch_shapes=scratch,
        compiler_params=pltpu.CompilerParams(vmem_limit_bytes=40 << 20),
        cost_estimate=pl.CostEstimate(flops=flops, bytes_accessed=size, transcendentals=0),
    )(*args)


def gathered_sum(part, axis, masks):
    own = lax.reduce_precision(part, 8, 7)
    sent = own.astype(BF16)
    terms = [own] + [swap(sent, axis, mask).astype(F32) for mask in masks]
    while len(terms) > 1:
        terms = [terms[i] + terms[i + 1] for i in range(0, len(terms), 2)]
    return terms[0]


def summed(total, meanwhile, work):
    half = total.shape[0] // 2
    low, high = total[:half], total[half:]
    first = lax.axis_index("depth") % 2 == 0
    got = swap(jnp.where(first, high, low), "depth", 1)
    part = jnp.where(first, low, high) + got
    for axis in AXES:
        count = lax.axis_size(axis)
        assert count & (count - 1) == 0
        bit = 2 if axis == "depth" else 1
        while bit < count:
            masks = [bit * way for way in WAYS[axis]] if 2 * bit < count else [bit]
            part = gathered_sum(part, axis, masks)
            bit *= len(masks) + 1
    part, done = lax.optimization_barrier((part, work(meanwhile)))
    other = swap(part, "depth", 1)
    return jnp.where(first, part, other), jnp.where(first, other, part), done


def local(inputs, weight, bias, cotangent):
    cubes, ci, depth, height, width = inputs.shape
    co = cotangent.shape[1]
    payload_rows = 9 * ci + 9 * ci // 2 + 16
    payload_shape = jax.ShapeDtypeStruct((payload_rows, 2 * co), F32)
    flops = 4 * width * 27 * ci * co
    total = None
    fields = []
    fields_in = [inputs[cube].transpose(1, 2, 0, 3) for cube in range(cubes)]
    rows = [(x[:, 0], x[:, -1]) for x in fields_in]
    rows, fields_in, weight, bias, cotangent = lax.optimization_barrier(
        (rows, fields_in, weight, bias, cotangent)
    )
    taps, bias_row, cotangent = loaded(weight.transpose(2, 3, 4, 1, 0), bias[None], cotangent)
    w1 = taps.transpose(2, 4, 0, 1, 3).reshape(3 * co, 9 * ci)
    for cube in range(cubes):
        x = fields_in[cube]
        cot = cotangent[cube].transpose(1, 2, 0, 3)
        parts = parts_of(depth, height)

        def forward(which, halos, so_far):
            count = len(parts[which])
            return call(
                functools.partial(forward_kernel, parts[which], len(halos)),
                (jax.ShapeDtypeStruct((count, co, width), BF16), payload_shape),
                [
                    pltpu.VMEM((9 * ci, count * width), BF16),
                    pltpu.VMEM((3 * co, count * width), F32),
                    pltpu.VMEM((3 * co, count * width), BF16),
                    pltpu.VMEM((9 * ci, 3 * co), F32),
                ],
                flops * count,
                x,
                *halos,
                w1,
                bias_row,
                cot,
                *so_far,
            )

        inner, part = forward(0, (), ())
        left, right = exchange(*rows[cube], "height")
        part, left, right = lax.optimization_barrier((part, left, right))

        def layer(at):
            return jnp.concatenate([left[at][None], x[at], right[at][None]], axis=0)

        low, high = exchange(layer(0), layer(-1), "depth")
        sides, part = forward(1, (left, right), (part,))
        ends, part = forward(2, (left, right, low, high), (part,))
        total = part if total is None else total + part
        below, above = exchange(ends[:height], ends[height:], "depth")
        below, above, taps = lax.optimization_barrier((below, above, taps))
        first_row = jnp.concatenate([ends[:1], sides[: depth - 2], ends[height : height + 1]], axis=0)
        last_row = jnp.concatenate([ends[height - 1 : height], sides[depth - 2 :], ends[-1:]], axis=0)
        around = exchange(*columns(first_row, last_row, below, above), "height")
        fields.append((inner, sides, ends, below, above, *around))
    w2 = jnp.flip(taps, (0, 1)).transpose(2, 3, 0, 1, 4).reshape(3 * ci, 9 * co)

    def input_gradients(fields):
        grads = []
        for field in fields:
            (grad,) = call(
                input_kernel,
                (jax.ShapeDtypeStruct((depth, height, ci, width), BF16),),
                [pltpu.VMEM(((depth + 2) * 3 * co, height * width), BF16)],
                flops // 2 * depth * height,
                *field,
                w2,
            )
            grads.append(grad.transpose(2, 0, 1, 3))
        return jnp.stack(grads)

    low, high, grads = summed(total, fields, input_gradients)
    voxels = cubes * depth * height * width
    for axis in AXES:
        voxels *= lax.axis_size(axis)
    scale = float(voxels) ** -0.5
    grad_taps, grad_bias = call(
        lambda *refs: unpack_kernel(scale, *refs),
        (jax.ShapeDtypeStruct((27 * ci, co), F32), jax.ShapeDtypeStruct((1, co), F32)),
        [pltpu.VMEM((payload_rows, 2 * co), F32)],
        payload_rows * 2 * co,
        low,
        high,
    )
    grad_weight = grad_taps.reshape(3, 3, 3, ci, co).transpose(4, 3, 0, 1, 2)
    return grads, grad_weight, grad_bias.reshape(co)


def solution(mesh):
    voxels = P("dp", None, "depth", "height", None)
    return jax.shard_map(
        local,
        mesh=mesh,
        in_specs=(voxels, P(), P(), voxels),
        out_specs=(voxels, P(), P()),
        check_vma=False,
    )
```
